32 devices in a mesh: dp: 8 (over y, x, core), layer: 4 (over z).
Axes of the slice: x: 2, y: 2, z: 4, core: 2. Of those that a mesh axis runs over, the one named last changes fastest.
Arguments:
- history: bfloat16 [16, 4096, 2048], P('layer', 'dp'), may hold values from -6 to 6
- mix_weights: float32 [4, 16, 4096], P(None, 'layer', 'dp'), may hold values from -1.5 to 1.5
- segments: int32 [8, 512], P('dp'), may hold values from 0 to 1, never falling along the last dimension, each value on 1 to 511 neighbouring positions
- w_query: float32 [2048, 2048], P('dp', 'layer'), may hold values from -0.125 to 0.125
- w_key: float32 [2048, 2048], P('dp', 'layer'), may hold values from -0.125 to 0.125
- w_value: float32 [2048, 2048], P('dp', 'layer'), may hold values from -0.125 to 0.125
- w_output: float32 [2048, 2048], P('layer', 'dp'), may hold values from -1 to 1
- w_up: float32 [2048, 8192], P('dp', 'layer'), may hold values from -0.125 to 0.125
- w_down: float32 [8192, 2048], P('layer', 'dp'), may hold values from -0.0625 to 0.0625
- norm_gains: float32 [5, 2048], replicated, may hold values from 0.5 to 1.5
- w_first: float32 [2048, 68], replicated, may hold values from -0.125 to 0.125
- w_second: float32 [68, 68], replicated, may hold values from -0.75 to 0.75
- out_cotangent: float32 [4096, 2048], P(('dp', 'layer')), may hold values from -6 to 6
- mix_cotangent: float32 [4096, 68], P(('dp', 'layer')), may hold values from -6 to 6
Outputs:
- block_out: bfloat16 [4096, 2048], P(('dp', 'layer'))
- next_mix: float32 [4096, 68], P(('dp', 'layer'))
- history_grad: bfloat16 [16, 4096, 2048], P('layer', 'dp')
- mix_grad: float32 [4, 16, 4096], P(None, 'layer', 'dp')
- query_grad: float32 [2048, 2048], P('dp', 'layer')
- key_grad: float32 [2048, 2048], P('dp', 'layer')
- value_grad: float32 [2048, 2048], P('dp', 'layer')
- output_grad: float32 [2048, 2048], P('layer', 'dp')
- up_grad: float32 [2048, 8192], P('dp', 'layer')
- down_grad: float32 [8192, 2048], P('layer', 'dp')
- gains_grad: float32 [5, 2048], replicated
- first_grad: float32 [2048, 68], replicated
- second_grad: float32 [68, 68], replicated
The draws below stay inside these ranges and needn't reach their ends.
Inputs may be any that keep to these rules, and one draw needn't show every extreme that they name: `segments`: ids never fall along a data row; each of the 2 documents of a row is nonempty and holds at most 511 tokens.
All inputs are finite; a program needn't handle non-finite values.
Results may differ from the reference program's by a relative error of at most 0.02.
Values may be sent and summed in bfloat16 or wider, within the bound.
No kernel may reach another device: no remote copies, remote signals or barrier semaphores. Data moves between devices by JAX's collectives and lax.ppermute only.
A program may use at most 192 MiB of HBM per device.

```python
import math
import jax
import jax.numpy as jnp
import numpy as np
from jax import lax

D = 2048
HEAD_DIM = 128
FF = 8192
HIST = 16
NMIX = 68
DOCS = 2
ROW_TOK = 512
DOC_MAX = 511
TOKENS = 4096
N_DP = 8


def levels(stream_key, shape, shards, least, top_value):
    level, own = 1.0, jax.random.fold_in(stream_key, 6)
    for position, blocks in shards:
        steps = jnp.exp(jax.random.uniform(jax.random.fold_in(own, position), (blocks,), jnp.float32, least / len(shards), top_value / len(shards)))
        level = level * jnp.repeat(steps, shape[position] // blocks).reshape([-1 if axis == position else 1 for axis in range(len(shape))])
    return level


def profile(count, total, most, skew):
    loads = [(1 << 20) // math.isqrt(standing ** skew) + 1 for standing in range(2, count + 1)]
    rest, counts = total - most - (count - 1), [1] * (count - 1)
    while rest > 0:
        free = [i for i in range(count - 1) if counts[i] < most]
        whole, left = sum([loads[i] for i in free]), rest
        for i in free:
            extra = min(most - counts[i], max(1, left * loads[i] // whole), rest)
            counts[i] = counts[i] + extra
            rest = rest - extra
    return np.array([most] + counts)


def ragged(stream_key, number_of, total, reach, lean):
    if number_of == 2:
        one = jax.random.randint(stream_key, (), max(1, total - reach), min(reach, total - 1) + 1)
        return jnp.stack([one, total - one])
    sizes = jnp.asarray(profile(number_of, total, reach, lean), jnp.int32)
    twos = (number_of - 1) // 2
    donor, taker = sizes[1:1 + 2 * twos:2], sizes[2:2 + 2 * twos:2]
    room = jnp.minimum(donor - 1, reach - taker)
    shifted = jax.random.randint(jax.random.fold_in(stream_key, 1), (twos,), 0, 1 << 20) % (room + 1)
    sizes = sizes.at[1:1 + 2 * twos:2].set(donor - shifted).at[2:2 + 2 * twos:2].set(taker + shifted)
    return sizes[jax.random.permutation(jax.random.fold_in(stream_key, 2), number_of)]


def gaussian(rng, shape, scale, reach, split=(), kind=jnp.bfloat16):
    values = jax.random.normal(rng, shape, jnp.float32) * scale
    if len(split) > 0:
        values = levels(rng, shape, split, -0.22, 0.18) * values
    return jnp.clip(values, min=-reach, max=reach).astype(kind)


def setup_inputs(seed: int = 0) -> dict:
    key_list = jax.random.split(jax.random.key(seed), 15)
    return {
        "history": gaussian(key_list[0], (HIST, TOKENS, D), 1.0, 6.0, ((0, 4), (1, 8))),
        "mix_weights": gaussian(key_list[1], (4, HIST, TOKENS), 0.25, 1.5, ((1, 4), (2, 8)), jnp.float32),
        "segments": jax.vmap(lambda own: jnp.searchsorted(jnp.cumsum(ragged(own, DOCS, ROW_TOK, DOC_MAX, 0)), jnp.arange(ROW_TOK), side="right"))(jax.random.split(key_list[2], N_DP)).reshape((N_DP, ROW_TOK)).astype(jnp.int32),
        "w_query": gaussian(key_list[3], (D, D), D ** -0.5, 0.125, ((0, 8), (1, 4)), jnp.float32),
        "w_key": gaussian(key_list[4], (D, D), D ** -0.5, 0.125, ((0, 8), (1, 4)), jnp.float32),
        "w_value": gaussian(key_list[5], (D, D), D ** -0.5, 0.125, ((0, 8), (1, 4)), jnp.float32),
        "w_output": gaussian(key_list[6], (D, D), (D // 64) ** -0.5, 1.0, ((0, 4), (1, 8)), jnp.float32),
        "w_up": gaussian(key_list[7], (D, FF), D ** -0.5, 0.125, ((0, 8), (1, 4)), jnp.float32),
        "w_down": gaussian(key_list[8], (FF, D), FF ** -0.5, 0.0625, ((0, 4), (1, 8)), jnp.float32),
        "norm_gains": jnp.clip(1.0 + 0.1 * jax.random.normal(key_list[9], (5, D), jnp.float32), 0.5, 1.5),
        "w_first": gaussian(key_list[10], (D, NMIX), D ** -0.5, 0.125, (), jnp.float32),
        "w_second": gaussian(key_list[11], (NMIX, NMIX), NMIX ** -0.5, 0.75, (), jnp.float32),
        "out_cotangent": gaussian(key_list[12], (TOKENS, D), 1.0, 6.0, ((0, 32),), jnp.float32),
        "mix_cotangent": gaussian(key_list[13], (TOKENS, NMIX), 1.0, 6.0, ((0, 32),), jnp.float32),
    }


highest = lax.Precision.HIGHEST
epsilon = 1e-05

@jax.custom_vjp
def low(v):
    return lax.optimization_barrier(v.astype(jnp.bfloat16)).astype(jnp.float32)

@jax.custom_vjp
def low_back(v):
    return v

def low_keep(v):
    return (low(v), None)

def low_pass(kept, grad):
    return (grad,)

def back_keep(v):
    return (v, None)

def back_low(kept, grad):
    return (low(grad),)
low.defvjp(low_keep, low_pass)
low_back.defvjp(back_keep, back_low)

def matmul(left, right):
    return jnp.dot(left, right, precision=highest)

def layer_norm(values, gain_vec):
    centre = values - lax.optimization_barrier(jnp.mean(values, axis=-1, keepdims=True))
    spread = lax.optimization_barrier(jnp.mean(centre * centre, axis=-1, keepdims=True))
    return centre * lax.rsqrt(spread + epsilon) * gain_vec

def rms_norm(values, gain_vec):
    square = lax.optimization_barrier(jnp.mean(values * values, axis=-1, keepdims=True))
    return values * lax.rsqrt(square + epsilon) * gain_vec

def gelu_exact(values):
    return jax.nn.gelu(values, approximate=False)

def doc_angles(seg_row, head_dim, doc_count):
    length = seg_row.shape[0]
    labels = jnp.arange(doc_count, dtype=jnp.int32)
    before = lax.optimization_barrier(jnp.sum((seg_row[None, :] < labels[:, None]).astype(jnp.int32), axis=1))
    member = (seg_row[:, None] == labels[None, :]).astype(jnp.int32)
    begins = lax.optimization_barrier(jnp.sum(member * before[None, :], axis=1))
    places = (jnp.arange(length, dtype=jnp.int32) - begins).astype(jnp.float32)
    half_dim = head_dim // 2
    frequency = jnp.exp(jnp.arange(half_dim, dtype=jnp.float32) * (-2.0 * math.log(10000.0) / head_dim))
    angles = places[:, None] * frequency[None, :]
    return (jnp.cos(angles)[:, None, :], jnp.sin(angles)[:, None, :])

def rotate(values, cosine, sine):
    half_dim = values.shape[-1] // 2
    first_half = values[..., :half_dim]
    second_half = values[..., half_dim:]
    return jnp.concatenate((first_half * cosine - second_half * sine, second_half * cosine + first_half * sine), axis=-1)

def allowed_pairs(seg_row):
    places = jnp.arange(seg_row.shape[0], dtype=jnp.int32)
    return (seg_row[:, None] == seg_row[None, :]) & (places[:, None] >= places[None, :])

def mixer(out_rows, gain_vec, first_matrix, second_matrix):
    hidden = gelu_exact(matmul(rms_norm(out_rows, gain_vec), first_matrix))
    return matmul(hidden, second_matrix)

def row_forward(weights, hist_row, mix_row, seg_row):
    wq_low, wk_low, wv_low, wo_low, wu_low, wd_low, gain_rows, first_matrix, second_matrix = weights
    length = hist_row.shape[1]
    width = hist_row.shape[2]
    head_dim = HEAD_DIM
    head_count = width // head_dim
    streams = jnp.einsum('sjt,jtd->std', mix_row, hist_row, precision=highest)
    query_in = low_back(streams[0])
    key_in = low_back(streams[1])
    value_in = low_back(streams[2])
    resid_in = low_back(streams[3])
    query_norm = low(layer_norm(query_in, gain_rows[0]))
    key_norm = low(layer_norm(key_in, gain_rows[1]))
    value_norm = low(layer_norm(value_in, gain_rows[2]))
    query_lin = low_back(matmul(query_norm, wq_low))
    key_lin = low_back(matmul(key_norm, wk_low))
    value_lin = low(low_back(matmul(value_norm, wv_low)))
    cosine, sine = doc_angles(seg_row, head_dim, DOCS)
    queries = low(rotate(query_lin.reshape(length, head_count, head_dim), cosine, sine))
    keys = low(rotate(key_lin.reshape(length, head_count, head_dim), cosine, sine))
    value_heads = value_lin.reshape(length, head_count, head_dim)
    scores = low_back(jnp.einsum('qhd,khd->hqk', queries, keys, precision=highest) * head_dim ** (-0.5))
    masked = jnp.where(allowed_pairs(seg_row)[None], scores, -1e+30)
    probs = low(jax.nn.softmax(masked, axis=-1))
    context = jnp.einsum('hqk,khd->qhd', probs, value_heads, precision=highest)
    context = low(low_back(context)).reshape(length, width)
    attn_branch = low_back(matmul(context, wo_low))
    hidden_in = resid_in + attn_branch
    mlp_norm = low(layer_norm(hidden_in, gain_rows[3]))
    up_proj = low_back(matmul(mlp_norm, wu_low))
    active = low(gelu_exact(up_proj))
    mlp_branch = low_back(matmul(active, wd_low))
    block = hidden_in + mlp_branch
    return (block, mixer(block, gain_rows[4], first_matrix, second_matrix))

def reference(history, mix_weights, segments, w_query, w_key, w_value, w_output, w_up, w_down, norm_gains, w_first, w_second, out_cotangent, mix_cotangent):
    hist_full = history.astype(jnp.float32)

    def forward(masters, hist_vals, mix_vals):
        weights = (low(masters[0]), low(masters[1]), low(masters[2]), low(masters[3]), low(masters[4]), low(masters[5]), masters[6], masters[7], masters[8])
        hist_rows = hist_vals.reshape(HIST, N_DP, ROW_TOK, D).transpose(1, 0, 2, 3)
        mix_rows = mix_vals.reshape(4, HIST, N_DP, ROW_TOK).transpose(2, 0, 1, 3)

        def one_row(item):
            return row_forward(weights, item[0], item[1], item[2])
        blocks, mixes = lax.map(jax.checkpoint(one_row), (hist_rows, mix_rows, segments))
        return (blocks.reshape(TOKENS, D), mixes.reshape(TOKENS, NMIX))
    masters = (w_query, w_key, w_value, w_output, w_up, w_down, norm_gains, w_first, w_second)
    outputs, pullback = jax.vjp(forward, masters, hist_full, mix_weights)
    master_grads, hist_grads, mix_grads = pullback((out_cotangent, mix_cotangent))
    return (outputs[0].astype(jnp.bfloat16), outputs[1], hist_grads.astype(jnp.bfloat16), mix_grads, master_grads[0], master_grads[1], master_grads[2], master_grads[3], master_grads[4], master_grads[5], master_grads[6], master_grads[7], master_grads[8])
```

```python
import math

import jax
import jax.numpy as jnp
from jax import lax
from jax.experimental import pallas as pl
from jax.experimental.pallas import tpu as pltpu
from jax.sharding import PartitionSpec as P

HEAD_DIM = 128
DOCS = 2


highest = lax.Precision.HIGHEST
epsilon = 1e-05
bf16 = jnp.bfloat16
f32 = jnp.float32
CHUNK = 16


def rms_norm(values, gain_vec):
    square = jnp.mean(values * values, axis=-1, keepdims=True)
    return values * lax.rsqrt(square + epsilon) * gain_vec


def gelu_exact(values):
    return jax.nn.gelu(values, approximate=False)


def mixer(out_rows, gain_vec, first_matrix, second_matrix):
    hidden = gelu_exact(jnp.dot(rms_norm(out_rows, gain_vec), first_matrix, precision=highest))
    return jnp.dot(hidden, second_matrix, precision=highest)


def plain_dot(left, right):
    return jnp.dot(left, right, preferred_element_type=f32)


def dot_left_t(left, right):
    return lax.dot_general(left, right, (((0,), (0,)), ((), ())), preferred_element_type=f32)


def dot_right_t(left, right):
    return lax.dot_general(left, right, (((1,), (1,)), ((), ())), preferred_element_type=f32)


def gather_blocks(block, count):
    return [block] + [
        lax.ppermute(block, "layer", [(i, (i + k) % count) for i in range(count)])
        for k in range(1, count)
    ]


def gather_line(block, count):
    ups, downs = [block], [block]
    for k in range(1, count):
        ups.append(lax.ppermute(ups[-1], "layer", [(i, i + 1) for i in range(k - 1, count - 1)]))
        downs.append(lax.ppermute(downs[-1], "layer", [(i + 1, i) for i in range(count - k)]))
    return [[block]] + [[ups[k], downs[count - k]] for k in range(1, count)]


def sum_line(blocks, count):
    up = down = None
    for k in range(1, count):
        up = blocks[k] if up is None else blocks[k] + up
        up = lax.ppermute(up, "layer", [(i, i + 1) for i in range(k)])
        down = blocks[count - k] if down is None else blocks[count - k] + down
        down = lax.ppermute(down, "layer", [(i, i - 1) for i in range(count - k, count)])
    return [blocks[0], up, down]


def total_of(pieces):
    total = pieces[0]
    for piece in pieces[1:]:
        total = total + piece
    return total


def after(value, *others):
    anywhere = pl.BlockSpec(memory_space=pl.ANY)
    return pl.pallas_call(
        lambda *refs: None,
        in_specs=[anywhere] * (1 + len(others)),
        out_specs=anywhere,
        out_shape=jax.ShapeDtypeStruct(value.shape, value.dtype),
        input_output_aliases={0: 0},
    )(value, *others)


def return_blocks(blocks, count):
    return [blocks[0]] + [
        lax.ppermute(blocks[k], "layer", [(i, (i - k) % count) for i in range(count)])
        for k in range(1, count)
    ]


def add_blocks(blocks):
    total = blocks[0].astype(f32)
    for block in blocks[1:]:
        total = total + block.astype(f32)
    return total


def vmem(megabytes):
    return pltpu.CompilerParams(vmem_limit_bytes=megabytes << 20)


def row_loop(rows, body, carry):
    return lax.fori_loop(
        0, rows // CHUNK, lambda i, c: body(pl.ds(pl.multiple_of(i * CHUNK, CHUNK), CHUNK), c), carry
    )


def stream_kernel(me_ref, mix_ref, hist_ref, *out_refs, stored, first):
    def body(at, carry):
        mix = mix_ref[at, :]
        totals = [None] * len(out_refs)
        for j in range(stored):
            rows = hist_ref[j, at, :].astype(f32)
            for s in range(len(out_refs)):
                i = (first + s) * stored + j
                term = rows * mix[:, i : i + 1]
                totals[s] = term if j == 0 else totals[s] + term
        for out_ref, total in zip(out_refs, totals):
            out_ref[at, :] = total.astype(bf16)
        return carry

    row_loop(out_refs[0].shape[0], body, 0)


def stream_sums(me, mix_cols, history, first, number, count):
    stored, tokens, width = history.shape
    rows = 128
    steps = tokens // count // rows
    where = lambda i, w: (w[0] - i // steps + count) % count * steps + i % steps
    return pl.pallas_call(
        lambda *refs: stream_kernel(*refs, stored=stored, first=first),
        grid_spec=pltpu.PrefetchScalarGridSpec(
            num_scalar_prefetch=1,
            grid=(tokens // rows,),
            in_specs=[
                pl.BlockSpec((rows, 4 * stored), lambda i, w: (where(i, w), 0)),
                pl.BlockSpec((stored, rows, width), lambda i, w: (0, where(i, w), 0)),
            ],
            out_specs=[pl.BlockSpec((rows, width), lambda i, w: (i, 0))] * number,
        ),
        out_shape=[jax.ShapeDtypeStruct((tokens, width), bf16)] * number,
        compiler_params=vmem(48),
    )(me.astype(jnp.int32).reshape(1), mix_cols, history)


def join_kernel(gain_ref, base_ref, *refs):
    parts, (sum_ref, norm_ref) = refs[:-2], refs[-2:]

    def body(at, carry):
        values = base_ref[at, :].astype(f32) + total_of([p[at, :].astype(f32) for p in parts])
        sum_ref[at, :] = values
        centre = values - jnp.mean(values, axis=1, keepdims=True)
        spread = jnp.mean(centre * centre, axis=1, keepdims=True)
        norm_ref[at, :] = (centre * lax.rsqrt(spread + epsilon) * gain_ref[...]).astype(bf16)
        return carry

    row_loop(base_ref.shape[0], body, 0)


def join_norm(base, parts, gain_vec):
    return pl.pallas_call(
        join_kernel,
        out_shape=[jax.ShapeDtypeStruct(base.shape, f32), jax.ShapeDtypeStruct(base.shape, bf16)],
        compiler_params=vmem(48),
    )(gain_vec[None], base, *parts)


def back_kernel(gain_ref, value_ref, *refs, parts, based):
    part_refs = refs[:parts]
    base_ref = refs[parts] if based else None
    out_ref, dgain_ref = refs[-2:]

    def body(at, dgain):
        values = value_ref[at, :].astype(f32)
        grad = total_of([p[at, :].astype(f32) for p in part_refs])
        centre = values - jnp.mean(values, axis=1, keepdims=True)
        inv = lax.rsqrt(jnp.mean(centre * centre, axis=1, keepdims=True) + epsilon)
        hat = centre * inv
        scaled = grad * gain_ref[...]
        back = (
            scaled
            - jnp.mean(scaled, axis=1, keepdims=True)
            - hat * jnp.mean(scaled * hat, axis=1, keepdims=True)
        ) * inv
        if based:
            back = back + base_ref[at, :]
        out_ref[at, :] = back.astype(bf16)
        return dgain + jnp.sum(grad * hat, axis=0, keepdims=True)

    dgain_ref[...] = row_loop(value_ref.shape[0], body, jnp.zeros(dgain_ref.shape, f32))


def norm_back(values, parts, gain_vec, base=None):
    operands = [gain_vec[None], values] + list(parts) + ([] if base is None else [base])
    back, dgain = pl.pallas_call(
        lambda *refs: back_kernel(*refs, parts=len(parts), based=base is not None),
        out_shape=[
            jax.ShapeDtypeStruct(values.shape, bf16),
            jax.ShapeDtypeStruct((1, values.shape[1]), f32),
        ],
        compiler_params=vmem(48),
    )(*operands)
    return back, dgain[0]


def history_kernel(me_ref, mix_ref, hist_ref, *refs, stored, counts):
    hist_out, mix_out = refs[-2:]
    width = hist_out.shape[2]
    lanes = 256

    def body(at, carry):
        mix = mix_ref[at, :]
        sums = [None] * (4 * stored)
        for c in range(0, width, lanes):
            cols = slice(c, c + lanes)
            wide, first = [], 0
            for n in counts:
                wide.append(total_of([r[at, cols].astype(f32) for r in refs[first : first + n]]))
                first += n
            for j in range(stored):
                stored_rows = hist_ref[j, at, cols].astype(f32)
                total = None
                for s in range(4):
                    i = s * stored + j
                    term = wide[s] * mix[:, i : i + 1]
                    total = term if total is None else total + term
                    product = stored_rows * wide[s]
                    product = total_of([product[:, l : l + 128] for l in range(0, lanes, 128)])
                    sums[i] = product if sums[i] is None else sums[i] + product
                hist_out[j, at, cols] = total.astype(bf16)
        mix_out[at, :] = jnp.concatenate([jnp.sum(v, axis=1, keepdims=True) for v in sums], axis=1)
        return carry

    row_loop(hist_out.shape[1], body, 0)


def history_block(where, mix_cols, history, grads, so_far):
    stored, tokens, width = history.shape
    counts = [len(g) for g in grads]
    pieces = [p for g in grads for p in g]
    block = pieces[0].shape[0]
    rows = 64
    steps = block // rows
    grad_spec = pl.BlockSpec((rows, width), lambda i, w: (i, 0))
    specs = [
        pl.BlockSpec((rows, 4 * stored), lambda i, w: (w[0] * steps + i, 0)),
        pl.BlockSpec((stored, rows, width), lambda i, w: (0, w[0] * steps + i, 0)),
    ] + [grad_spec] * len(pieces)
    operands = [mix_cols, history] + pieces
    aliases = {}
    if so_far is not None:
        specs += [pl.BlockSpec(memory_space=pl.ANY)] * 2
        aliases = {1 + len(operands): 0, 2 + len(operands): 1}
        operands += so_far
    return pl.pallas_call(
        lambda *refs: history_kernel(*refs, stored=stored, counts=counts),
        grid_spec=pltpu.PrefetchScalarGridSpec(
            num_scalar_prefetch=1,
            grid=(steps,),
            in_specs=specs,
            out_specs=[
                pl.BlockSpec((stored, rows, width), lambda i, w: (0, w[0] * steps + i, 0)),
                pl.BlockSpec((rows, 4 * stored), lambda i, w: (w[0] * steps + i, 0)),
            ],
        ),
        out_shape=[
            jax.ShapeDtypeStruct((stored, tokens, width), bf16),
            jax.ShapeDtypeStruct((tokens, 4 * stored), f32),
        ],
        input_output_aliases=aliases,
        compiler_params=vmem(48),
    )(where, *operands)


def turn(values, cosine, sine):
    return values * cosine + pltpu.roll(values, HEAD_DIM // 2, 1) * sine


def score_block(queries, keys, allowed):
    scores = lax.dot_general(
        queries, keys, (((1,), (1,)), ((), ())), preferred_element_type=f32
    ) * (HEAD_DIM ** (-0.5))
    return jnp.where(allowed, scores, -1e30)


def allowed_block(row_ids, col_ids):
    return (row_ids[:, 0:1] == col_ids[0:1, :]) & (row_ids[:, 1:2] >= col_ids[1:2, :])


def attend_kernel(rows_ref, cols_ref, cos_ref, sin_ref, q_ref, k_ref, v_ref, ctx_ref, qr_ref, kr_ref, lse_ref):
    allowed = allowed_block(rows_ref[...], cols_ref[...])
    queries = turn(q_ref[...], cos_ref[...], sin_ref[...]).astype(bf16)
    keys = turn(k_ref[...], cos_ref[...], sin_ref[...]).astype(bf16)
    qr_ref[...] = queries
    kr_ref[...] = keys
    scores = score_block(queries, keys, allowed)
    row_max = jnp.max(scores, axis=1, keepdims=True)
    shifted = jnp.exp(scores - row_max)
    row_sum = jnp.sum(shifted, axis=1, keepdims=True)
    probs = (shifted / row_sum).astype(bf16)
    ctx_ref[...] = jnp.dot(probs, v_ref[...], preferred_element_type=f32).astype(bf16)
    lse_ref[0] = row_max + jnp.log(row_sum)


def attend(row_ids, col_ids, cosine, sine, q_lin, k_lin, v_lin):
    tokens, width = q_lin.shape
    heads = width // HEAD_DIM
    full = lambda a: pl.BlockSpec(a.shape, lambda h: (0,) * a.ndim)
    head = pl.BlockSpec((tokens, HEAD_DIM), lambda h: (0, h))
    return pl.pallas_call(
        attend_kernel,
        grid=(heads,),
        in_specs=[full(row_ids), full(col_ids), full(cosine), full(sine), head, head, head],
        out_specs=[head, head, head, pl.BlockSpec((1, tokens, 1), lambda h: (h, 0, 0))],
        out_shape=[jax.ShapeDtypeStruct((tokens, width), bf16)] * 3
        + [jax.ShapeDtypeStruct((heads, tokens, 1), f32)],
        compiler_params=vmem(56),
    )(row_ids, col_ids, cosine, sine, q_lin, k_lin, v_lin)


def attend_back_kernel(
    rows_ref, cols_ref, cos_ref, sin_ref, q_ref, k_ref, v_ref, lse_ref, grad_ref, dq_ref, dk_ref, dv_ref
):
    allowed = allowed_block(rows_ref[...], cols_ref[...])
    queries, keys, values, grad = q_ref[...], k_ref[...], v_ref[...], grad_ref[...]
    scale = HEAD_DIM ** (-0.5)
    probs = jnp.exp(score_block(queries, keys, allowed) - lse_ref[0])
    prob_grad = lax.dot_general(grad, values, (((1,), (1,)), ((), ())), preferred_element_type=f32)
    dv_ref[...] = lax.dot_general(
        probs.astype(bf16), grad, (((0,), (0,)), ((), ())), preferred_element_type=f32
    ).astype(bf16)
    centre = jnp.sum(probs * prob_grad, axis=1, keepdims=True)
    score_grad = (probs * (prob_grad - centre)).astype(bf16)
    dq = jnp.dot(score_grad, keys, preferred_element_type=f32) * scale
    dk = (
        lax.dot_general(score_grad, queries, (((0,), (0,)), ((), ())), preferred_element_type=f32)
        * scale
    )
    dq_ref[...] = turn(dq, cos_ref[...], -sin_ref[...]).astype(bf16)
    dk_ref[...] = turn(dk, cos_ref[...], -sin_ref[...]).astype(bf16)


def attend_back(row_ids, col_ids, cosine, sine, queries, keys, v_lin, lse, grad):
    tokens, width = queries.shape
    heads = width // HEAD_DIM
    full = lambda a: pl.BlockSpec(a.shape, lambda h: (0,) * a.ndim)
    head = pl.BlockSpec((tokens, HEAD_DIM), lambda h: (0, h))
    return pl.pallas_call(
        attend_back_kernel,
        grid=(heads,),
        in_specs=[full(row_ids), full(col_ids), full(cosine), full(sine), head, head, head]
        + [pl.BlockSpec((1, tokens, 1), lambda h: (h, 0, 0)), head],
        out_specs=[head, head, head],
        out_shape=[jax.ShapeDtypeStruct((tokens, width), bf16)] * 3,
        compiler_params=vmem(56),
    )(row_ids, col_ids, cosine, sine, queries, keys, v_lin, lse, grad)


def places(seg_row):
    length = seg_row.shape[0]
    labels = jnp.arange(DOCS, dtype=jnp.int32)
    before = jnp.sum((seg_row[None, :] < labels[:, None]).astype(jnp.int32), axis=1)
    member = (seg_row[:, None] == labels[None, :]).astype(jnp.int32)
    begins = jnp.sum(member * before[None, :], axis=1)
    return jnp.arange(length, dtype=jnp.int32) - begins


def local(
    history,
    mix_weights,
    segments,
    w_query,
    w_key,
    w_value,
    w_output,
    w_up,
    w_down,
    norm_gains,
    w_first,
    w_second,
    out_cotangent,
    mix_cotangent,
):
    stored, row_tok, width = history.shape
    count = lax.axis_size("layer")
    me = lax.axis_index("layer")
    own_tok = row_tok // count
    order = [(me - k) % count for k in range(count)]

    query_low = jnp.concatenate([w_query, w_key, w_value], axis=1).astype(bf16)
    full_qkv = lax.all_gather(query_low, "dp", axis=0, tiled=True)
    head_cols = w_query.shape[1]
    full_query = full_qkv[:, :head_cols]
    full_key = full_qkv[:, head_cols : 2 * head_cols]
    full_value = full_qkv[:, 2 * head_cols :]
    full_output = lax.all_gather(w_output.astype(bf16), "dp", axis=1, tiled=True)
    full_up = lax.all_gather(w_up.astype(bf16), "dp", axis=0, tiled=True)
    full_down = lax.all_gather(w_down.astype(bf16), "dp", axis=1, tiled=True)

    mix_cols = mix_weights.reshape(4 * stored, row_tok).T
    def block_of(rows, k):
        return rows[k * own_tok : (k + 1) * own_tok]

    def blocks_of(rows):
        return [block_of(rows, k) for k in range(count)]

    shares = list(stream_sums(me, mix_cols, history, 0, 2, count))
    shares += stream_sums(me, mix_cols, history, 2, 2, count)
    stream_own, normed, lin, normed_rows = [], [], [], []
    for s in range(4):
        if s == 2:
            shares[2] = after(shares[2], normed[0])
        if s == 3:
            shares[3] = after(shares[3], normed[1])
        pieces = sum_line(blocks_of(shares[s]), count)
        if s < 3:
            own, norm = join_norm(pieces[0], pieces[1:], norm_gains[s])
            stream_own.append(own)
            normed.append(norm)
        else:
            residual = pieces
    for s, weight in enumerate((full_query, full_key, full_value)):
        rows = jnp.concatenate([total_of(b) for b in gather_line(normed[s], count)], axis=0)
        normed_rows.append(rows)
        lin.append(plain_dot(rows, weight))
    q_lin, k_lin, v_lin = lin[0], lin[1], lin[2].astype(bf16)

    seg_row = segments[0]
    place = places(seg_row)
    index = jnp.arange(row_tok, dtype=jnp.int32)
    ids = jnp.stack([seg_row, index, place])
    ids = jnp.concatenate(
        [lax.dynamic_slice_in_dim(ids, k * own_tok, own_tok, axis=1) for k in order], axis=1
    )
    half = HEAD_DIM // 2
    frequency = jnp.exp(
        jnp.arange(half, dtype=f32) * (-2.0 * math.log(10000.0) / HEAD_DIM)
    )
    angles = ids[2].astype(f32)[:, None] * frequency[None, :]
    cosine, sine = jnp.cos(angles), jnp.sin(angles)
    cosine = jnp.concatenate([cosine, cosine], axis=1)
    sine = jnp.concatenate([-sine, sine], axis=1)
    col_ids = ids[:2]
    row_ids = col_ids.T

    context, queries, keys, lse = attend(row_ids, col_ids, cosine, sine, q_lin, k_lin, v_lin)

    attn = return_blocks(
        [plain_dot(block_of(context, k), full_output).astype(bf16) for k in range(count)], count
    )
    hidden_in, mlp_norm = join_norm(residual[0], residual[1:] + attn, norm_gains[3])
    mlp_blocks = gather_blocks(mlp_norm, count)
    ups, actives, mlp = [], [], []
    for k in range(count):
        up_proj = plain_dot(mlp_blocks[k], full_up)
        active = gelu_exact(up_proj).astype(bf16)
        ups.append(up_proj)
        actives.append(active)
        mlp.append(plain_dot(active, full_down).astype(bf16))
        if k == 0:
            mlp_blocks[1] = after(mlp_blocks[1], mlp[0], *mlp_blocks[2:])
    block = hidden_in + add_blocks(return_blocks(mlp, count))

    next_mix, mixer_pull = jax.vjp(mixer, block, norm_gains[4], w_first, w_second)
    block_part, mixer_gain_grad, first_grad, second_grad = mixer_pull(mix_cotangent)
    block_grad = out_cotangent + block_part
    first_sum = lax.psum(first_grad, ("dp", "layer"))
    branch_blocks = gather_blocks(block_grad.astype(bf16), count)

    up_lows, mlp_backs = [], []
    for k in range(count):
        active_grad = dot_right_t(branch_blocks[k], full_down)
        up_low = jax.vjp(gelu_exact, ups[k])[1](active_grad)[0].astype(bf16)
        up_lows.append(up_low)
        mlp_backs.append(dot_right_t(up_low, full_up).astype(bf16))
        if k == 0:
            branch_blocks[1] = after(branch_blocks[1], mlp_backs[0], *branch_blocks[2:])
    returned = return_blocks(mlp_backs, count)
    branch_rows = jnp.concatenate(branch_blocks, axis=0)
    active_rows = after(jnp.concatenate(actives, axis=0), *mlp_backs)
    down_grad = dot_left_t(active_rows, branch_rows).astype(bf16)
    down_sum = lax.psum_scatter(down_grad, "dp", scatter_dimension=1, tiled=True)
    up_rows = after(jnp.concatenate(up_lows, axis=0), *mlp_backs)
    up_grad = dot_left_t(jnp.concatenate(mlp_blocks, axis=0), up_rows).astype(bf16)
    up_sum = lax.psum_scatter(up_grad, "dp", scatter_dimension=0, tiled=True)
    returned[1] = after(returned[1], down_grad, up_grad)
    hidden_low, mlp_gain_grad = norm_back(hidden_in, returned, norm_gains[3], block_grad)
    hidden_blocks = gather_blocks(hidden_low, count)
    hidden_rows = jnp.concatenate(hidden_blocks, axis=0)
    context_grad = dot_right_t(hidden_rows, full_output).astype(bf16)

    lin_grads = attend_back(
        row_ids, col_ids, cosine, sine, queries, keys, v_lin, lse, context_grad
    )
    lin_grads = [after(lin_grads[0], down_sum), lin_grads[1], lin_grads[2]]

    weights = (full_query, full_key, full_value)
    parts = [dot_right_t(lin_grads[s], weights[s]).astype(bf16) for s in range(3)]
    gain_grads, stream_blocks, early = [], [], None
    for s in range(3):
        share = parts[s]
        if s == 2:
            share = after(share, gained[0])
        gained = norm_back(stream_own[s], sum_line(blocks_of(share), count), norm_gains[s])
        gain_grads.append(gained[1])
        early = gained[0] if early is None else early
        if s < 2:
            stream_blocks.append(gather_line(gained[0], count))
        else:
            stream_blocks.append([[b] for b in gather_blocks(gained[0], count)])
    stream_blocks.append([[b] for b in hidden_blocks])

    held_rows = after(hidden_rows, early)
    output_grad = dot_left_t(context, held_rows).astype(bf16)
    output_sum = lax.psum_scatter(output_grad, "dp", scatter_dimension=1, tiled=True)
    qkv_grad = jnp.concatenate(
        [
            dot_left_t(normed_rows[s], after(lin_grads[s], early)).astype(bf16)
            for s in range(3)
        ],
        axis=1,
    )
    qkv_sum = lax.psum_scatter(qkv_grad, "dp", scatter_dimension=0, tiled=True)
    gain_rows = jnp.stack(gain_grads + [mlp_gain_grad, mixer_gain_grad])
    gains_sum, second_sum = lax.psum((gain_rows, second_grad), ("dp", "layer"))

    so_far = None
    for k in range(count):
        if k == 0:
            stream_blocks[2][0][0] = after(stream_blocks[2][0][0], first_sum, gains_sum)
        so_far = history_block(
            order[k].astype(jnp.int32).reshape(1),
            mix_cols,
            history,
            [stream_blocks[s][k] for s in range(4)],
            so_far,
        )
    history_grad, mix_back = so_far
    mix_grad = mix_back.T.reshape(4, stored, row_tok)

    qkv_sum = qkv_sum.astype(f32)
    return (
        block.astype(bf16),
        next_mix,
        history_grad,
        mix_grad,
        qkv_sum[:, :head_cols],
        qkv_sum[:, head_cols : 2 * head_cols],
        qkv_sum[:, 2 * head_cols :],
        output_sum.astype(f32),
        up_sum.astype(f32),
        down_sum.astype(f32),
        gains_sum,
        first_sum,
        second_sum,
    )


def solution(mesh):
    placed = (
        P("layer", "dp", None),
        P(None, "layer", "dp"),
        P("dp", None),
        P("dp", "layer"),
        P("dp", "layer"),
        P("dp", "layer"),
        P("layer", "dp"),
        P("dp", "layer"),
        P("layer", "dp"),
        P(),
        P(),
        P(),
        P(("dp", "layer"), None),
        P(("dp", "layer"), None),
    )
    return jax.shard_map(
        local,
        mesh=mesh,
        in_specs=placed,
        out_specs=(
            P(("dp", "layer"), None),
            P(("dp", "layer"), None),
            P("layer", "dp", None),
            P(None, "layer", "dp"),
            P("dp", "layer"),
            P("dp", "layer"),
            P("dp", "layer"),
            P("layer", "dp"),
            P("dp", "layer"),
            P("layer", "dp"),
            P(),
            P(),
            P(),
        ),
        check_vma=False,
    )
```

```python
import math

import jax
import jax.numpy as jnp
from jax import lax
from jax.experimental import pallas as pl
from jax.experimental.pallas import tpu as pltpu
from jax.sharding import PartitionSpec as P

HEAD_DIM = 128
DOCS = 2


highest = lax.Precision.HIGHEST
epsilon = 1e-05
bf16 = jnp.bfloat16
f32 = jnp.float32
CHUNK = 16


def rms_norm(values, gain_vec):
    square = jnp.mean(values * values, axis=-1, keepdims=True)
    return values * lax.rsqrt(square + epsilon) * gain_vec


def gelu_exact(values):
    return jax.nn.gelu(values, approximate=False)


def mixer(out_rows, gain_vec, first_matrix, second_matrix):
    hidden = gelu_exact(jnp.dot(rms_norm(out_rows, gain_vec), first_matrix, precision=highest))
    return jnp.dot(hidden, second_matrix, precision=highest)


def plain_dot(left, right):
    return jnp.dot(left, right, preferred_element_type=f32)


def dot_left_t(left, right):
    return lax.dot_general(left, right, (((0,), (0,)), ((), ())), preferred_element_type=f32)


def dot_right_t(left, right):
    return lax.dot_general(left, right, (((1,), (1,)), ((), ())), preferred_element_type=f32)


def total_of(pieces):
    total = pieces[0]
    for piece in pieces[1:]:
        total = total + piece
    return total


def join(values, others):
    anywhere = pl.BlockSpec(memory_space=pl.ANY)
    return list(
        pl.pallas_call(
            lambda *refs: None,
            in_specs=[anywhere] * (len(values) + len(others)),
            out_specs=[anywhere] * len(values),
            out_shape=[jax.ShapeDtypeStruct(v.shape, v.dtype) for v in values],
            input_output_aliases={i: i for i in range(len(values))},
        )(*values, *others)
    )


def after(value, *others):
    return join([value], others)[0]


def gather_line(block, count):
    ups, downs = [block], [block]
    for k in range(1, count):
        ups.append(lax.ppermute(ups[-1], "layer", [(i, i + 1) for i in range(k - 1, count - 1)]))
        downs.append(lax.ppermute(downs[-1], "layer", [(i + 1, i) for i in range(count - k)]))
    return [[block]] + [[ups[k], downs[count - k]] for k in range(1, count)]


def sum_line(blocks, count):
    up = down = None
    for k in range(1, count):
        up = blocks[k] if up is None else blocks[k] + up
        up = lax.ppermute(up, "layer", [(i, i + 1) for i in range(k)])
        down = blocks[count - k] if down is None else blocks[count - k] + down
        down = lax.ppermute(down, "layer", [(i, i - 1) for i in range(count - k, count)])
    return [blocks[0], up, down]


def vmem(megabytes):
    return pltpu.CompilerParams(vmem_limit_bytes=megabytes << 20)


def row_loop(rows, body, carry):
    return lax.fori_loop(
        0, rows // CHUNK, lambda i, c: body(pl.ds(pl.multiple_of(i * CHUNK, CHUNK), CHUNK), c), carry
    )


def stream_kernel(me_ref, mix_ref, hist_ref, *out_refs, stored, first):
    def body(at, carry):
        mix = mix_ref[at, :]
        totals = [None] * len(out_refs)
        for j in range(stored):
            rows = hist_ref[j, at, :].astype(f32)
            for s in range(len(out_refs)):
                i = (first + s) * stored + j
                term = rows * mix[:, i : i + 1]
                totals[s] = term if j == 0 else totals[s] + term
        for out_ref, total in zip(out_refs, totals):
            out_ref[at, :] = total.astype(bf16)
        return carry

    row_loop(out_refs[0].shape[0], body, 0)


def stream_sums(me, mix_cols, history, first, number, count, order=(), tokens_last=False):
    stored, tokens, width = history.shape
    rows = 128
    steps = tokens // count // rows
    where = lambda i, w: (w[0] - i // steps + count) % count * steps + i % steps
    outs = [pl.BlockSpec((rows, width), lambda i, w: (i, 0))] * number
    if tokens_last:
        outs[-1] = pl.BlockSpec((rows, width), lambda i, w: (where(i, w), 0))
    return pl.pallas_call(
        lambda *refs: stream_kernel(*refs[:3], *refs[3 + len(order) :], stored=stored, first=first),
        grid_spec=pltpu.PrefetchScalarGridSpec(
            num_scalar_prefetch=1,
            grid=(tokens // rows,),
            in_specs=[
                pl.BlockSpec((rows, 4 * stored), lambda i, w: (where(i, w), 0)),
                pl.BlockSpec((stored, rows, width), lambda i, w: (0, where(i, w), 0)),
            ]
            + [pl.BlockSpec(memory_space=pl.ANY)] * len(order),
            out_specs=outs,
        ),
        out_shape=[jax.ShapeDtypeStruct((tokens, width), bf16)] * number,
        compiler_params=vmem(48),
    )(me.astype(jnp.int32).reshape(1), mix_cols, history, *order)


def join_kernel(gain_ref, base_ref, *refs):
    parts, (sum_ref, norm_ref) = refs[:-2], refs[-2:]

    def body(at, carry):
        values = base_ref[at, :].astype(f32) + total_of([p[at, :].astype(f32) for p in parts])
        sum_ref[at, :] = values
        centre = values - jnp.mean(values, axis=1, keepdims=True)
        spread = jnp.mean(centre * centre, axis=1, keepdims=True)
        norm_ref[at, :] = (centre * lax.rsqrt(spread + epsilon) * gain_ref[...]).astype(bf16)
        return carry

    row_loop(base_ref.shape[0], body, 0)


def join_norm(base, parts, gain_vec):
    return pl.pallas_call(
        join_kernel,
        out_shape=[jax.ShapeDtypeStruct(base.shape, f32), jax.ShapeDtypeStruct(base.shape, bf16)],
        compiler_params=vmem(48),
    )(gain_vec[None], base, *parts)


def norm_grad(values, grad, gain):
    centre = values - jnp.mean(values, axis=1, keepdims=True)
    inv = lax.rsqrt(jnp.mean(centre * centre, axis=1, keepdims=True) + epsilon)
    hat = centre * inv
    scaled = grad * gain
    back = (
        scaled
        - jnp.mean(scaled, axis=1, keepdims=True)
        - hat * jnp.mean(scaled * hat, axis=1, keepdims=True)
    ) * inv
    return back, jnp.sum(grad * hat, axis=0, keepdims=True)


def back_kernel(gain_ref, value_ref, *refs, parts, based):
    part_refs = refs[:parts]
    base_ref = refs[parts] if based else None
    out_ref, dgain_ref = refs[-2:]

    def body(at, dgain):
        values = value_ref[at, :].astype(f32)
        grad = total_of([p[at, :].astype(f32) for p in part_refs])
        back, dgain_rows = norm_grad(values, grad, gain_ref[...])
        if based:
            back = back + base_ref[at, :]
        out_ref[at, :] = back.astype(bf16)
        return dgain + dgain_rows

    dgain_ref[...] = row_loop(value_ref.shape[0], body, jnp.zeros(dgain_ref.shape, f32))


def norm_back(values, parts, gain_vec, base=None, order=()):
    operands = [gain_vec[None], values] + list(parts) + ([] if base is None else [base])
    number = len(operands)
    back, dgain = pl.pallas_call(
        lambda *refs: back_kernel(
            *refs[:number], *refs[-2:], parts=len(parts), based=base is not None
        ),
        in_specs=[pl.BlockSpec(memory_space=pltpu.VMEM)] * number
        + [pl.BlockSpec(memory_space=pl.ANY)] * len(order),
        out_shape=[
            jax.ShapeDtypeStruct(values.shape, bf16),
            jax.ShapeDtypeStruct((1, values.shape[1]), f32),
        ],
        compiler_params=vmem(48),
    )(*operands, *order)
    return back, dgain[0]


def history_kernel(mix_ref, hist_ref, near_ref, hidden_ref, *refs, stored):
    hist_out, mix_out = refs[-2:]
    width = hist_out.shape[2]
    lanes = 256

    def body(at, carry):
        mix = mix_ref[at, :]
        sums = [None] * (4 * stored)
        for c in range(0, width, lanes):
            cols = slice(c, c + lanes)
            wide = [near_ref[at, s * width + c : s * width + c + lanes].astype(f32) for s in range(3)]
            wide.append(hidden_ref[at, cols].astype(f32))
            for j in range(stored):
                stored_rows = hist_ref[j, at, cols].astype(f32)
                total = None
                for s in range(4):
                    i = s * stored + j
                    term = wide[s] * mix[:, i : i + 1]
                    total = term if total is None else total + term
                    product = stored_rows * wide[s]
                    product = total_of([product[:, l : l + 128] for l in range(0, lanes, 128)])
                    sums[i] = product if sums[i] is None else sums[i] + product
                hist_out[j, at, cols] = total.astype(bf16)
        mix_out[at, :] = jnp.concatenate([jnp.sum(v, axis=1, keepdims=True) for v in sums], axis=1)
        return carry

    row_loop(hist_out.shape[1], body, 0)


def history_grads(mix_cols, history, near, hidden, order):
    stored, tokens, width = history.shape
    rows = 64
    here = lambda i: (i, 0)
    there = lambda i: (0, i, 0)
    return pl.pallas_call(
        lambda *refs: history_kernel(*refs, stored=stored),
        grid=(tokens // rows,),
        in_specs=[
            pl.BlockSpec((rows, 4 * stored), here),
            pl.BlockSpec((stored, rows, width), there),
            pl.BlockSpec((rows, 3 * width), here),
            pl.BlockSpec((rows, width), here),
        ]
        + [pl.BlockSpec(memory_space=pl.ANY)] * len(order),
        out_specs=[
            pl.BlockSpec((stored, rows, width), there),
            pl.BlockSpec((rows, 4 * stored), here),
        ],
        out_shape=[
            jax.ShapeDtypeStruct((stored, tokens, width), bf16),
            jax.ShapeDtypeStruct((tokens, 4 * stored), f32),
        ],
        compiler_params=vmem(48),
    )(mix_cols, history, near, hidden, *order)


def contract_rows(left, right):
    return lax.dot_general(left, right, (((0,), (0,)), ((), ())), preferred_element_type=f32)


def contract_cols(left, right):
    return lax.dot_general(left, right, (((1,), (1,)), ((), ())), preferred_element_type=f32)


def resident(array):
    return pl.BlockSpec(array.shape, lambda i: (0,) * array.ndim)


def mlp_grads(mlp_rows, up_low, branch_rows, active, part):
    tokens, width = mlp_rows.shape
    hidden = active.shape[1]
    rows = 256

    def kernel(mlp_ref, up_ref, branch_ref, active_ref, out_ref):
        out_ref[:, :hidden] = contract_rows(mlp_ref[...], up_ref[...]).astype(bf16)
        out_ref[:, hidden : 2 * hidden] = contract_rows(branch_ref[...], active_ref[...]).astype(bf16)
        out_ref[:, 2 * hidden :] = jnp.zeros((rows, 2 * part - 2 * hidden), bf16)

    side = pl.BlockSpec((tokens, rows), lambda i: (0, i))
    return pl.pallas_call(
        kernel,
        grid=(width // rows,),
        in_specs=[side, resident(up_low), side, resident(active)],
        out_specs=pl.BlockSpec((rows, 2 * part), lambda i: (i, 0)),
        out_shape=jax.ShapeDtypeStruct((width, 3 * part), bf16),
        compiler_params=vmem(56),
    )(mlp_rows, up_low, branch_rows, active)


def attention_grads(so_far, normed_rows, lin_grads, hidden_rows, context, first, part):
    tokens, width = hidden_rows.shape
    heads = context.shape[1]
    rows = 256

    def kernel(q_ref, k_ref, v_ref, dq_ref, dk_ref, dv_ref, hidden_ref, ctx_ref, first_ref, _, out_ref):
        pairs = ((q_ref, dq_ref), (k_ref, dk_ref), (v_ref, dv_ref), (hidden_ref, ctx_ref))
        for s, (left, right) in enumerate(pairs):
            out_ref[:, s * heads : (s + 1) * heads] = contract_rows(left[...], right[...]).astype(bf16)
        out_ref[:, 4 * heads :] = first_ref[...].astype(bf16)

    side = pl.BlockSpec((tokens, rows), lambda i: (0, i))
    return pl.pallas_call(
        kernel,
        grid=(width // rows,),
        in_specs=[side] * 3
        + [resident(lin_grads[0])] * 3
        + [side, resident(context)]
        + [pl.BlockSpec((rows, first.shape[1]), lambda i: (i, 0)), pl.BlockSpec(memory_space=pl.ANY)],
        out_specs=pl.BlockSpec((rows, part), lambda i: (i, 2)),
        out_shape=jax.ShapeDtypeStruct(so_far.shape, bf16),
        input_output_aliases={9: 0},
        compiler_params=vmem(56),
    )(*normed_rows, *lin_grads, hidden_rows, context, first, so_far)


def round_weights(w_up, w_down, w_query, w_key, w_value, w_output, order):
    rows, hidden = w_up.shape
    heads = w_query.shape[1]

    def kernel(up_ref, down_ref, q_ref, k_ref, v_ref, o_ref, _, out_ref):
        out_ref[:, :hidden] = up_ref[...].astype(bf16)
        out_ref[:, hidden : 2 * hidden] = down_ref[...].T.astype(bf16)
        for s, ref in enumerate((q_ref, k_ref, v_ref)):
            out_ref[:, 2 * hidden + s * heads : 2 * hidden + (s + 1) * heads] = ref[...].astype(bf16)
        out_ref[:, 2 * hidden + 3 * heads :] = o_ref[...].T.astype(bf16)

    return pl.pallas_call(
        kernel,
        in_specs=[pl.BlockSpec(memory_space=pltpu.VMEM)] * 6 + [pl.BlockSpec(memory_space=pl.ANY)],
        out_shape=jax.ShapeDtypeStruct((rows, 2 * hidden + 4 * heads), bf16),
        compiler_params=vmem(56),
    )(w_up, w_down, w_query, w_key, w_value, w_output, order)


def project(blocks, full, heads, place, kind):
    pieces = [p for b in blocks for p in b]
    counts = [len(b) for b in blocks]
    block, width = pieces[0].shape
    tokens = block * len(blocks)

    def kernel(full_ref, *refs):
        rows_ref, out_ref = refs[-2:]
        first = 0
        for k, n in enumerate(counts):
            rows_ref[k * block : (k + 1) * block, :] = total_of([r[...] for r in refs[first : first + n]])
            first += n
        out_ref[...] = jnp.dot(rows_ref[...], full_ref[...], preferred_element_type=f32).astype(kind)

    whole = pl.BlockSpec((block, width), lambda i: (0, 0))
    return pl.pallas_call(
        kernel,
        grid=(1,),
        in_specs=[pl.BlockSpec((width, heads), lambda i: (0, place))] + [whole] * len(pieces),
        out_specs=[
            pl.BlockSpec((tokens, width), lambda i: (0, 0)),
            pl.BlockSpec((tokens, heads), lambda i: (0, 0)),
        ],
        out_shape=[
            jax.ShapeDtypeStruct((tokens, width), bf16),
            jax.ShapeDtypeStruct((tokens, heads), kind),
        ],
        compiler_params=vmem(56),
    )(full, *pieces)


def feed_forward(rows, full, hidden):
    tokens, width = rows.shape
    cols = 512
    steps = hidden // cols

    def kernel(rows_ref, up_ref, down_ref, active_ref, slope_ref, out_ref, total_ref):
        step = pl.program_id(0)
        up = jnp.dot(rows_ref[...], up_ref[...], preferred_element_type=f32)
        below = 0.5 * (1.0 + lax.erf(up * (0.5**0.5)))
        active = (up * below).astype(bf16)
        active_ref[...] = active
        slope_ref[...] = below + up * jnp.exp(-0.5 * up * up) * ((2.0 * math.pi) ** -0.5)
        share = contract_cols(active, down_ref[...])

        @pl.when(step == 0)
        def _():
            total_ref[...] = share

        @pl.when(step > 0)
        def _():
            total_ref[...] += share

        @pl.when(step == steps - 1)
        def _():
            out_ref[...] = total_ref[...].astype(bf16)

    part = pl.BlockSpec((tokens, cols), lambda i: (0, i))
    return pl.pallas_call(
        kernel,
        grid=(steps,),
        in_specs=[
            resident(rows),
            pl.BlockSpec((width, cols), lambda i: (0, i)),
            pl.BlockSpec((width, cols), lambda i: (0, steps + i)),
        ],
        out_specs=[part, part, pl.BlockSpec((tokens, width), lambda i: (0, 0))],
        out_shape=[
            jax.ShapeDtypeStruct((tokens, hidden), bf16),
            jax.ShapeDtypeStruct((tokens, hidden), f32),
            jax.ShapeDtypeStruct((tokens, width), bf16),
        ],
        scratch_shapes=[pltpu.VMEM((tokens, width), f32)],
        compiler_params=vmem(60),
    )(rows, full, full)


def feed_back(rows, full, slope):
    tokens, width = rows.shape
    hidden = slope.shape[1]
    cols = 512
    steps = hidden // cols

    def kernel(rows_ref, up_ref, down_ref, slope_ref, low_ref, out_ref, total_ref):
        step = pl.program_id(0)
        grad = jnp.dot(rows_ref[...], down_ref[...], preferred_element_type=f32)
        low = (grad * slope_ref[...]).astype(bf16)
        low_ref[...] = low
        share = contract_cols(low, up_ref[...])

        @pl.when(step == 0)
        def _():
            total_ref[...] = share

        @pl.when(step > 0)
        def _():
            total_ref[...] += share

        @pl.when(step == steps - 1)
        def _():
            out_ref[...] = total_ref[...].astype(bf16)

    part = pl.BlockSpec((tokens, cols), lambda i: (0, i))
    return pl.pallas_call(
        kernel,
        grid=(steps,),
        in_specs=[
            resident(rows),
            pl.BlockSpec((width, cols), lambda i: (0, i)),
            pl.BlockSpec((width, cols), lambda i: (0, steps + i)),
            part,
        ],
        out_specs=[part, pl.BlockSpec((tokens, width), lambda i: (0, 0))],
        out_shape=[
            jax.ShapeDtypeStruct((tokens, hidden), bf16),
            jax.ShapeDtypeStruct((tokens, width), bf16),
        ],
        scratch_shapes=[pltpu.VMEM((tokens, width), f32)],
        compiler_params=vmem(60),
    )(rows, full, full, slope)


def turn(values, cosine, sine):
    return values * cosine + pltpu.roll(values, HEAD_DIM // 2, 1) * sine


def score_block(queries, keys, allowed):
    scores = lax.dot_general(
        queries, keys, (((1,), (1,)), ((), ())), preferred_element_type=f32
    ) * (HEAD_DIM ** (-0.5))
    return jnp.where(allowed, scores, -1e30)


def allowed_block(row_ids, col_ids):
    return (row_ids[:, 0:1] == col_ids[0:1, :]) & (row_ids[:, 1:2] >= col_ids[1:2, :])


def attend_kernel(rows_ref, cols_ref, cos_ref, sin_ref, q_ref, k_ref, v_ref, ctx_ref, qr_ref, kr_ref, lse_ref):
    allowed = allowed_block(rows_ref[...], cols_ref[...])
    queries = turn(q_ref[...], cos_ref[...], sin_ref[...]).astype(bf16)
    keys = turn(k_ref[...], cos_ref[...], sin_ref[...]).astype(bf16)
    qr_ref[...] = queries
    kr_ref[...] = keys
    scores = score_block(queries, keys, allowed)
    row_max = jnp.max(scores, axis=1, keepdims=True)
    shifted = jnp.exp(scores - row_max)
    row_sum = jnp.sum(shifted, axis=1, keepdims=True)
    probs = (shifted / row_sum).astype(bf16)
    ctx_ref[...] = jnp.dot(probs, v_ref[...], preferred_element_type=f32).astype(bf16)
    lse_ref[0] = row_max + jnp.log(row_sum)


def attend(row_ids, col_ids, cosine, sine, q_lin, k_lin, v_lin):
    tokens, width = q_lin.shape
    heads = width // HEAD_DIM
    full = lambda a: pl.BlockSpec(a.shape, lambda h: (0,) * a.ndim)
    head = pl.BlockSpec((tokens, HEAD_DIM), lambda h: (0, h))
    return pl.pallas_call(
        attend_kernel,
        grid=(heads,),
        in_specs=[full(row_ids), full(col_ids), full(cosine), full(sine), head, head, head],
        out_specs=[head, head, head, pl.BlockSpec((1, tokens, 1), lambda h: (h, 0, 0))],
        out_shape=[jax.ShapeDtypeStruct((tokens, width), bf16)] * 3
        + [jax.ShapeDtypeStruct((heads, tokens, 1), f32)],
        compiler_params=vmem(56),
    )(row_ids, col_ids, cosine, sine, q_lin, k_lin, v_lin)


def attend_back_kernel(
    rows_ref, cols_ref, cos_ref, sin_ref, q_ref, k_ref, v_ref, lse_ref, grad_ref, dq_ref, dk_ref, dv_ref
):
    allowed = allowed_block(rows_ref[...], cols_ref[...])
    queries, keys, values, grad = q_ref[...], k_ref[...], v_ref[...], grad_ref[...]
    scale = HEAD_DIM ** (-0.5)
    probs = jnp.exp(score_block(queries, keys, allowed) - lse_ref[0])
    prob_grad = lax.dot_general(grad, values, (((1,), (1,)), ((), ())), preferred_element_type=f32)
    dv_ref[...] = lax.dot_general(
        probs.astype(bf16), grad, (((0,), (0,)), ((), ())), preferred_element_type=f32
    ).astype(bf16)
    centre = jnp.sum(probs * prob_grad, axis=1, keepdims=True)
    score_grad = (probs * (prob_grad - centre)).astype(bf16)
    dq = jnp.dot(score_grad, keys, preferred_element_type=f32) * scale
    dk = (
        lax.dot_general(score_grad, queries, (((0,), (0,)), ((), ())), preferred_element_type=f32)
        * scale
    )
    dq_ref[...] = turn(dq, cos_ref[...], -sin_ref[...]).astype(bf16)
    dk_ref[...] = turn(dk, cos_ref[...], -sin_ref[...]).astype(bf16)


def attend_back(row_ids, col_ids, cosine, sine, queries, keys, v_lin, lse, grad):
    tokens, width = queries.shape
    heads = width // HEAD_DIM
    full = lambda a: pl.BlockSpec(a.shape, lambda h: (0,) * a.ndim)
    head = pl.BlockSpec((tokens, HEAD_DIM), lambda h: (0, h))
    return pl.pallas_call(
        attend_back_kernel,
        grid=(heads,),
        in_specs=[full(row_ids), full(col_ids), full(cosine), full(sine), head, head, head]
        + [pl.BlockSpec((1, tokens, 1), lambda h: (h, 0, 0)), head],
        out_specs=[head, head, head],
        out_shape=[jax.ShapeDtypeStruct((tokens, width), bf16)] * 3,
        compiler_params=vmem(56),
    )(row_ids, col_ids, cosine, sine, queries, keys, v_lin, lse, grad)


def unpack_grads(weight_sum, hidden, heads, part, order):
    rows = weight_sum.shape[0]

    def kernel(sum_ref, *refs):
        up_ref, down_ref, q_ref, k_ref, v_ref, o_ref, first_ref = refs[-7:]
        up_ref[...] = sum_ref[:, :hidden].astype(f32)
        down_ref[...] = sum_ref[:, hidden : 2 * hidden].astype(f32).T
        at = 2 * part
        for ref in (q_ref, k_ref, v_ref):
            ref[...] = sum_ref[:, at : at + heads].astype(f32)
            at += heads
        o_ref[...] = sum_ref[:, at : at + heads].astype(f32).T
        first_ref[...] = sum_ref[:, at + heads :].astype(f32)

    shapes = [(rows, hidden), (hidden, rows)] + [(rows, heads)] * 3
    shapes += [(heads, rows), (rows, 3 * part - 2 * part - 4 * heads)]
    return pl.pallas_call(
        kernel,
        in_specs=[pl.BlockSpec(memory_space=pltpu.VMEM)]
        + [pl.BlockSpec(memory_space=pl.ANY)] * len(order),
        out_shape=[jax.ShapeDtypeStruct(shape, f32) for shape in shapes],
        compiler_params=vmem(56),
    )(weight_sum, *order)


def places(seg_row):
    length = seg_row.shape[0]
    labels = jnp.arange(DOCS, dtype=jnp.int32)
    before = jnp.sum((seg_row[None, :] < labels[:, None]).astype(jnp.int32), axis=1)
    member = (seg_row[:, None] == labels[None, :]).astype(jnp.int32)
    begins = jnp.sum(member * before[None, :], axis=1)
    return jnp.arange(length, dtype=jnp.int32) - begins


def local(
    history,
    mix_weights,
    segments,
    w_query,
    w_key,
    w_value,
    w_output,
    w_up,
    w_down,
    norm_gains,
    w_first,
    w_second,
    out_cotangent,
    mix_cotangent,
):
    stored, row_tok, width = history.shape
    count = lax.axis_size("layer")
    me = lax.axis_index("layer")
    own_tok = row_tok // count
    order = [(me - k) % count for k in range(count)]

    def block_of(rows, k):
        return rows[k * own_tok : (k + 1) * own_tok]

    def blocks_of(rows):
        return [block_of(rows, k) for k in range(count)]

    def reorder(rows):
        return jnp.concatenate(
            [lax.dynamic_slice_in_dim(rows, k * own_tok, own_tok, axis=0) for k in order], axis=0
        )

    mix_cols = mix_weights.reshape(4 * stored, row_tok).T
    shares = stream_sums(me, mix_cols, history, 0, 4, count, tokens_last=True)

    hidden = w_up.shape[1]
    heads = w_query.shape[1]
    low = round_weights(w_up, w_down, w_query, w_key, w_value, w_output, shares[0])
    full = lax.all_gather(low, "dp", axis=0, tiled=True)
    place = 2 * hidden // heads

    def columns(first, number):
        return full[:, first : first + number]

    stream_own, normed, lin, normed_rows = [], [], [], []
    for s in range(3):
        pieces = sum_line(blocks_of(shares[s]), count)
        own, norm = join_norm(pieces[0], pieces[1:], norm_gains[s])
        stream_own.append(own)
        normed.append(norm)
    residual = lax.psum_scatter(
        after(shares[3], *normed), "layer", scatter_dimension=0, tiled=True
    )
    for s in range(3):
        rows, out = project(
            gather_line(normed[s], count), full, heads, place + s, f32 if s < 2 else bf16
        )
        normed_rows.append(rows)
        lin.append(out)
    q_lin, k_lin, v_lin = lin
    q_lin = after(q_lin, residual)

    seg_row = segments[0]
    place = places(seg_row)
    index = jnp.arange(row_tok, dtype=jnp.int32)
    ids = jnp.stack([seg_row, index, place])
    ids = jnp.concatenate(
        [lax.dynamic_slice_in_dim(ids, k * own_tok, own_tok, axis=1) for k in order], axis=1
    )
    half = HEAD_DIM // 2
    frequency = jnp.exp(
        jnp.arange(half, dtype=f32) * (-2.0 * math.log(10000.0) / HEAD_DIM)
    )
    angles = ids[2].astype(f32)[:, None] * frequency[None, :]
    cosine, sine = jnp.cos(angles), jnp.sin(angles)
    cosine = jnp.concatenate([cosine, cosine], axis=1)
    sine = jnp.concatenate([-sine, sine], axis=1)
    col_ids = ids[:2]
    row_ids = col_ids.T

    context, queries, keys, lse = attend(row_ids, col_ids, cosine, sine, q_lin, k_lin, v_lin)

    context = reorder(context)

    def collect(rows):
        return lax.all_gather(rows, "layer", axis=0, tiled=True)

    def spread(rows):
        return lax.psum_scatter(rows.astype(bf16), "layer", scatter_dimension=0, tiled=True)

    out_weight = columns(2 * hidden + 3 * heads, heads)
    attn = spread(dot_right_t(context, out_weight))
    hidden_in, mlp_norm = join_norm(residual, [attn], norm_gains[3])
    mlp_rows = collect(mlp_norm)
    active, slope, mlp_part = feed_forward(mlp_rows, full, hidden)
    block = hidden_in + spread(mlp_part).astype(f32)

    next_mix, mixer_pull = jax.vjp(mixer, block, norm_gains[4], w_first, w_second)
    block_part, mixer_gain_grad, first_grad, second_grad = mixer_pull(mix_cotangent)
    block_grad = out_cotangent + block_part
    branch_rows = collect(block_grad.astype(bf16))
    up_low, mlp_part = feed_back(branch_rows, full, slope)
    mlp_back = spread(mlp_part)
    part = 4 * heads + 128
    weight_grads = mlp_grads(mlp_rows, after(up_low, mlp_part), branch_rows, active, part)
    hidden_low, mlp_gain_grad = norm_back(
        hidden_in, [mlp_back], norm_gains[3], block_grad, [weight_grads]
    )
    hidden_rows = collect(hidden_low)
    context_grad = reorder(plain_dot(hidden_rows, out_weight).astype(bf16))
    lin_grads = attend_back(
        row_ids, col_ids, cosine, sine, queries, keys, v_lin, lse, context_grad
    )
    mixes = first_grad.shape[1]
    first_wide = jnp.pad(first_grad, ((0, 0), (0, 128 - mixes)))
    weight_grads = attention_grads(
        weight_grads, normed_rows, lin_grads, hidden_rows, context, first_wide, part
    )
    weight_sum = lax.psum_scatter(weight_grads, "dp", scatter_dimension=0, tiled=True)

    gain_grads, stream_low = [], []
    for s in range(3):
        share = dot_right_t(lin_grads[s], columns(2 * hidden + s * heads, heads)).astype(bf16)
        low, gain_grad = norm_back(
            stream_own[s], sum_line(blocks_of(share), count), norm_gains[s]
        )
        gain_grads.append(gain_grad)
        stream_low.append(low)
    near = collect(jnp.concatenate(stream_low, axis=1))

    gain_rows = jnp.stack(gain_grads + [mlp_gain_grad, mixer_gain_grad])
    gains_sum, second_sum = lax.psum((gain_rows, second_grad), ("dp", "layer"))
    up_sum, down_sum, *projections, output_sum, first_part = unpack_grads(
        weight_sum, hidden, heads, part, []
    )
    first_sum = total_of(
        [first_part]
        + [
            lax.ppermute(first_part, "layer", [(i, (i + k) % count) for i in range(count)])
            for k in range(1, count)
        ]
    )
    first_sum = lax.all_gather(first_sum[:, :mixes], "dp", axis=0, tiled=True)
    history_grad, mix_back = history_grads(
        mix_cols, history, near, hidden_rows, [output_sum, first_sum, gains_sum]
    )
    mix_grad = mix_back.T.reshape(4, stored, row_tok)
    return (
        block.astype(bf16),
        next_mix,
        history_grad,
        mix_grad,
        *projections,
        output_sum,
        up_sum,
        down_sum,
        gains_sum,
        first_sum,
        second_sum,
    )


def solution(mesh):
    placed = (
        P("layer", "dp", None),
        P(None, "layer", "dp"),
        P("dp", None),
        P("dp", "layer"),
        P("dp", "layer"),
        P("dp", "layer"),
        P("layer", "dp"),
        P("dp", "layer"),
        P("layer", "dp"),
        P(),
        P(),
        P(),
        P(("dp", "layer"), None),
        P(("dp", "layer"), None),
    )
    return jax.shard_map(
        local,
        mesh=mesh,
        in_specs=placed,
        out_specs=(
            P(("dp", "layer"), None),
            P(("dp", "layer"), None),
            P("layer", "dp", None),
            P(None, "layer", "dp"),
            P("dp", "layer"),
            P("dp", "layer"),
            P("dp", "layer"),
            P("layer", "dp"),
            P("dp", "layer"),
            P("layer", "dp"),
            P(),
            P(),
            P(),
        ),
        check_vma=False,
    )
```

```python
import math

import jax
import jax.numpy as jnp
from jax import lax
from jax.experimental import pallas as pl
from jax.experimental.pallas import tpu as pltpu
from jax.sharding import PartitionSpec as P

HEAD_DIM = 128
DOCS = 2


highest = lax.Precision.HIGHEST
epsilon = 1e-05
bf16 = jnp.bfloat16
f32 = jnp.float32
CHUNK = 16


def rms_norm(values, gain_vec):
    square = jnp.mean(values * values, axis=-1, keepdims=True)
    return values * lax.rsqrt(square + epsilon) * gain_vec


def gelu_exact(values):
    return jax.nn.gelu(values, approximate=False)


def mixer(out_rows, gain_vec, first_matrix, second_matrix):
    hidden = gelu_exact(jnp.dot(rms_norm(out_rows, gain_vec), first_matrix, precision=highest))
    return jnp.dot(hidden, second_matrix, precision=highest)


def plain_dot(left, right):
    return jnp.dot(left, right, preferred_element_type=f32)


def dot_left_t(left, right):
    return lax.dot_general(left, right, (((0,), (0,)), ((), ())), preferred_element_type=f32)


def dot_right_t(left, right):
    return lax.dot_general(left, right, (((1,), (1,)), ((), ())), preferred_element_type=f32)


def doubling_sum(value, axis):
    size = lax.axis_size(axis)
    step = 1
    while step < size:
        value = value + lax.ppermute(value, axis, [(i, i ^ step) for i in range(size)])
        step *= 2
    return value


def total_of(pieces):
    total = pieces[0]
    for piece in pieces[1:]:
        total = total + piece
    return total


def join(values, others):
    anywhere = pl.BlockSpec(memory_space=pl.ANY)
    return list(
        pl.pallas_call(
            lambda *refs: None,
            in_specs=[anywhere] * (len(values) + len(others)),
            out_specs=[anywhere] * len(values),
            out_shape=[jax.ShapeDtypeStruct(v.shape, v.dtype) for v in values],
            input_output_aliases={i: i for i in range(len(values))},
        )(*values, *others)
    )


def after(value, *others):
    return join([value], others)[0]


def sum_line(blocks, count):
    up = down = None
    for k in range(1, count):
        up = blocks[k] if up is None else blocks[k] + up
        up = lax.ppermute(up, "layer", [(i, i + 1) for i in range(k)])
        down = blocks[count - k] if down is None else blocks[count - k] + down
        down = lax.ppermute(down, "layer", [(i, i - 1) for i in range(count - k, count)])
    return [blocks[0], up, down]


def vmem(megabytes):
    return pltpu.CompilerParams(vmem_limit_bytes=megabytes << 20)


def row_loop(rows, body, carry):
    return lax.fori_loop(
        0, rows // CHUNK, lambda i, c: body(pl.ds(pl.multiple_of(i * CHUNK, CHUNK), CHUNK), c), carry
    )


def stream_kernel(mix_ref, hist_ref, near_ref, rest_ref, *, stored):
    width = rest_ref.shape[1]
    lanes = 512

    def body(at, carry):
        mix = mix_ref[at, :]
        for c in range(0, width, lanes):
            rows = [hist_ref[j, at, c : c + lanes].astype(f32) for j in range(stored)]
            for s in range(4):
                total = total_of(
                    [rows[j] * mix[:, s * stored + j : s * stored + j + 1] for j in range(stored)]
                ).astype(bf16)
                if s < 3:
                    near_ref[at, s * width + c : s * width + c + lanes] = total
                else:
                    rest_ref[at, c : c + lanes] = total
        return carry

    row_loop(rest_ref.shape[0], body, 0)


def stream_sums(mix_cols, history):
    stored, tokens, width = history.shape
    rows = 128
    here = lambda i: (i, 0)
    return pl.pallas_call(
        lambda *refs: stream_kernel(*refs, stored=stored),
        grid=(tokens // rows,),
        in_specs=[
            pl.BlockSpec((rows, 4 * stored), here),
            pl.BlockSpec((stored, rows, width), lambda i: (0, i, 0)),
        ],
        out_specs=[pl.BlockSpec((rows, 3 * width), here), pl.BlockSpec((rows, width), here)],
        out_shape=[
            jax.ShapeDtypeStruct((tokens, 3 * width), bf16),
            jax.ShapeDtypeStruct((tokens, width), bf16),
        ],
        compiler_params=vmem(48),
    )(mix_cols, history)


def streams_norm(values, gains):
    width = gains.shape[1]

    def kernel(gain_ref, value_ref, norm_ref):
        for s in range(3):
            cols = slice(s * width, (s + 1) * width)

            def body(at, carry, s=s, cols=cols):
                rows = value_ref[at, cols].astype(f32)
                centre = rows - jnp.mean(rows, axis=1, keepdims=True)
                spread = jnp.mean(centre * centre, axis=1, keepdims=True)
                normed = centre * lax.rsqrt(spread + epsilon) * gain_ref[s : s + 1, :]
                norm_ref[at, cols] = normed.astype(bf16)
                return carry

            row_loop(value_ref.shape[0], body, 0)

    return pl.pallas_call(
        kernel,
        out_shape=jax.ShapeDtypeStruct(values.shape, bf16),
        compiler_params=vmem(48),
    )(gains, values)


def row_norm(values, gain_vec):
    def kernel(gain_ref, value_ref, norm_ref):
        def body(at, carry):
            rows = value_ref[at, :].astype(f32)
            centre = rows - jnp.mean(rows, axis=1, keepdims=True)
            spread = jnp.mean(centre * centre, axis=1, keepdims=True)
            norm_ref[at, :] = (centre * lax.rsqrt(spread + epsilon) * gain_ref[...]).astype(bf16)
            return carry

        row_loop(value_ref.shape[0], body, 0)

    return pl.pallas_call(
        kernel,
        out_shape=jax.ShapeDtypeStruct(values.shape, bf16),
        compiler_params=vmem(48),
    )(gain_vec[None], values)


def norm_grad(values, grad, gain):
    centre = values - jnp.mean(values, axis=1, keepdims=True)
    inv = lax.rsqrt(jnp.mean(centre * centre, axis=1, keepdims=True) + epsilon)
    hat = centre * inv
    scaled = grad * gain
    back = (
        scaled
        - jnp.mean(scaled, axis=1, keepdims=True)
        - hat * jnp.mean(scaled * hat, axis=1, keepdims=True)
    ) * inv
    return back, jnp.sum(grad * hat, axis=0, keepdims=True)


def back_kernel(gain_ref, value_ref, *refs, parts, based):
    part_refs = refs[:parts]
    base_ref = refs[parts] if based else None
    out_ref, dgain_ref = refs[-2:]

    def body(at, dgain):
        values = value_ref[at, :].astype(f32)
        grad = total_of([p[at, :].astype(f32) for p in part_refs])
        back, dgain_rows = norm_grad(values, grad, gain_ref[...])
        if based:
            back = back + base_ref[at, :]
        out_ref[at, :] = back.astype(bf16)
        return dgain + dgain_rows

    dgain_ref[...] = row_loop(value_ref.shape[0], body, jnp.zeros(dgain_ref.shape, f32))


def norm_back(values, parts, gain_vec, base=None, order=()):
    width = gain_vec.shape[0]
    operands = [gain_vec[None], values] + list(parts) + ([] if base is None else [base])
    arrays, specs = [], []
    for operand in operands:
        array, column = operand if isinstance(operand, tuple) else (operand, 0)
        rows = 1 if array.shape[0] == 1 else values_rows(values)
        arrays.append(array)
        specs.append(pl.BlockSpec((rows, width), lambda i, column=column: (0, column)))
    number = len(arrays)
    rows = values_rows(values)
    whole = lambda i: (0, 0)
    back, dgain = pl.pallas_call(
        lambda *refs: back_kernel(
            *refs[:number], *refs[-2:], parts=len(parts), based=base is not None
        ),
        grid=(1,),
        in_specs=specs + [pl.BlockSpec(memory_space=pl.ANY)] * len(order),
        out_specs=[pl.BlockSpec((rows, width), whole), pl.BlockSpec((1, width), whole)],
        out_shape=[
            jax.ShapeDtypeStruct((rows, width), bf16),
            jax.ShapeDtypeStruct((1, width), f32),
        ],
        compiler_params=vmem(48),
    )(*arrays, *order)
    return back, dgain[0]


def values_rows(values):
    return (values[0] if isinstance(values, tuple) else values).shape[0]


def history_kernel(mix_ref, hist_ref, *refs, stored):
    grad_refs, (hist_out, mix_out) = refs[:4], refs[-2:]
    rows, width = hist_out.shape[1:]
    lanes = 512
    group = 64

    token = lax.broadcasted_iota(jnp.int32, (group, stored * group), 0)
    other = lax.broadcasted_iota(jnp.int32, (group, stored * group), 1)
    for g in range(0, rows, group):
        grads = jnp.concatenate([r[g : g + group, :] for r in grad_refs], axis=0)
        stored_rows = jnp.concatenate([hist_ref[j, g : g + group, :] for j in range(stored)], axis=0)
        pairs = contract_cols(grads, stored_rows)
        columns = []
        for s in range(4):
            part = pairs[s * group : (s + 1) * group, :]
            for j in range(stored):
                kept = jnp.where(other == token + j * group, part, 0.0)
                columns.append(jnp.sum(kept, axis=1, keepdims=True))
        mix_out[g : g + group, :] = jnp.concatenate(columns, axis=1)

    def body(at, carry):
        mix = mix_ref[at, :]
        for c in range(0, width, lanes):
            cols = slice(c, c + lanes)
            wide = [r[at, cols].astype(f32) for r in grad_refs]
            for j in range(stored):
                total = total_of(
                    [wide[s] * mix[:, s * stored + j : s * stored + j + 1] for s in range(4)]
                )
                hist_out[j, at, cols] = total.astype(bf16)
        return carry

    row_loop(rows, body, 0)


def history_grads(mix_cols, history, grads, order):
    stored, tokens, width = history.shape
    rows = 128
    here = lambda i: (i, 0)
    there = lambda i: (0, i, 0)
    return pl.pallas_call(
        lambda *refs: history_kernel(*refs, stored=stored),
        grid=(tokens // rows,),
        in_specs=[
            pl.BlockSpec((rows, 4 * stored), here),
            pl.BlockSpec((stored, rows, width), there),
        ]
        + [pl.BlockSpec((rows, width), lambda i, column=column: (i, column)) for _, column in grads]
        + [pl.BlockSpec(memory_space=pl.ANY)] * len(order),
        out_specs=[
            pl.BlockSpec((stored, rows, width), there),
            pl.BlockSpec((rows, 4 * stored), here),
        ],
        out_shape=[
            jax.ShapeDtypeStruct((stored, tokens, width), bf16),
            jax.ShapeDtypeStruct((tokens, 4 * stored), f32),
        ],
        compiler_params=vmem(48),
    )(mix_cols, history, *[g for g, _ in grads], *order)


def contract_rows(left, right):
    return lax.dot_general(left, right, (((0,), (0,)), ((), ())), preferred_element_type=f32)


def contract_cols(left, right):
    return lax.dot_general(left, right, (((1,), (1,)), ((), ())), preferred_element_type=f32)


def mlp_grads(mlp_rows, up_low, branch_rows, active, part):
    tokens, width = mlp_rows.shape
    hidden = active.shape[1]
    rows = 256

    def kernel(mlp_ref, up_ref, branch_ref, active_ref, out_ref):
        out_ref[:, :hidden] = contract_rows(mlp_ref[...], up_ref[...]).astype(bf16)
        out_ref[:, hidden : 2 * hidden] = contract_rows(branch_ref[...], active_ref[...]).astype(bf16)
        out_ref[:, 2 * hidden :] = jnp.zeros((rows, 2 * part - 2 * hidden), bf16)

    side = pl.BlockSpec((tokens, rows), lambda i: (0, i))
    return pl.pallas_call(
        kernel,
        grid=(width // rows,),
        in_specs=[side, resident(up_low), side, resident(active)],
        out_specs=pl.BlockSpec((rows, 2 * part), lambda i: (i, 0)),
        out_shape=jax.ShapeDtypeStruct((width, 3 * part), bf16),
        compiler_params=vmem(56),
    )(mlp_rows, up_low, branch_rows, active)


def attention_grads(so_far, near, lin_grads, hidden_rows, context, first, part, order):
    tokens, width = hidden_rows.shape
    heads = context.shape[1]
    rows = 256

    def kernel(q_ref, k_ref, v_ref, dq_ref, dk_ref, dv_ref, hidden_ref, ctx_ref, first_ref, *refs):
        out_ref = refs[-1]
        pairs = ((q_ref, dq_ref), (k_ref, dk_ref), (v_ref, dv_ref), (hidden_ref, ctx_ref))
        for s, (left, right) in enumerate(pairs):
            out_ref[:, s * heads : (s + 1) * heads] = contract_rows(left[...], right[...]).astype(bf16)
        out_ref[:, 4 * heads :] = first_ref[...].astype(bf16)

    side = pl.BlockSpec((tokens, rows), lambda i: (0, i))
    return pl.pallas_call(
        kernel,
        grid=(width // rows,),
        in_specs=[
            pl.BlockSpec((tokens, rows), lambda i, s=s: (0, s * (width // rows) + i))
            for s in range(3)
        ]
        + [resident(lin_grads[0])] * 3
        + [side, resident(context)]
        + [pl.BlockSpec((rows, first.shape[1]), lambda i: (i, 0))]
        + [pl.BlockSpec(memory_space=pl.ANY)] * (1 + len(order)),
        out_specs=pl.BlockSpec((rows, part), lambda i: (i, 2)),
        out_shape=jax.ShapeDtypeStruct(so_far.shape, bf16),
        input_output_aliases={9: 0},
        compiler_params=vmem(56),
    )(near, near, near, *lin_grads, hidden_rows, context, first, so_far, *order)


def round_weights(weights, turned, order):
    heights = [w.shape[1] if t else w.shape[0] for w, t in zip(weights, turned)]
    widths = [w.shape[0] if t else w.shape[1] for w, t in zip(weights, turned)]
    number = len(weights)

    def kernel(*refs):
        at = 0
        for ref, t, size in zip(refs[:number], turned, widths):
            value = ref[...].T if t else ref[...]
            refs[-1][:, at : at + size] = value.astype(bf16)
            at += size

    return pl.pallas_call(
        kernel,
        in_specs=[pl.BlockSpec(memory_space=pltpu.VMEM)] * number
        + [pl.BlockSpec(memory_space=pl.ANY)] * len(order),
        out_shape=jax.ShapeDtypeStruct((heights[0], sum(widths)), bf16),
        compiler_params=vmem(56),
    )(*weights, *order)


def feed_forward(rows, full, up_first):
    tokens, width = rows.shape
    hidden = (full.shape[1] - up_first) // 2
    cols = 512
    first = up_first // cols
    steps = hidden // cols

    def kernel(rows_ref, up_ref, down_ref, active_ref, slope_ref, out_ref, total_ref):
        step = pl.program_id(0)
        up = jnp.dot(rows_ref[...], up_ref[...], preferred_element_type=f32)
        below = 0.5 * (1.0 + lax.erf(up * (0.5**0.5)))
        active = (up * below).astype(bf16)
        active_ref[...] = active
        slope_ref[...] = below + up * jnp.exp(-0.5 * up * up) * ((2.0 * math.pi) ** -0.5)
        share = contract_cols(active, down_ref[...])

        @pl.when(step == 0)
        def _():
            total_ref[...] = share

        @pl.when(step > 0)
        def _():
            total_ref[...] += share

        @pl.when(step == steps - 1)
        def _():
            out_ref[...] = total_ref[...].astype(bf16)

    part = pl.BlockSpec((tokens, cols), lambda i: (0, i))
    return pl.pallas_call(
        kernel,
        grid=(steps,),
        in_specs=[
            resident(rows),
            pl.BlockSpec((width, cols), lambda i: (0, first + i)),
            pl.BlockSpec((width, cols), lambda i: (0, first + steps + i)),
        ],
        out_specs=[part, part, pl.BlockSpec((tokens, width), lambda i: (0, 0))],
        out_shape=[
            jax.ShapeDtypeStruct((tokens, hidden), bf16),
            jax.ShapeDtypeStruct((tokens, hidden), f32),
            jax.ShapeDtypeStruct((tokens, width), bf16),
        ],
        scratch_shapes=[pltpu.VMEM((tokens, width), f32)],
        compiler_params=vmem(60),
    )(rows, full, full)


def feed_back(rows, full, up_first, slope):
    tokens, width = rows.shape
    hidden = slope.shape[1]
    cols = 512
    first = up_first // cols
    steps = hidden // cols

    def kernel(rows_ref, up_ref, down_ref, slope_ref, *refs):
        low_ref, out_ref, total_ref = refs[-3:]
        step = pl.program_id(0)
        grad = jnp.dot(rows_ref[...], down_ref[...], preferred_element_type=f32)
        low = (grad * slope_ref[...]).astype(bf16)
        low_ref[...] = low
        share = contract_cols(low, up_ref[...])

        @pl.when(step == 0)
        def _():
            total_ref[...] = share

        @pl.when(step > 0)
        def _():
            total_ref[...] += share

        @pl.when(step == steps - 1)
        def _():
            out_ref[...] = total_ref[...].astype(bf16)

    part = pl.BlockSpec((tokens, cols), lambda i: (0, i))
    return pl.pallas_call(
        kernel,
        grid=(steps,),
        in_specs=[
            resident(rows),
            pl.BlockSpec((width, cols), lambda i: (0, first + i)),
            pl.BlockSpec((width, cols), lambda i: (0, first + steps + i)),
            part,
        ],
        out_specs=[part, pl.BlockSpec((tokens, width), lambda i: (0, 0))],
        out_shape=[
            jax.ShapeDtypeStruct((tokens, hidden), bf16),
            jax.ShapeDtypeStruct((tokens, width), bf16),
        ],
        scratch_shapes=[pltpu.VMEM((tokens, width), f32)],
        compiler_params=vmem(60),
    )(rows, full, full, slope)


def turn(values, cosine, sine):
    return values * cosine + pltpu.roll(values, HEAD_DIM // 2, 1) * sine


def score_block(queries, keys, allowed):
    scores = lax.dot_general(
        queries, keys, (((1,), (1,)), ((), ())), preferred_element_type=f32
    ) * (HEAD_DIM ** (-0.5))
    return jnp.where(allowed, scores, -1e30)


def allowed_block(row_ids, col_ids):
    return (row_ids[:, 0:1] == col_ids[0:1, :]) & (row_ids[:, 1:2] >= col_ids[1:2, :])


GROUP = 2


def attend_kernel(
    rows_ref, cols_ref, cos_ref, sin_ref, near_ref, rest_ref, wq_ref, wk_ref, wv_ref, wo_ref,
    ctx_ref, qr_ref, kr_ref, v_ref, lse_ref, out_ref, total_ref,
):
    step = pl.program_id(0)
    width = out_ref.shape[1]
    allowed = allowed_block(rows_ref[...], cols_ref[...])

    def lin(s, weight_ref):
        rows = near_ref[:, s * width : (s + 1) * width]
        return jnp.dot(rows, weight_ref[...], preferred_element_type=f32)

    q_lin, k_lin = lin(0, wq_ref), lin(1, wk_ref)
    v_ref[...] = lin(2, wv_ref).astype(bf16)
    for g in range(GROUP):
        cols = slice(g * HEAD_DIM, (g + 1) * HEAD_DIM)
        queries = turn(q_lin[:, cols], cos_ref[...], sin_ref[...]).astype(bf16)
        keys = turn(k_lin[:, cols], cos_ref[...], sin_ref[...]).astype(bf16)
        qr_ref[:, cols] = queries
        kr_ref[:, cols] = keys
        scores = score_block(queries, keys, allowed)
        row_max = jnp.max(scores, axis=1, keepdims=True)
        shifted = jnp.exp(scores - row_max)
        row_sum = jnp.sum(shifted, axis=1, keepdims=True)
        probs = (shifted / row_sum).astype(bf16)
        context = jnp.dot(probs, v_ref[:, cols], preferred_element_type=f32)
        ctx_ref[:, cols] = context.astype(bf16)
        lse_ref[g] = row_max + jnp.log(row_sum)
    share = contract_cols(ctx_ref[...], wo_ref[...])

    @pl.when(step == 0)
    def _():
        total_ref[...] = share + rest_ref[...].astype(f32)

    @pl.when(step > 0)
    def _():
        total_ref[...] += share

    @pl.when(step == pl.num_programs(0) - 1)
    def _():
        out_ref[...] = total_ref[...].astype(bf16)


def resident(array):
    return pl.BlockSpec(
        array.shape, lambda i: (0,) * array.ndim, pipeline_mode=pl.Buffered(buffer_count=1)
    )


def head_columns(full, first):
    lanes = GROUP * HEAD_DIM
    return pl.BlockSpec((full.shape[0], lanes), lambda h: (0, first // lanes + h))


def attend(row_ids, col_ids, cosine, sine, near, rest, full, heads):
    tokens, width = rest.shape
    head = pl.BlockSpec((tokens, GROUP * HEAD_DIM), lambda h: (0, h))
    fixed = [row_ids, col_ids, cosine, sine, near, rest]

    return pl.pallas_call(
        attend_kernel,
        grid=(heads // HEAD_DIM // GROUP,),
        in_specs=[resident(a) for a in fixed]
        + [head_columns(full, s * heads) for s in range(4)],
        out_specs=[head] * 4
        + [
            pl.BlockSpec((GROUP, tokens, 1), lambda h: (h, 0, 0)),
            pl.BlockSpec((tokens, width), lambda h: (0, 0)),
        ],
        out_shape=[jax.ShapeDtypeStruct((tokens, heads), bf16)] * 4
        + [
            jax.ShapeDtypeStruct((heads // HEAD_DIM, tokens, 1), f32),
            jax.ShapeDtypeStruct((tokens, width), bf16),
        ],
        scratch_shapes=[pltpu.VMEM((tokens, width), f32)],
        compiler_params=vmem(60),
    )(*fixed, *[full] * 4)


def attend_back_kernel(
    rows_ref, cols_ref, cos_ref, sin_ref, hidden_ref, wo_ref, q_ref, k_ref, v_ref, lse_ref,
    dq_ref, dk_ref, dv_ref,
):
    allowed = allowed_block(rows_ref[...], cols_ref[...])
    scale = HEAD_DIM ** (-0.5)
    grads = jnp.dot(hidden_ref[...], wo_ref[...], preferred_element_type=f32).astype(bf16)
    for g in range(GROUP):
        cols = slice(g * HEAD_DIM, (g + 1) * HEAD_DIM)
        queries, keys, values, grad = q_ref[:, cols], k_ref[:, cols], v_ref[:, cols], grads[:, cols]
        probs = jnp.exp(score_block(queries, keys, allowed) - lse_ref[g])
        prob_grad = contract_cols(grad, values)
        dv_ref[:, cols] = contract_rows(probs.astype(bf16), grad).astype(bf16)
        centre = jnp.sum(probs * prob_grad, axis=1, keepdims=True)
        score_grad = (probs * (prob_grad - centre)).astype(bf16)
        dq = jnp.dot(score_grad, keys, preferred_element_type=f32) * scale
        dk = contract_rows(score_grad, queries) * scale
        dq_ref[:, cols] = turn(dq, cos_ref[...], -sin_ref[...]).astype(bf16)
        dk_ref[:, cols] = turn(dk, cos_ref[...], -sin_ref[...]).astype(bf16)


def attend_back(row_ids, col_ids, cosine, sine, hidden_rows, full, queries, keys, values, lse):
    tokens, heads = queries.shape
    head = pl.BlockSpec((tokens, GROUP * HEAD_DIM), lambda h: (0, h))
    fixed = [row_ids, col_ids, cosine, sine, hidden_rows]

    return pl.pallas_call(
        attend_back_kernel,
        grid=(heads // HEAD_DIM // GROUP,),
        in_specs=[resident(a) for a in fixed]
        + [head_columns(full, 3 * heads), head, head, head]
        + [pl.BlockSpec((GROUP, tokens, 1), lambda h: (h, 0, 0))],
        out_specs=[head, head, head],
        out_shape=[jax.ShapeDtypeStruct((tokens, heads), bf16)] * 3,
        compiler_params=vmem(60),
    )(*fixed, full, queries, keys, values, lse)


def stream_shares(where, lin_grads, full):
    tokens, heads = lin_grads[0].shape
    width = full.shape[0]
    count = where.shape[0]
    block = tokens // count

    def kernel(where_ref, dq_ref, dk_ref, dv_ref, full_ref, *out_refs):
        for s, ref in enumerate((dq_ref, dk_ref, dv_ref)):

            @pl.when(pl.program_id(0) == s)
            def _(ref=ref, out_ref=out_refs[s]):
                share = contract_cols(ref[...], full_ref[...]).astype(bf16)
                for j in range(count):
                    at = pl.ds(pl.multiple_of(where_ref[j] * block, block), block)
                    out_ref[at, :] = share[j * block : (j + 1) * block, :]

    fixed = pl.BlockSpec(
        (tokens, heads), lambda s, w: (0, 0), pipeline_mode=pl.Buffered(buffer_count=1)
    )
    return pl.pallas_call(
        kernel,
        grid_spec=pltpu.PrefetchScalarGridSpec(
            num_scalar_prefetch=1,
            grid=(3,),
            in_specs=[fixed] * 3 + [pl.BlockSpec((width, heads), lambda s, w: (0, s))],
            out_specs=[pl.BlockSpec((tokens, width), lambda s, w: (0, 0))] * 3,
        ),
        out_shape=[jax.ShapeDtypeStruct((tokens, width), bf16)] * 3,
        compiler_params=vmem(56),
    )(where, *lin_grads, full)


def unpack_grads(weight_sum, hidden, heads, part, mixes, order):
    rows = weight_sum.shape[0]

    def kernel(sum_ref, *refs):
        up_ref, down_ref, q_ref, k_ref, v_ref, o_ref, first_ref = refs[-7:]
        up_ref[...] = sum_ref[:, :hidden].astype(f32)
        down_ref[...] = sum_ref[:, hidden : 2 * hidden].astype(f32).T
        at = 2 * part
        for ref in (q_ref, k_ref, v_ref):
            ref[...] = sum_ref[:, at : at + heads].astype(f32)
            at += heads
        o_ref[...] = sum_ref[:, at : at + heads].astype(f32).T
        first_ref[...] = sum_ref[:, at + heads :].astype(f32).T[: first_ref.shape[0], :]

    shapes = [(rows, hidden), (hidden, rows)] + [(rows, heads)] * 3
    shapes += [(heads, rows), (mixes + -mixes % 8, rows)]
    return pl.pallas_call(
        kernel,
        in_specs=[pl.BlockSpec(memory_space=pltpu.VMEM)]
        + [pl.BlockSpec(memory_space=pl.ANY)] * len(order),
        out_shape=[jax.ShapeDtypeStruct(shape, f32) for shape in shapes],
        compiler_params=vmem(56),
    )(weight_sum, *order)


def places(seg_row):
    length = seg_row.shape[0]
    labels = jnp.arange(DOCS, dtype=jnp.int32)
    before = jnp.sum((seg_row[None, :] < labels[:, None]).astype(jnp.int32), axis=1)
    member = (seg_row[:, None] == labels[None, :]).astype(jnp.int32)
    begins = jnp.sum(member * before[None, :], axis=1)
    return jnp.arange(length, dtype=jnp.int32) - begins


def local(
    history,
    mix_weights,
    segments,
    w_query,
    w_key,
    w_value,
    w_output,
    w_up,
    w_down,
    norm_gains,
    w_first,
    w_second,
    out_cotangent,
    mix_cotangent,
):
    stored, row_tok, width = history.shape
    count = lax.axis_size("layer")
    me = lax.axis_index("layer")
    own_tok = row_tok // count
    order = [(me - k) % count for k in range(count)]

    def block_of(rows, k):
        return rows[k * own_tok : (k + 1) * own_tok]

    def blocks_of(rows):
        return [block_of(rows, k) for k in range(count)]

    def collect(rows):
        return lax.all_gather(rows, "layer", axis=0, tiled=True)

    def spread(rows):
        return lax.psum_scatter(rows, "layer", scatter_dimension=0, tiled=True)

    hidden = w_up.shape[1]
    heads = w_query.shape[1]
    mix_cols = mix_weights.reshape(4 * stored, row_tok).T
    near_shares, rest_share = stream_sums(mix_cols, history)
    low = round_weights(
        [w_query, w_key, w_value, w_output, w_up, w_down],
        [False, False, False, True, False, True],
        [near_shares],
    )
    full = lax.all_gather(low, "dp", axis=0, tiled=True)
    stream_own = spread(near_shares)
    normed_rows = collect(after(streams_norm(stream_own, norm_gains[:3]), full))

    seg_row = segments[0]
    place_row = places(seg_row)
    col_ids = jnp.stack([seg_row, jnp.arange(row_tok, dtype=jnp.int32)])
    half = HEAD_DIM // 2
    frequency = jnp.exp(jnp.arange(half, dtype=f32) * (-2.0 * math.log(10000.0) / HEAD_DIM))
    angles = place_row.astype(f32)[:, None] * frequency[None, :]
    cosine, sine = jnp.cos(angles), jnp.sin(angles)
    cosine = jnp.concatenate([cosine, cosine], axis=1)
    sine = jnp.concatenate([-sine, sine], axis=1)
    row_ids = col_ids.T

    context, queries, keys, values, lse, hidden_part = attend(
        row_ids, col_ids, cosine, sine, normed_rows, rest_share, full, heads
    )
    hidden_in = spread(hidden_part)
    mlp_norm = row_norm(hidden_in, norm_gains[3])
    mlp_rows = collect(mlp_norm)
    active, slope, mlp_part = feed_forward(mlp_rows, full, 4 * heads)
    block = hidden_in.astype(f32) + spread(mlp_part).astype(f32)

    next_mix, mixer_pull = jax.vjp(mixer, block, norm_gains[4], w_first, w_second)
    block_part, mixer_gain_grad, first_grad, second_grad = mixer_pull(mix_cotangent)
    block_grad = out_cotangent + block_part
    branch_rows = collect(block_grad.astype(bf16))
    up_low, mlp_part = feed_back(branch_rows, full, 4 * heads, slope)
    mlp_back = spread(mlp_part)
    part = 4 * heads + 128
    weight_grads = mlp_grads(mlp_rows, after(up_low, mlp_part), branch_rows, active, part)
    hidden_low, mlp_gain_grad = norm_back(
        hidden_in, [mlp_back], norm_gains[3], block_grad, [weight_grads]
    )
    hidden_rows = collect(hidden_low)
    lin_grads = attend_back(
        row_ids, col_ids, cosine, sine, hidden_rows, full, queries, keys, values, lse
    )
    table = jnp.stack(order).astype(jnp.int32)
    stream_parts = stream_shares(table, lin_grads, full)
    mixes = first_grad.shape[1]
    weight_grads = attention_grads(
        weight_grads,
        normed_rows,
        lin_grads,
        hidden_rows,
        context,
        jnp.pad(first_grad, ((0, 0), (0, 128 - mixes))),
        part,
        [stream_parts[0]],
    )
    weight_sum = lax.psum_scatter(weight_grads, "dp", scatter_dimension=0, tiled=True)
    gain_grads, stream_low = [], []
    for s in range(3):
        low, gain_grad = norm_back(
            (stream_own, s), sum_line(blocks_of(stream_parts[s]), count), norm_gains[s]
        )
        gain_grads.append(gain_grad)
        stream_low.append(low)
    near = collect(jnp.concatenate(stream_low, axis=1))

    gain_rows = jnp.stack(gain_grads + [mlp_gain_grad, mixer_gain_grad])
    lines = -(-mixes * mixes // width)
    second_flat = jnp.pad(second_grad.reshape(-1), (0, lines * width - mixes * mixes))
    small = jnp.concatenate([gain_rows, second_flat.reshape(lines, width)])
    small = doubling_sum(doubling_sum(small, "dp"), "layer")
    up_sum, down_sum, *projections, output_sum, first_part = unpack_grads(
        weight_sum, hidden, heads, part, mixes, [small]
    )
    gains_sum = small[:5]
    second_sum = small[5:].reshape(-1)[: mixes * mixes].reshape(mixes, mixes)
    first_sum = lax.all_gather(doubling_sum(first_part, "layer"), "dp", axis=1, tiled=True)[:mixes].T
    history_grad, mix_back = history_grads(
        mix_cols,
        history,
        [(near, 0), (near, 1), (near, 2), (hidden_rows, 0)],
        [output_sum, first_sum, small],
    )
    mix_grad = mix_back.T.reshape(4, stored, row_tok)
    return (
        block.astype(bf16),
        next_mix,
        history_grad,
        mix_grad,
        *projections,
        output_sum,
        up_sum,
        down_sum,
        gains_sum,
        first_sum,
        second_sum,
    )


def solution(mesh):
    placed = (
        P("layer", "dp", None),
        P(None, "layer", "dp"),
        P("dp", None),
        P("dp", "layer"),
        P("dp", "layer"),
        P("dp", "layer"),
        P("layer", "dp"),
        P("dp", "layer"),
        P("layer", "dp"),
        P(),
        P(),
        P(),
        P(("dp", "layer"), None),
        P(("dp", "layer"), None),
    )
    return jax.shard_map(
        local,
        mesh=mesh,
        in_specs=placed,
        out_specs=(
            P(("dp", "layer"), None),
            P(("dp", "layer"), None),
            P("layer", "dp", None),
            P(None, "layer", "dp"),
            P("dp", "layer"),
            P("dp", "layer"),
            P("dp", "layer"),
            P("layer", "dp"),
            P("dp", "layer"),
            P("layer", "dp"),
            P(),
            P(),
            P(),
        ),
        check_vma=False,
    )
```

```python
import math

import jax
import jax.numpy as jnp
from jax import lax
from jax.experimental import pallas as pl
from jax.experimental.pallas import tpu as pltpu
from jax.sharding import PartitionSpec as P

HEAD_DIM = 128
DOCS = 2


highest = lax.Precision.HIGHEST
epsilon = 1e-05
bf16 = jnp.bfloat16
f32 = jnp.float32
CHUNK = 16


def rms_norm(values, gain_vec):
    square = jnp.mean(values * values, axis=-1, keepdims=True)
    return values * lax.rsqrt(square + epsilon) * gain_vec


def gelu_exact(values):
    return jax.nn.gelu(values, approximate=False)


def mixer(out_rows, gain_vec, first_matrix, second_matrix):
    hidden = gelu_exact(jnp.dot(rms_norm(out_rows, gain_vec), first_matrix, precision=highest))
    return jnp.dot(hidden, second_matrix, precision=highest)


def plain_dot(left, right):
    return jnp.dot(left, right, preferred_element_type=f32)


def dot_left_t(left, right):
    return lax.dot_general(left, right, (((0,), (0,)), ((), ())), preferred_element_type=f32)


def dot_right_t(left, right):
    return lax.dot_general(left, right, (((1,), (1,)), ((), ())), preferred_element_type=f32)


def doubling_sum(value, axis):
    size = lax.axis_size(axis)
    step = 1
    while step < size:
        value = value + lax.ppermute(value, axis, [(i, i ^ step) for i in range(size)])
        step *= 2
    return value


def total_of(pieces):
    total = pieces[0]
    for piece in pieces[1:]:
        total = total + piece
    return total


def join(values, others):
    anywhere = pl.BlockSpec(memory_space=pl.ANY)
    return list(
        pl.pallas_call(
            lambda *refs: None,
            in_specs=[anywhere] * (len(values) + len(others)),
            out_specs=[anywhere] * len(values),
            out_shape=[jax.ShapeDtypeStruct(v.shape, v.dtype) for v in values],
            input_output_aliases={i: i for i in range(len(values))},
        )(*values, *others)
    )


def after(value, *others):
    return join([value], others)[0]


def sum_hop(blocks, k, came, count):
    up, down = blocks[k], blocks[count - k]
    if came:
        up, down = up + came[0], down + came[1]
    return [
        lax.ppermute(up, "layer", [(i, i + 1) for i in range(k)]),
        lax.ppermute(down, "layer", [(i, i - 1) for i in range(count - k, count)]),
    ]


def vmem(megabytes):
    return pltpu.CompilerParams(vmem_limit_bytes=megabytes << 20)


def row_loop(rows, body, carry):
    return lax.fori_loop(
        0, rows // CHUNK, lambda i, c: body(pl.ds(pl.multiple_of(i * CHUNK, CHUNK), CHUNK), c), carry
    )


def stream_kernel(mix_ref, hist_ref, near_ref, rest_ref, *, stored):
    width = rest_ref.shape[1]
    lanes = 512

    def body(at, carry):
        mix = mix_ref[at, :]
        for c in range(0, width, lanes):
            rows = [hist_ref[j, at, c : c + lanes].astype(f32) for j in range(stored)]
            for s in range(4):
                total = total_of(
                    [rows[j] * mix[:, s * stored + j : s * stored + j + 1] for j in range(stored)]
                ).astype(bf16)
                if s < 3:
                    near_ref[at, s * width + c : s * width + c + lanes] = total
                else:
                    rest_ref[at, c : c + lanes] = total
        return carry

    row_loop(rest_ref.shape[0], body, 0)


def stream_sums(mix_cols, history):
    stored, tokens, width = history.shape
    rows = 128
    here = lambda i: (i, 0)
    return pl.pallas_call(
        lambda *refs: stream_kernel(*refs, stored=stored),
        grid=(tokens // rows,),
        in_specs=[
            pl.BlockSpec((rows, 4 * stored), here),
            pl.BlockSpec((stored, rows, width), lambda i: (0, i, 0)),
        ],
        out_specs=[pl.BlockSpec((rows, 3 * width), here), pl.BlockSpec((rows, width), here)],
        out_shape=[
            jax.ShapeDtypeStruct((tokens, 3 * width), bf16),
            jax.ShapeDtypeStruct((tokens, width), bf16),
        ],
        compiler_params=vmem(48),
    )(mix_cols, history)


def streams_norm(values, gains):
    block, width = values.shape[0], gains.shape[1]

    def kernel(gain_ref, value_ref, norm_ref):
        gain = gain_ref[pl.ds(pl.program_id(0), 1), :]

        def body(at, carry):
            rows = value_ref[at, :].astype(f32)
            centre = rows - jnp.mean(rows, axis=1, keepdims=True)
            spread = jnp.mean(centre * centre, axis=1, keepdims=True)
            norm_ref[at, :] = (centre * lax.rsqrt(spread + epsilon) * gain).astype(bf16)
            return carry

        row_loop(block, body, 0)

    stream = pl.BlockSpec((block, width), lambda s: (0, s))
    return pl.pallas_call(
        kernel,
        grid=(3,),
        in_specs=[pl.BlockSpec(gains.shape, lambda s: (0, 0)), stream],
        out_specs=stream,
        out_shape=jax.ShapeDtypeStruct(values.shape, bf16),
        compiler_params=vmem(48),
    )(gains, values)


def row_norm(values, gain_vec):
    def kernel(gain_ref, value_ref, norm_ref):
        def body(at, carry):
            rows = value_ref[at, :].astype(f32)
            centre = rows - jnp.mean(rows, axis=1, keepdims=True)
            spread = jnp.mean(centre * centre, axis=1, keepdims=True)
            norm_ref[at, :] = (centre * lax.rsqrt(spread + epsilon) * gain_ref[...]).astype(bf16)
            return carry

        row_loop(value_ref.shape[0], body, 0)

    return pl.pallas_call(
        kernel,
        out_shape=jax.ShapeDtypeStruct(values.shape, bf16),
        compiler_params=vmem(48),
    )(gain_vec[None], values)


def norm_grad(values, grad, gain):
    centre = values - jnp.mean(values, axis=1, keepdims=True)
    inv = lax.rsqrt(jnp.mean(centre * centre, axis=1, keepdims=True) + epsilon)
    hat = centre * inv
    scaled = grad * gain
    back = (
        scaled
        - jnp.mean(scaled, axis=1, keepdims=True)
        - hat * jnp.mean(scaled * hat, axis=1, keepdims=True)
    ) * inv
    return back, jnp.sum(grad * hat, axis=0, keepdims=True)


def back_kernel(gain_ref, value_ref, *refs, parts, based):
    part_refs = refs[:parts]
    base_ref = refs[parts] if based else None
    out_ref, dgain_ref = refs[-2:]

    def body(at, dgain):
        values = value_ref[at, :].astype(f32)
        grad = total_of([p[at, :].astype(f32) for p in part_refs])
        back, dgain_rows = norm_grad(values, grad, gain_ref[...])
        if based:
            back = back + base_ref[at, :]
        out_ref[at, :] = back.astype(bf16)
        return dgain + dgain_rows

    dgain_ref[...] = row_loop(value_ref.shape[0], body, jnp.zeros(dgain_ref.shape, f32))


def norm_back(values, parts, gain_vec, base=None, order=()):
    width = gain_vec.shape[0]
    operands = [gain_vec[None], values] + list(parts) + ([] if base is None else [base])
    arrays, specs = [], []
    for operand in operands:
        array, column = operand if isinstance(operand, tuple) else (operand, 0)
        rows = 1 if array.shape[0] == 1 else values_rows(values)
        arrays.append(array)
        specs.append(pl.BlockSpec((rows, width), lambda i, column=column: (0, column)))
    number = len(arrays)
    rows = values_rows(values)
    whole = lambda i: (0, 0)
    back, dgain = pl.pallas_call(
        lambda *refs: back_kernel(
            *refs[:number], *refs[-2:], parts=len(parts), based=base is not None
        ),
        grid=(1,),
        in_specs=specs + [pl.BlockSpec(memory_space=pl.ANY)] * len(order),
        out_specs=[pl.BlockSpec((rows, width), whole), pl.BlockSpec((1, width), whole)],
        out_shape=[
            jax.ShapeDtypeStruct((rows, width), bf16),
            jax.ShapeDtypeStruct((1, width), f32),
        ],
        compiler_params=vmem(48),
    )(*arrays, *order)
    return back, dgain[0]


def values_rows(values):
    return (values[0] if isinstance(values, tuple) else values).shape[0]


def history_kernel(mix_ref, hist_ref, *refs, stored):
    grad_refs, (hist_out, mix_out) = refs[:4], refs[-2:]
    rows, width = hist_out.shape[1:]
    lanes = 512
    group = 64

    token = lax.broadcasted_iota(jnp.int32, (group, stored * group), 0)
    other = lax.broadcasted_iota(jnp.int32, (group, stored * group), 1)
    for g in range(0, rows, group):
        grads = jnp.concatenate([r[g : g + group, :] for r in grad_refs], axis=0)
        stored_rows = jnp.concatenate([hist_ref[j, g : g + group, :] for j in range(stored)], axis=0)
        pairs = contract_cols(grads, stored_rows)
        columns = []
        for s in range(4):
            part = pairs[s * group : (s + 1) * group, :]
            for j in range(stored):
                kept = jnp.where(other == token + j * group, part, 0.0)
                columns.append(jnp.sum(kept, axis=1, keepdims=True))
        mix_out[g : g + group, :] = jnp.concatenate(columns, axis=1)

    def body(at, carry):
        mix = mix_ref[at, :]
        for c in range(0, width, lanes):
            cols = slice(c, c + lanes)
            wide = [r[at, cols].astype(f32) for r in grad_refs]
            for j in range(stored):
                total = total_of(
                    [wide[s] * mix[:, s * stored + j : s * stored + j + 1] for s in range(4)]
                )
                hist_out[j, at, cols] = total.astype(bf16)
        return carry

    row_loop(rows, body, 0)


def history_grads(mix_cols, history, grads, order):
    stored, tokens, width = history.shape
    rows = 128
    here = lambda i: (i, 0)
    there = lambda i: (0, i, 0)
    return pl.pallas_call(
        lambda *refs: history_kernel(*refs, stored=stored),
        grid=(tokens // rows,),
        in_specs=[
            pl.BlockSpec((rows, 4 * stored), here),
            pl.BlockSpec((stored, rows, width), there),
        ]
        + [pl.BlockSpec((rows, width), lambda i, column=column: (i, column)) for _, column in grads]
        + [pl.BlockSpec(memory_space=pl.ANY)] * len(order),
        out_specs=[
            pl.BlockSpec((stored, rows, width), there),
            pl.BlockSpec((rows, 4 * stored), here),
        ],
        out_shape=[
            jax.ShapeDtypeStruct((stored, tokens, width), bf16),
            jax.ShapeDtypeStruct((tokens, 4 * stored), f32),
        ],
        compiler_params=vmem(48),
    )(mix_cols, history, *[g for g, _ in grads], *order)


def contract_rows(left, right):
    return lax.dot_general(left, right, (((0,), (0,)), ((), ())), preferred_element_type=f32)


def contract_cols(left, right):
    return lax.dot_general(left, right, (((1,), (1,)), ((), ())), preferred_element_type=f32)


def mlp_grads(mlp_rows, up_low, branch_rows, active, first):
    tokens, width = mlp_rows.shape
    hidden = active.shape[1]
    rows = 256
    total = 2 * hidden + first.shape[1]

    def kernel(mlp_ref, up_ref, branch_ref, active_ref, first_ref, out_ref):
        out_ref[:, :hidden] = contract_rows(mlp_ref[...], up_ref[...]).astype(bf16)
        out_ref[:, hidden : 2 * hidden] = contract_rows(branch_ref[...], active_ref[...]).astype(bf16)
        out_ref[:, 2 * hidden :] = first_ref[...].astype(bf16)

    side = pl.BlockSpec((tokens, rows), lambda i: (0, i))
    return pl.pallas_call(
        kernel,
        grid=(width // rows,),
        in_specs=[side, resident(up_low), side, resident(active)]
        + [pl.BlockSpec((rows, first.shape[1]), lambda i: (i, 0))],
        out_specs=pl.BlockSpec((rows, total), lambda i: (i, 0)),
        out_shape=jax.ShapeDtypeStruct((width, total), bf16),
        compiler_params=vmem(56),
    )(mlp_rows, up_low, branch_rows, active, first)


def attention_grads(near, lin_grads, hidden_rows, context, order):
    tokens, width = hidden_rows.shape
    heads = context.shape[1]
    rows = 256

    def kernel(q_ref, k_ref, v_ref, dq_ref, dk_ref, dv_ref, hidden_ref, ctx_ref, *refs):
        out_ref = refs[-1]
        pairs = ((q_ref, dq_ref), (k_ref, dk_ref), (v_ref, dv_ref), (hidden_ref, ctx_ref))
        for s, (left, right) in enumerate(pairs):
            out_ref[:, s * heads : (s + 1) * heads] = contract_rows(left[...], right[...]).astype(bf16)

    side = pl.BlockSpec((tokens, rows), lambda i: (0, i))
    return pl.pallas_call(
        kernel,
        grid=(width // rows,),
        in_specs=[
            pl.BlockSpec((tokens, rows), lambda i, s=s: (0, s * (width // rows) + i))
            for s in range(3)
        ]
        + [resident(lin_grads[0])] * 3
        + [side, resident(context)]
        + [pl.BlockSpec(memory_space=pl.ANY)] * len(order),
        out_specs=pl.BlockSpec((rows, 4 * heads), lambda i: (i, 0)),
        out_shape=jax.ShapeDtypeStruct((width, 4 * heads), bf16),
        compiler_params=vmem(56),
    )(near, near, near, *lin_grads, hidden_rows, context, *order)


def round_weights(weights, turned, order):
    heights = [w.shape[1] if t else w.shape[0] for w, t in zip(weights, turned)]
    widths = [w.shape[0] if t else w.shape[1] for w, t in zip(weights, turned)]
    number = len(weights)

    def kernel(*refs):
        at = 0
        for ref, t, size in zip(refs[:number], turned, widths):
            value = ref[...].T if t else ref[...]
            refs[-1][:, at : at + size] = value.astype(bf16)
            at += size

    return pl.pallas_call(
        kernel,
        in_specs=[pl.BlockSpec(memory_space=pltpu.VMEM)] * number
        + [pl.BlockSpec(memory_space=pl.ANY)] * len(order),
        out_shape=jax.ShapeDtypeStruct((heights[0], sum(widths)), bf16),
        compiler_params=vmem(56),
    )(*weights, *order)


def feed_forward(rows, full, up_first):
    tokens, width = rows.shape
    hidden = (full.shape[1] - up_first) // 2
    cols = 512
    first = up_first // cols
    steps = hidden // cols

    def kernel(rows_ref, up_ref, down_ref, active_ref, slope_ref, out_ref, total_ref):
        step = pl.program_id(0)
        up = jnp.dot(rows_ref[...], up_ref[...], preferred_element_type=f32)
        below = 0.5 * (1.0 + lax.erf(up * (0.5**0.5)))
        active = (up * below).astype(bf16)
        active_ref[...] = active
        slope_ref[...] = below + up * jnp.exp(-0.5 * up * up) * ((2.0 * math.pi) ** -0.5)
        share = contract_cols(active, down_ref[...])

        @pl.when(step == 0)
        def _():
            total_ref[...] = share

        @pl.when(step > 0)
        def _():
            total_ref[...] += share

        @pl.when(step == steps - 1)
        def _():
            out_ref[...] = total_ref[...].astype(bf16)

    part = pl.BlockSpec((tokens, cols), lambda i: (0, i))
    return pl.pallas_call(
        kernel,
        grid=(steps,),
        in_specs=[
            resident(rows),
            pl.BlockSpec((width, cols), lambda i: (0, first + i)),
            pl.BlockSpec((width, cols), lambda i: (0, first + steps + i)),
        ],
        out_specs=[part, part, pl.BlockSpec((tokens, width), lambda i: (0, 0))],
        out_shape=[
            jax.ShapeDtypeStruct((tokens, hidden), bf16),
            jax.ShapeDtypeStruct((tokens, hidden), f32),
            jax.ShapeDtypeStruct((tokens, width), bf16),
        ],
        scratch_shapes=[pltpu.VMEM((tokens, width), f32)],
        compiler_params=vmem(60),
    )(rows, full, full)


def feed_back(rows, full, up_first, slope):
    tokens, width = rows.shape
    hidden = slope.shape[1]
    cols = 512
    first = up_first // cols
    steps = hidden // cols

    def kernel(rows_ref, up_ref, down_ref, slope_ref, *refs):
        low_ref, out_ref, total_ref = refs[-3:]
        step = pl.program_id(0)
        grad = jnp.dot(rows_ref[...], down_ref[...], preferred_element_type=f32)
        low = (grad * slope_ref[...]).astype(bf16)
        low_ref[...] = low
        share = contract_cols(low, up_ref[...])

        @pl.when(step == 0)
        def _():
            total_ref[...] = share

        @pl.when(step > 0)
        def _():
            total_ref[...] += share

        @pl.when(step == steps - 1)
        def _():
            out_ref[...] = total_ref[...].astype(bf16)

    part = pl.BlockSpec((tokens, cols), lambda i: (0, i))
    return pl.pallas_call(
        kernel,
        grid=(steps,),
        in_specs=[
            resident(rows),
            pl.BlockSpec((width, cols), lambda i: (0, first + i)),
            pl.BlockSpec((width, cols), lambda i: (0, first + steps + i)),
            part,
        ],
        out_specs=[part, pl.BlockSpec((tokens, width), lambda i: (0, 0))],
        out_shape=[
            jax.ShapeDtypeStruct((tokens, hidden), bf16),
            jax.ShapeDtypeStruct((tokens, width), bf16),
        ],
        scratch_shapes=[pltpu.VMEM((tokens, width), f32)],
        compiler_params=vmem(60),
    )(rows, full, full, slope)


def turn(values, cosine, sine):
    return values * cosine + pltpu.roll(values, HEAD_DIM // 2, 1) * sine


def score_block(queries, keys, allowed):
    scores = lax.dot_general(
        queries, keys, (((1,), (1,)), ((), ())), preferred_element_type=f32
    ) * (HEAD_DIM ** (-0.5))
    return jnp.where(allowed, scores, -1e30)


def allowed_block(row_ids, col_ids):
    return (row_ids[:, 0:1] == col_ids[0:1, :]) & (row_ids[:, 1:2] >= col_ids[1:2, :])


GROUP = 2


def attend_kernel(
    rows_ref, cols_ref, cos_ref, sin_ref, near_ref, rest_ref, wq_ref, wk_ref, wv_ref, wo_ref,
    ctx_ref, qr_ref, kr_ref, v_ref, lse_ref, out_ref, total_ref,
):
    step = pl.program_id(0)
    width = out_ref.shape[1]
    allowed = allowed_block(rows_ref[...], cols_ref[...])

    def lin(s, weight_ref):
        rows = near_ref[:, s * width : (s + 1) * width]
        return jnp.dot(rows, weight_ref[...], preferred_element_type=f32)

    q_lin, k_lin = lin(0, wq_ref), lin(1, wk_ref)
    v_ref[...] = lin(2, wv_ref).astype(bf16)
    for g in range(GROUP):
        cols = slice(g * HEAD_DIM, (g + 1) * HEAD_DIM)
        queries = turn(q_lin[:, cols], cos_ref[...], sin_ref[...]).astype(bf16)
        keys = turn(k_lin[:, cols], cos_ref[...], sin_ref[...]).astype(bf16)
        qr_ref[:, cols] = queries
        kr_ref[:, cols] = keys
        scores = score_block(queries, keys, allowed)
        row_max = jnp.max(scores, axis=1, keepdims=True)
        shifted = jnp.exp(scores - row_max)
        row_sum = jnp.sum(shifted, axis=1, keepdims=True)
        probs = (shifted / row_sum).astype(bf16)
        context = jnp.dot(probs, v_ref[:, cols], preferred_element_type=f32)
        ctx_ref[:, cols] = context.astype(bf16)
        lse_ref[g] = row_max + jnp.log(row_sum)
    share = contract_cols(ctx_ref[...], wo_ref[...])

    @pl.when(step == 0)
    def _():
        total_ref[...] = share + rest_ref[...].astype(f32)

    @pl.when(step > 0)
    def _():
        total_ref[...] += share

    @pl.when(step == pl.num_programs(0) - 1)
    def _():
        out_ref[...] = total_ref[...].astype(bf16)


def resident(array):
    return pl.BlockSpec(
        array.shape, lambda i: (0,) * array.ndim, pipeline_mode=pl.Buffered(buffer_count=1)
    )


def head_columns(full, first):
    lanes = GROUP * HEAD_DIM
    return pl.BlockSpec((full.shape[0], lanes), lambda h: (0, first // lanes + h))


def attend(row_ids, col_ids, cosine, sine, near, rest, full, heads):
    tokens, width = rest.shape
    head = pl.BlockSpec((tokens, GROUP * HEAD_DIM), lambda h: (0, h))
    fixed = [row_ids, col_ids, cosine, sine, near, rest]

    return pl.pallas_call(
        attend_kernel,
        grid=(heads // HEAD_DIM // GROUP,),
        in_specs=[resident(a) for a in fixed]
        + [head_columns(full, s * heads) for s in range(4)],
        out_specs=[head] * 4
        + [
            pl.BlockSpec((GROUP, tokens, 1), lambda h: (h, 0, 0)),
            pl.BlockSpec((tokens, width), lambda h: (0, 0)),
        ],
        out_shape=[jax.ShapeDtypeStruct((tokens, heads), bf16)] * 4
        + [
            jax.ShapeDtypeStruct((heads // HEAD_DIM, tokens, 1), f32),
            jax.ShapeDtypeStruct((tokens, width), bf16),
        ],
        scratch_shapes=[pltpu.VMEM((tokens, width), f32)],
        compiler_params=vmem(60),
    )(*fixed, *[full] * 4)


def attend_back_kernel(
    rows_ref, cols_ref, cos_ref, sin_ref, hidden_ref, wo_ref, q_ref, k_ref, v_ref, lse_ref,
    dq_ref, dk_ref, dv_ref,
):
    allowed = allowed_block(rows_ref[...], cols_ref[...])
    scale = HEAD_DIM ** (-0.5)
    grads = jnp.dot(hidden_ref[...], wo_ref[...], preferred_element_type=f32).astype(bf16)
    for g in range(GROUP):
        cols = slice(g * HEAD_DIM, (g + 1) * HEAD_DIM)
        queries, keys, values, grad = q_ref[:, cols], k_ref[:, cols], v_ref[:, cols], grads[:, cols]
        probs = jnp.exp(score_block(queries, keys, allowed) - lse_ref[g])
        prob_grad = contract_cols(grad, values)
        dv_ref[:, cols] = contract_rows(probs.astype(bf16), grad).astype(bf16)
        centre = jnp.sum(probs * prob_grad, axis=1, keepdims=True)
        score_grad = (probs * (prob_grad - centre)).astype(bf16)
        dq = jnp.dot(score_grad, keys, preferred_element_type=f32) * scale
        dk = contract_rows(score_grad, queries) * scale
        dq_ref[:, cols] = turn(dq, cos_ref[...], -sin_ref[...]).astype(bf16)
        dk_ref[:, cols] = turn(dk, cos_ref[...], -sin_ref[...]).astype(bf16)


def attend_back(row_ids, col_ids, cosine, sine, hidden_rows, full, queries, keys, values, lse):
    tokens, heads = queries.shape
    head = pl.BlockSpec((tokens, GROUP * HEAD_DIM), lambda h: (0, h))
    fixed = [row_ids, col_ids, cosine, sine, hidden_rows]

    return pl.pallas_call(
        attend_back_kernel,
        grid=(heads // HEAD_DIM // GROUP,),
        in_specs=[resident(a) for a in fixed]
        + [head_columns(full, 3 * heads), head, head, head]
        + [pl.BlockSpec((GROUP, tokens, 1), lambda h: (h, 0, 0))],
        out_specs=[head, head, head],
        out_shape=[jax.ShapeDtypeStruct((tokens, heads), bf16)] * 3,
        compiler_params=vmem(60),
    )(*fixed, full, queries, keys, values, lse)


def stream_shares(where, lin_grads, full):
    tokens, heads = lin_grads[0].shape
    width = full.shape[0]
    count = where.shape[0]
    block = tokens // count

    def kernel(where_ref, dq_ref, dk_ref, dv_ref, full_ref, *out_refs):
        for s, ref in enumerate((dq_ref, dk_ref, dv_ref)):

            @pl.when(pl.program_id(0) == s)
            def _(ref=ref, out_ref=out_refs[s]):
                share = contract_cols(ref[...], full_ref[...]).astype(bf16)
                for j in range(count):
                    at = pl.ds(pl.multiple_of(where_ref[j] * block, block), block)
                    out_ref[at, :] = share[j * block : (j + 1) * block, :]

    fixed = pl.BlockSpec(
        (tokens, heads), lambda s, w: (0, 0), pipeline_mode=pl.Buffered(buffer_count=1)
    )
    return pl.pallas_call(
        kernel,
        grid_spec=pltpu.PrefetchScalarGridSpec(
            num_scalar_prefetch=1,
            grid=(3,),
            in_specs=[fixed] * 3 + [pl.BlockSpec((width, heads), lambda s, w: (0, s))],
            out_specs=[pl.BlockSpec((tokens, width), lambda s, w: (0, 0))] * 3,
        ),
        out_shape=[jax.ShapeDtypeStruct((tokens, width), bf16)] * 3,
        compiler_params=vmem(56),
    )(where, *lin_grads, full)


def unpack_mlp(mlp_sum, hidden, mixes):
    rows = mlp_sum.shape[0]

    def kernel(sum_ref, up_ref, down_ref, first_ref):
        up_ref[...] = sum_ref[:, :hidden].astype(f32)
        down_ref[...] = sum_ref[:, hidden : 2 * hidden].astype(f32).T
        first_ref[...] = sum_ref[:, 2 * hidden :].astype(f32).T[: first_ref.shape[0], :]

    return pl.pallas_call(
        kernel,
        out_shape=[
            jax.ShapeDtypeStruct((rows, hidden), f32),
            jax.ShapeDtypeStruct((hidden, rows), f32),
            jax.ShapeDtypeStruct((mixes + -mixes % 8, rows), f32),
        ],
        compiler_params=vmem(56),
    )(mlp_sum)


def unpack_attention(attention_sum, heads):
    rows = attention_sum.shape[0]

    def kernel(sum_ref, q_ref, k_ref, v_ref, o_ref):
        for s, ref in enumerate((q_ref, k_ref, v_ref)):
            ref[...] = sum_ref[:, s * heads : (s + 1) * heads].astype(f32)
        o_ref[...] = sum_ref[:, 3 * heads :].astype(f32).T

    shapes = [(rows, heads)] * 3 + [(heads, rows)]
    return pl.pallas_call(
        kernel,
        out_shape=[jax.ShapeDtypeStruct(shape, f32) for shape in shapes],
        compiler_params=vmem(56),
    )(attention_sum)


def places(seg_row):
    length = seg_row.shape[0]
    labels = jnp.arange(DOCS, dtype=jnp.int32)
    before = jnp.sum((seg_row[None, :] < labels[:, None]).astype(jnp.int32), axis=1)
    member = (seg_row[:, None] == labels[None, :]).astype(jnp.int32)
    begins = jnp.sum(member * before[None, :], axis=1)
    return jnp.arange(length, dtype=jnp.int32) - begins


def local(
    history,
    mix_weights,
    segments,
    w_query,
    w_key,
    w_value,
    w_output,
    w_up,
    w_down,
    norm_gains,
    w_first,
    w_second,
    out_cotangent,
    mix_cotangent,
):
    stored, row_tok, width = history.shape
    count = lax.axis_size("layer")
    me = lax.axis_index("layer")
    own_tok = row_tok // count
    order = [(me - k) % count for k in range(count)]

    def block_of(rows, k):
        return rows[k * own_tok : (k + 1) * own_tok]

    def blocks_of(rows):
        return [block_of(rows, k) for k in range(count)]

    def collect(rows):
        return lax.all_gather(rows, "layer", axis=0, tiled=True)

    def spread(rows):
        return lax.psum_scatter(rows, "layer", scatter_dimension=0, tiled=True)

    hidden = w_up.shape[1]
    heads = w_query.shape[1]
    mix_cols = mix_weights.reshape(4 * stored, row_tok).T
    near_shares, rest_share = stream_sums(mix_cols, history)
    low = round_weights(
        [w_query, w_key, w_value, w_output, w_up, w_down],
        [False, False, False, True, False, True],
        [near_shares],
    )
    full = lax.all_gather(low, "dp", axis=0, tiled=True)
    stream_own = spread(near_shares)
    normed_rows = collect(after(streams_norm(stream_own, norm_gains[:3]), full))

    seg_row = segments[0]
    place_row = places(seg_row)
    col_ids = jnp.stack([seg_row, jnp.arange(row_tok, dtype=jnp.int32)])
    half = HEAD_DIM // 2
    frequency = jnp.exp(jnp.arange(half, dtype=f32) * (-2.0 * math.log(10000.0) / HEAD_DIM))
    angles = place_row.astype(f32)[:, None] * frequency[None, :]
    cosine, sine = jnp.cos(angles), jnp.sin(angles)
    cosine = jnp.concatenate([cosine, cosine], axis=1)
    sine = jnp.concatenate([-sine, sine], axis=1)
    row_ids = col_ids.T

    context, queries, keys, values, lse, hidden_part = attend(
        row_ids, col_ids, cosine, sine, normed_rows, rest_share, full, heads
    )
    hidden_in = spread(hidden_part)
    mlp_norm = row_norm(hidden_in, norm_gains[3])
    mlp_rows = collect(mlp_norm)
    active, slope, mlp_part = feed_forward(mlp_rows, full, 4 * heads)
    block = hidden_in.astype(f32) + spread(mlp_part).astype(f32)

    next_mix, mixer_pull = jax.vjp(mixer, block, norm_gains[4], w_first, w_second)
    block_part, mixer_gain_grad, first_grad, second_grad = mixer_pull(mix_cotangent)
    block_grad = out_cotangent + block_part
    branch_rows = collect(block_grad.astype(bf16))
    up_low, mlp_part = feed_back(branch_rows, full, 4 * heads, slope)
    mlp_back = spread(mlp_part)
    mixes = first_grad.shape[1]
    first_wide = jnp.pad(first_grad, ((0, 0), (0, -mixes % 128)))
    mlp_grad = mlp_grads(mlp_rows, after(up_low, mlp_part), branch_rows, active, first_wide)
    hidden_low, mlp_gain_grad = norm_back(
        hidden_in, [mlp_back], norm_gains[3], block_grad, [mlp_grad]
    )
    hidden_rows = collect(hidden_low)
    lin_grads = attend_back(
        row_ids, col_ids, cosine, sine, hidden_rows, full, queries, keys, values, lse
    )
    table = jnp.stack(order).astype(jnp.int32)
    stream_parts = stream_shares(table, lin_grads, full)
    mlp_sum = lax.psum_scatter(mlp_grad, "dp", scatter_dimension=0, tiled=True)
    gain_grads, stream_low = [], []
    for s in range(3):
        blocks = blocks_of(stream_parts[s])
        came = []
        for k in range(1, count):
            came = sum_hop(blocks, k, came, count)
        low, gain_grad = norm_back((stream_own, s), blocks[:1] + came, norm_gains[s])
        gain_grads.append(gain_grad)
        stream_low.append(low)
    near = collect(jnp.concatenate(stream_low, axis=1))

    gain_rows = jnp.stack(gain_grads + [mlp_gain_grad, mixer_gain_grad])
    lines = -(-mixes * mixes // width)
    second_flat = jnp.pad(second_grad.reshape(-1), (0, lines * width - mixes * mixes))
    small = jnp.concatenate([gain_rows, second_flat.reshape(lines, width)])
    small = doubling_sum(doubling_sum(small, "layer"), "dp")
    gains_sum = small[:5]
    second_sum = small[5:].reshape(-1)[: mixes * mixes].reshape(mixes, mixes)
    attention_grad = attention_grads(
        normed_rows, lin_grads, hidden_rows, context, stream_low + [mlp_sum]
    )
    attention_sum = lax.psum_scatter(attention_grad, "dp", scatter_dimension=0, tiled=True)
    up_sum, down_sum, first_part = unpack_mlp(mlp_sum, hidden, mixes)
    first_sum = lax.all_gather(doubling_sum(first_part, "layer"), "dp", axis=1, tiled=True)[:mixes].T
    history_grad, mix_back = history_grads(
        mix_cols,
        history,
        [(near, 0), (near, 1), (near, 2), (hidden_rows, 0)],
        [down_sum, first_sum, small, attention_grad],
    )
    *projections, output_sum = unpack_attention(attention_sum, heads)
    mix_grad = mix_back.T.reshape(4, stored, row_tok)
    return (
        block.astype(bf16),
        next_mix,
        history_grad,
        mix_grad,
        *projections,
        output_sum,
        up_sum,
        down_sum,
        gains_sum,
        first_sum,
        second_sum,
    )


def solution(mesh):
    placed = (
        P("layer", "dp", None),
        P(None, "layer", "dp"),
        P("dp", None),
        P("dp", "layer"),
        P("dp", "layer"),
        P("dp", "layer"),
        P("layer", "dp"),
        P("dp", "layer"),
        P("layer", "dp"),
        P(),
        P(),
        P(),
        P(("dp", "layer"), None),
        P(("dp", "layer"), None),
    )
    return jax.shard_map(
        local,
        mesh=mesh,
        in_specs=placed,
        out_specs=(
            P(("dp", "layer"), None),
            P(("dp", "layer"), None),
            P("layer", "dp", None),
            P(None, "layer", "dp"),
            P("dp", "layer"),
            P("dp", "layer"),
            P("dp", "layer"),
            P("layer", "dp"),
            P("dp", "layer"),
            P("layer", "dp"),
            P(),
            P(),
            P(),
        ),
        check_vma=False,
    )
```

```python
import math

import jax
import jax.numpy as jnp
from jax import lax
from jax.experimental import pallas as pl
from jax.experimental.pallas import tpu as pltpu
from jax.sharding import PartitionSpec as P

HEAD_DIM = 128
DOCS = 2


highest = lax.Precision.HIGHEST
epsilon = 1e-05
bf16 = jnp.bfloat16
f32 = jnp.float32
CHUNK = 16


def rms_norm(values, gain_vec):
    square = jnp.mean(values * values, axis=-1, keepdims=True)
    return values * lax.rsqrt(square + epsilon) * gain_vec


def gelu_exact(values):
    return jax.nn.gelu(values, approximate=False)


def mixer(out_rows, gain_vec, first_matrix, second_matrix):
    hidden = gelu_exact(jnp.dot(rms_norm(out_rows, gain_vec), first_matrix, precision=highest))
    return jnp.dot(hidden, second_matrix, precision=highest)


def plain_dot(left, right):
    return jnp.dot(left, right, preferred_element_type=f32)


def dot_left_t(left, right):
    return lax.dot_general(left, right, (((0,), (0,)), ((), ())), preferred_element_type=f32)


def dot_right_t(left, right):
    return lax.dot_general(left, right, (((1,), (1,)), ((), ())), preferred_element_type=f32)


def doubling_sum(value, axis):
    size = lax.axis_size(axis)
    step = 1
    while step < size:
        value = value + lax.ppermute(value, axis, [(i, i ^ step) for i in range(size)])
        step *= 2
    return value


def total_of(pieces):
    total = pieces[0]
    for piece in pieces[1:]:
        total = total + piece
    return total


def join(values, others):
    anywhere = pl.BlockSpec(memory_space=pl.ANY)
    return list(
        pl.pallas_call(
            lambda *refs: None,
            in_specs=[anywhere] * (len(values) + len(others)),
            out_specs=[anywhere] * len(values),
            out_shape=[jax.ShapeDtypeStruct(v.shape, v.dtype) for v in values],
            input_output_aliases={i: i for i in range(len(values))},
        )(*values, *others)
    )


def after(value, *others):
    return join([value], others)[0]


def sum_hop(blocks, k, came, count):
    up, down = blocks[k], blocks[count - k]
    if came:
        up, down = up + came[0], down + came[1]
    return [
        lax.ppermute(up, "layer", [(i, i + 1) for i in range(k)]),
        lax.ppermute(down, "layer", [(i, i - 1) for i in range(count - k, count)]),
    ]


def vmem(megabytes):
    return pltpu.CompilerParams(vmem_limit_bytes=megabytes << 20)


def row_loop(rows, body, carry):
    return lax.fori_loop(
        0, rows // CHUNK, lambda i, c: body(pl.ds(pl.multiple_of(i * CHUNK, CHUNK), CHUNK), c), carry
    )


def stream_kernel(mix_ref, hist_ref, *refs, stored, streams):
    out_ref = refs[-1]
    width = hist_ref.shape[2]
    lanes = 512

    def body(at, carry):
        mix = mix_ref[at, :]
        for c in range(0, width, lanes):
            rows = [hist_ref[j, at, c : c + lanes].astype(f32) for j in range(stored)]
            for n, s in enumerate(streams):
                total = total_of(
                    [rows[j] * mix[:, s * stored + j : s * stored + j + 1] for j in range(stored)]
                )
                out_ref[at, n * width + c : n * width + c + lanes] = total.astype(bf16)
        return carry

    row_loop(out_ref.shape[0], body, 0)


def stream_sums(mix_cols, history, streams, order):
    stored, tokens, width = history.shape
    rows = 128
    here = lambda i: (i, 0)
    return pl.pallas_call(
        lambda *refs: stream_kernel(*refs, stored=stored, streams=streams),
        grid=(tokens // rows,),
        in_specs=[
            pl.BlockSpec((rows, 4 * stored), here),
            pl.BlockSpec((stored, rows, width), lambda i: (0, i, 0)),
        ]
        + [pl.BlockSpec(memory_space=pl.ANY)] * len(order),
        out_specs=pl.BlockSpec((rows, len(streams) * width), here),
        out_shape=jax.ShapeDtypeStruct((tokens, len(streams) * width), bf16),
        compiler_params=vmem(48),
    )(mix_cols, history, *order)


def streams_norm(values, gains):
    block, width = values.shape[0], gains.shape[1]

    def kernel(gain_ref, value_ref, norm_ref):
        gain = gain_ref[pl.ds(pl.program_id(0), 1), :]

        def body(at, carry):
            rows = value_ref[at, :].astype(f32)
            centre = rows - jnp.mean(rows, axis=1, keepdims=True)
            spread = jnp.mean(centre * centre, axis=1, keepdims=True)
            norm_ref[at, :] = (centre * lax.rsqrt(spread + epsilon) * gain).astype(bf16)
            return carry

        row_loop(block, body, 0)

    stream = pl.BlockSpec((block, width), lambda s: (0, s))
    return pl.pallas_call(
        kernel,
        grid=(3,),
        in_specs=[pl.BlockSpec(gains.shape, lambda s: (0, 0)), stream],
        out_specs=stream,
        out_shape=jax.ShapeDtypeStruct(values.shape, bf16),
        compiler_params=vmem(48),
    )(gains, values)


def row_norm(values, gain_vec):
    def kernel(gain_ref, value_ref, norm_ref):
        def body(at, carry):
            rows = value_ref[at, :].astype(f32)
            centre = rows - jnp.mean(rows, axis=1, keepdims=True)
            spread = jnp.mean(centre * centre, axis=1, keepdims=True)
            norm_ref[at, :] = (centre * lax.rsqrt(spread + epsilon) * gain_ref[...]).astype(bf16)
            return carry

        row_loop(value_ref.shape[0], body, 0)

    return pl.pallas_call(
        kernel,
        out_shape=jax.ShapeDtypeStruct(values.shape, bf16),
        compiler_params=vmem(48),
    )(gain_vec[None], values)


def norm_grad(values, grad, gain):
    centre = values - jnp.mean(values, axis=1, keepdims=True)
    inv = lax.rsqrt(jnp.mean(centre * centre, axis=1, keepdims=True) + epsilon)
    hat = centre * inv
    scaled = grad * gain
    back = (
        scaled
        - jnp.mean(scaled, axis=1, keepdims=True)
        - hat * jnp.mean(scaled * hat, axis=1, keepdims=True)
    ) * inv
    return back, jnp.sum(grad * hat, axis=0, keepdims=True)


def back_kernel(gain_ref, value_ref, *refs, parts, based):
    part_refs = refs[:parts]
    base_ref = refs[parts] if based else None
    out_ref, dgain_ref = refs[-2:]

    def body(at, dgain):
        values = value_ref[at, :].astype(f32)
        grad = total_of([p[at, :].astype(f32) for p in part_refs])
        back, dgain_rows = norm_grad(values, grad, gain_ref[...])
        if based:
            back = back + base_ref[at, :]
        out_ref[at, :] = back.astype(bf16)
        return dgain + dgain_rows

    dgain_ref[...] = row_loop(value_ref.shape[0], body, jnp.zeros(dgain_ref.shape, f32))


def norm_back(values, parts, gain_vec, base=None, order=()):
    width = gain_vec.shape[0]
    operands = [gain_vec[None], values] + list(parts) + ([] if base is None else [base])
    arrays, specs = [], []
    for operand in operands:
        array, column = operand if isinstance(operand, tuple) else (operand, 0)
        rows = 1 if array.shape[0] == 1 else values_rows(values)
        arrays.append(array)
        specs.append(pl.BlockSpec((rows, width), lambda i, column=column: (0, column)))
    number = len(arrays)
    rows = values_rows(values)
    whole = lambda i: (0, 0)
    back, dgain = pl.pallas_call(
        lambda *refs: back_kernel(
            *refs[:number], *refs[-2:], parts=len(parts), based=base is not None
        ),
        grid=(1,),
        in_specs=specs + [pl.BlockSpec(memory_space=pl.ANY)] * len(order),
        out_specs=[pl.BlockSpec((rows, width), whole), pl.BlockSpec((1, width), whole)],
        out_shape=[
            jax.ShapeDtypeStruct((rows, width), bf16),
            jax.ShapeDtypeStruct((1, width), f32),
        ],
        compiler_params=vmem(48),
    )(*arrays, *order)
    return back, dgain[0]


def values_rows(values):
    return (values[0] if isinstance(values, tuple) else values).shape[0]


def history_kernel(mix_ref, hist_ref, *refs, stored):
    grad_refs, (hist_out, mix_out) = refs[:4], refs[-2:]
    rows, width = hist_out.shape[1:]
    lanes = 512
    group = 64

    token = lax.broadcasted_iota(jnp.int32, (group, stored * group), 0)
    other = lax.broadcasted_iota(jnp.int32, (group, stored * group), 1)
    for g in range(0, rows, group):
        grads = jnp.concatenate([r[g : g + group, :] for r in grad_refs], axis=0)
        stored_rows = jnp.concatenate([hist_ref[j, g : g + group, :] for j in range(stored)], axis=0)
        pairs = contract_cols(grads, stored_rows)
        columns = []
        for s in range(4):
            part = pairs[s * group : (s + 1) * group, :]
            for j in range(stored):
                kept = jnp.where(other == token + j * group, part, 0.0)
                columns.append(jnp.sum(kept, axis=1, keepdims=True))
        mix_out[g : g + group, :] = jnp.concatenate(columns, axis=1)

    def body(at, carry):
        mix = mix_ref[at, :]
        for c in range(0, width, lanes):
            cols = slice(c, c + lanes)
            wide = [r[at, cols].astype(f32) for r in grad_refs]
            for j in range(stored):
                total = total_of(
                    [wide[s] * mix[:, s * stored + j : s * stored + j + 1] for s in range(4)]
                )
                hist_out[j, at, cols] = total.astype(bf16)
        return carry

    row_loop(rows, body, 0)


def history_grads(mix_cols, history, grads, order):
    stored, tokens, width = history.shape
    rows = 128
    here = lambda i: (i, 0)
    there = lambda i: (0, i, 0)
    return pl.pallas_call(
        lambda *refs: history_kernel(*refs, stored=stored),
        grid=(tokens // rows,),
        in_specs=[
            pl.BlockSpec((rows, 4 * stored), here),
            pl.BlockSpec((stored, rows, width), there),
        ]
        + [pl.BlockSpec((rows, width), lambda i, column=column: (i, column)) for _, column in grads]
        + [pl.BlockSpec(memory_space=pl.ANY)] * len(order),
        out_specs=[
            pl.BlockSpec((stored, rows, width), there),
            pl.BlockSpec((rows, 4 * stored), here),
        ],
        out_shape=[
            jax.ShapeDtypeStruct((stored, tokens, width), bf16),
            jax.ShapeDtypeStruct((tokens, 4 * stored), f32),
        ],
        compiler_params=vmem(48),
    )(mix_cols, history, *[g for g, _ in grads], *order)


def contract_rows(left, right):
    return lax.dot_general(left, right, (((0,), (0,)), ((), ())), preferred_element_type=f32)


def contract_cols(left, right):
    return lax.dot_general(left, right, (((1,), (1,)), ((), ())), preferred_element_type=f32)


def mlp_grads(mlp_rows, up_low, branch_rows, active, first):
    tokens, width = mlp_rows.shape
    hidden = active.shape[1]
    rows = 256
    total = 2 * hidden + first.shape[1]

    def kernel(mlp_ref, up_ref, branch_ref, active_ref, first_ref, out_ref):
        out_ref[:, :hidden] = contract_rows(mlp_ref[...], up_ref[...]).astype(bf16)
        out_ref[:, hidden : 2 * hidden] = contract_rows(branch_ref[...], active_ref[...]).astype(bf16)
        out_ref[:, 2 * hidden :] = first_ref[...].astype(bf16)

    side = pl.BlockSpec((tokens, rows), lambda i: (0, i))
    return pl.pallas_call(
        kernel,
        grid=(width // rows,),
        in_specs=[side, resident(up_low), side, resident(active)]
        + [pl.BlockSpec((rows, first.shape[1]), lambda i: (i, 0))],
        out_specs=pl.BlockSpec((rows, total), lambda i: (i, 0)),
        out_shape=jax.ShapeDtypeStruct((width, total), bf16),
        compiler_params=vmem(56),
    )(mlp_rows, up_low, branch_rows, active, first)


def attention_grads(near, lin_grads, hidden_rows, context, order):
    tokens, width = hidden_rows.shape
    heads = context.shape[1]
    rows = 256

    def kernel(q_ref, k_ref, v_ref, dq_ref, dk_ref, dv_ref, hidden_ref, ctx_ref, *refs):
        out_ref = refs[-1]
        pairs = ((q_ref, dq_ref), (k_ref, dk_ref), (v_ref, dv_ref), (hidden_ref, ctx_ref))
        for s, (left, right) in enumerate(pairs):
            out_ref[:, s * heads : (s + 1) * heads] = contract_rows(left[...], right[...]).astype(bf16)

    side = pl.BlockSpec((tokens, rows), lambda i: (0, i))
    return pl.pallas_call(
        kernel,
        grid=(width // rows,),
        in_specs=[
            pl.BlockSpec((tokens, rows), lambda i, s=s: (0, s * (width // rows) + i))
            for s in range(3)
        ]
        + [resident(lin_grads[0])] * 3
        + [side, resident(context)]
        + [pl.BlockSpec(memory_space=pl.ANY)] * len(order),
        out_specs=pl.BlockSpec((rows, 4 * heads), lambda i: (i, 0)),
        out_shape=jax.ShapeDtypeStruct((width, 4 * heads), bf16),
        compiler_params=vmem(56),
    )(near, near, near, *lin_grads, hidden_rows, context, *order)


def round_weights(weights, turned, order):
    heights = [w.shape[1] if t else w.shape[0] for w, t in zip(weights, turned)]
    widths = [w.shape[0] if t else w.shape[1] for w, t in zip(weights, turned)]
    number = len(weights)

    def kernel(*refs):
        at = 0
        for ref, t, size in zip(refs[:number], turned, widths):
            value = ref[...].T if t else ref[...]
            refs[-1][:, at : at + size] = value.astype(bf16)
            at += size

    return pl.pallas_call(
        kernel,
        in_specs=[pl.BlockSpec(memory_space=pltpu.VMEM)] * number
        + [pl.BlockSpec(memory_space=pl.ANY)] * len(order),
        out_shape=jax.ShapeDtypeStruct((heights[0], sum(widths)), bf16),
        compiler_params=vmem(56),
    )(*weights, *order)


def feed_forward(rows, full, up_first):
    tokens, width = rows.shape
    hidden = (full.shape[1] - up_first) // 2
    cols = 512
    first = up_first // cols
    steps = hidden // cols

    def kernel(rows_ref, up_ref, down_ref, active_ref, slope_ref, out_ref, total_ref):
        step = pl.program_id(0)
        up = jnp.dot(rows_ref[...], up_ref[...], preferred_element_type=f32)
        below = 0.5 * (1.0 + lax.erf(up * (0.5**0.5)))
        active = (up * below).astype(bf16)
        active_ref[...] = active
        slope_ref[...] = below + up * jnp.exp(-0.5 * up * up) * ((2.0 * math.pi) ** -0.5)
        share = contract_cols(active, down_ref[...])

        @pl.when(step == 0)
        def _():
            total_ref[...] = share

        @pl.when(step > 0)
        def _():
            total_ref[...] += share

        @pl.when(step == steps - 1)
        def _():
            out_ref[...] = total_ref[...].astype(bf16)

    part = pl.BlockSpec((tokens, cols), lambda i: (0, i))
    return pl.pallas_call(
        kernel,
        grid=(steps,),
        in_specs=[
            resident(rows),
            pl.BlockSpec((width, cols), lambda i: (0, first + i)),
            pl.BlockSpec((width, cols), lambda i: (0, first + steps + i)),
        ],
        out_specs=[part, part, pl.BlockSpec((tokens, width), lambda i: (0, 0))],
        out_shape=[
            jax.ShapeDtypeStruct((tokens, hidden), bf16),
            jax.ShapeDtypeStruct((tokens, hidden), f32),
            jax.ShapeDtypeStruct((tokens, width), bf16),
        ],
        scratch_shapes=[pltpu.VMEM((tokens, width), f32)],
        compiler_params=vmem(60),
    )(rows, full, full)


def feed_back(rows, full, up_first, slope):
    tokens, width = rows.shape
    hidden = slope.shape[1]
    cols = 512
    first = up_first // cols
    steps = hidden // cols

    def kernel(rows_ref, up_ref, down_ref, slope_ref, *refs):
        low_ref, out_ref, total_ref = refs[-3:]
        step = pl.program_id(0)
        grad = jnp.dot(rows_ref[...], down_ref[...], preferred_element_type=f32)
        low = (grad * slope_ref[...]).astype(bf16)
        low_ref[...] = low
        share = contract_cols(low, up_ref[...])

        @pl.when(step == 0)
        def _():
            total_ref[...] = share

        @pl.when(step > 0)
        def _():
            total_ref[...] += share

        @pl.when(step == steps - 1)
        def _():
            out_ref[...] = total_ref[...].astype(bf16)

    part = pl.BlockSpec((tokens, cols), lambda i: (0, i))
    return pl.pallas_call(
        kernel,
        grid=(steps,),
        in_specs=[
            resident(rows),
            pl.BlockSpec((width, cols), lambda i: (0, first + i)),
            pl.BlockSpec((width, cols), lambda i: (0, first + steps + i)),
            part,
        ],
        out_specs=[part, pl.BlockSpec((tokens, width), lambda i: (0, 0))],
        out_shape=[
            jax.ShapeDtypeStruct((tokens, hidden), bf16),
            jax.ShapeDtypeStruct((tokens, width), bf16),
        ],
        scratch_shapes=[pltpu.VMEM((tokens, width), f32)],
        compiler_params=vmem(60),
    )(rows, full, full, slope)


def turn(values, cosine, sine):
    return values * cosine + pltpu.roll(values, HEAD_DIM // 2, 1) * sine


def score_block(queries, keys, allowed):
    scores = lax.dot_general(
        queries, keys, (((1,), (1,)), ((), ())), preferred_element_type=f32
    ) * (HEAD_DIM ** (-0.5))
    return jnp.where(allowed, scores, -1e30)


def allowed_block(row_ids, col_ids):
    return (row_ids[:, 0:1] == col_ids[0:1, :]) & (row_ids[:, 1:2] >= col_ids[1:2, :])


GROUP = 2


def attend_kernel(
    rows_ref, cols_ref, cos_ref, sin_ref, near_ref, rest_ref, wq_ref, wk_ref, wv_ref, wo_ref,
    ctx_ref, qr_ref, kr_ref, v_ref, lse_ref, out_ref, total_ref,
):
    step = pl.program_id(0)
    width = out_ref.shape[1]
    allowed = allowed_block(rows_ref[...], cols_ref[...])

    def lin(s, weight_ref):
        rows = near_ref[:, s * width : (s + 1) * width]
        return jnp.dot(rows, weight_ref[...], preferred_element_type=f32)

    q_lin, k_lin = lin(0, wq_ref), lin(1, wk_ref)
    v_ref[...] = lin(2, wv_ref).astype(bf16)
    for g in range(GROUP):
        cols = slice(g * HEAD_DIM, (g + 1) * HEAD_DIM)
        queries = turn(q_lin[:, cols], cos_ref[...], sin_ref[...]).astype(bf16)
        keys = turn(k_lin[:, cols], cos_ref[...], sin_ref[...]).astype(bf16)
        qr_ref[:, cols] = queries
        kr_ref[:, cols] = keys
        scores = score_block(queries, keys, allowed)
        row_max = jnp.max(scores, axis=1, keepdims=True)
        shifted = jnp.exp(scores - row_max)
        row_sum = jnp.sum(shifted, axis=1, keepdims=True)
        probs = (shifted / row_sum).astype(bf16)
        context = jnp.dot(probs, v_ref[:, cols], preferred_element_type=f32)
        ctx_ref[:, cols] = context.astype(bf16)
        lse_ref[g] = row_max + jnp.log(row_sum)
    share = contract_cols(ctx_ref[...], wo_ref[...])

    @pl.when(step == 0)
    def _():
        total_ref[...] = share + rest_ref[...].astype(f32)

    @pl.when(step > 0)
    def _():
        total_ref[...] += share

    @pl.when(step == pl.num_programs(0) - 1)
    def _():
        out_ref[...] = total_ref[...].astype(bf16)


def resident(array):
    return pl.BlockSpec(
        array.shape, lambda i: (0,) * array.ndim, pipeline_mode=pl.Buffered(buffer_count=1)
    )


def head_columns(full, first):
    lanes = GROUP * HEAD_DIM
    return pl.BlockSpec((full.shape[0], lanes), lambda h: (0, first // lanes + h))


def attend(row_ids, col_ids, cosine, sine, near, rest, full, heads):
    tokens, width = rest.shape
    head = pl.BlockSpec((tokens, GROUP * HEAD_DIM), lambda h: (0, h))
    fixed = [row_ids, col_ids, cosine, sine, near, rest]

    return pl.pallas_call(
        attend_kernel,
        grid=(heads // HEAD_DIM // GROUP,),
        in_specs=[resident(a) for a in fixed]
        + [head_columns(full, s * heads) for s in range(4)],
        out_specs=[head] * 4
        + [
            pl.BlockSpec((GROUP, tokens, 1), lambda h: (h, 0, 0)),
            pl.BlockSpec((tokens, width), lambda h: (0, 0)),
        ],
        out_shape=[jax.ShapeDtypeStruct((tokens, heads), bf16)] * 4
        + [
            jax.ShapeDtypeStruct((heads // HEAD_DIM, tokens, 1), f32),
            jax.ShapeDtypeStruct((tokens, width), bf16),
        ],
        scratch_shapes=[pltpu.VMEM((tokens, width), f32)],
        compiler_params=vmem(60),
    )(*fixed, *[full] * 4)


def attend_back_kernel(
    rows_ref, cols_ref, cos_ref, sin_ref, hidden_ref, wo_ref, q_ref, k_ref, v_ref, lse_ref,
    dq_ref, dk_ref, dv_ref,
):
    allowed = allowed_block(rows_ref[...], cols_ref[...])
    scale = HEAD_DIM ** (-0.5)
    grads = jnp.dot(hidden_ref[...], wo_ref[...], preferred_element_type=f32).astype(bf16)
    for g in range(GROUP):
        cols = slice(g * HEAD_DIM, (g + 1) * HEAD_DIM)
        queries, keys, values, grad = q_ref[:, cols], k_ref[:, cols], v_ref[:, cols], grads[:, cols]
        probs = jnp.exp(score_block(queries, keys, allowed) - lse_ref[g])
        prob_grad = contract_cols(grad, values)
        dv_ref[:, cols] = contract_rows(probs.astype(bf16), grad).astype(bf16)
        centre = jnp.sum(probs * prob_grad, axis=1, keepdims=True)
        score_grad = (probs * (prob_grad - centre)).astype(bf16)
        dq = jnp.dot(score_grad, keys, preferred_element_type=f32) * scale
        dk = contract_rows(score_grad, queries) * scale
        dq_ref[:, cols] = turn(dq, cos_ref[...], -sin_ref[...]).astype(bf16)
        dk_ref[:, cols] = turn(dk, cos_ref[...], -sin_ref[...]).astype(bf16)


def attend_back(row_ids, col_ids, cosine, sine, hidden_rows, full, queries, keys, values, lse):
    tokens, heads = queries.shape
    head = pl.BlockSpec((tokens, GROUP * HEAD_DIM), lambda h: (0, h))
    fixed = [row_ids, col_ids, cosine, sine, hidden_rows]

    return pl.pallas_call(
        attend_back_kernel,
        grid=(heads // HEAD_DIM // GROUP,),
        in_specs=[resident(a) for a in fixed]
        + [head_columns(full, 3 * heads), head, head, head]
        + [pl.BlockSpec((GROUP, tokens, 1), lambda h: (h, 0, 0))],
        out_specs=[head, head, head],
        out_shape=[jax.ShapeDtypeStruct((tokens, heads), bf16)] * 3,
        compiler_params=vmem(60),
    )(*fixed, full, queries, keys, values, lse)


def stream_shares(where, lin_grads, full):
    tokens, heads = lin_grads[0].shape
    width = full.shape[0]
    count = where.shape[0]
    block = tokens // count

    def kernel(where_ref, dq_ref, dk_ref, dv_ref, full_ref, *out_refs):
        for s, ref in enumerate((dq_ref, dk_ref, dv_ref)):

            @pl.when(pl.program_id(0) == s)
            def _(ref=ref, out_ref=out_refs[s]):
                share = contract_cols(ref[...], full_ref[...]).astype(bf16)
                for j in range(count):
                    at = pl.ds(pl.multiple_of(where_ref[j] * block, block), block)
                    out_ref[at, :] = share[j * block : (j + 1) * block, :]

    fixed = pl.BlockSpec(
        (tokens, heads), lambda s, w: (0, 0), pipeline_mode=pl.Buffered(buffer_count=1)
    )
    return pl.pallas_call(
        kernel,
        grid_spec=pltpu.PrefetchScalarGridSpec(
            num_scalar_prefetch=1,
            grid=(3,),
            in_specs=[fixed] * 3 + [pl.BlockSpec((width, heads), lambda s, w: (0, s))],
            out_specs=[pl.BlockSpec((tokens, width), lambda s, w: (0, 0))] * 3,
        ),
        out_shape=[jax.ShapeDtypeStruct((tokens, width), bf16)] * 3,
        compiler_params=vmem(56),
    )(where, *lin_grads, full)


def unpack_mlp(mlp_sum, hidden, mixes):
    rows = mlp_sum.shape[0]

    def kernel(sum_ref, up_ref, down_ref, first_ref):
        up_ref[...] = sum_ref[:, :hidden].astype(f32)
        down_ref[...] = sum_ref[:, hidden : 2 * hidden].astype(f32).T
        first_ref[...] = sum_ref[:, 2 * hidden :].astype(f32).T[: first_ref.shape[0], :]

    return pl.pallas_call(
        kernel,
        out_shape=[
            jax.ShapeDtypeStruct((rows, hidden), f32),
            jax.ShapeDtypeStruct((hidden, rows), f32),
            jax.ShapeDtypeStruct((mixes + -mixes % 8, rows), f32),
        ],
        compiler_params=vmem(56),
    )(mlp_sum)


def unpack_attention(attention_sum, heads):
    rows = attention_sum.shape[0]

    def kernel(sum_ref, q_ref, k_ref, v_ref, o_ref):
        for s, ref in enumerate((q_ref, k_ref, v_ref)):
            ref[...] = sum_ref[:, s * heads : (s + 1) * heads].astype(f32)
        o_ref[...] = sum_ref[:, 3 * heads :].astype(f32).T

    shapes = [(rows, heads)] * 3 + [(heads, rows)]
    return pl.pallas_call(
        kernel,
        out_shape=[jax.ShapeDtypeStruct(shape, f32) for shape in shapes],
        compiler_params=vmem(56),
    )(attention_sum)


def places(seg_row):
    length = seg_row.shape[0]
    labels = jnp.arange(DOCS, dtype=jnp.int32)
    before = jnp.sum((seg_row[None, :] < labels[:, None]).astype(jnp.int32), axis=1)
    member = (seg_row[:, None] == labels[None, :]).astype(jnp.int32)
    begins = jnp.sum(member * before[None, :], axis=1)
    return jnp.arange(length, dtype=jnp.int32) - begins


def local(
    history,
    mix_weights,
    segments,
    w_query,
    w_key,
    w_value,
    w_output,
    w_up,
    w_down,
    norm_gains,
    w_first,
    w_second,
    out_cotangent,
    mix_cotangent,
):
    stored, row_tok, width = history.shape
    count = lax.axis_size("layer")
    me = lax.axis_index("layer")
    own_tok = row_tok // count
    order = [(me - k) % count for k in range(count)]

    def block_of(rows, k):
        return rows[k * own_tok : (k + 1) * own_tok]

    def blocks_of(rows):
        return [block_of(rows, k) for k in range(count)]

    def collect(rows):
        return lax.all_gather(rows, "layer", axis=0, tiled=True)

    def spread(rows):
        return lax.psum_scatter(rows, "layer", scatter_dimension=0, tiled=True)

    hidden = w_up.shape[1]
    heads = w_query.shape[1]
    mix_cols = mix_weights.reshape(4 * stored, row_tok).T
    near_shares = stream_sums(mix_cols, history, (0, 1, 2), [])
    low = round_weights(
        [w_query, w_key, w_value, w_output, w_up, w_down],
        [False, False, False, True, False, True],
        [near_shares],
    )
    full = lax.all_gather(low, "dp", axis=0, tiled=True)
    stream_own = spread(near_shares)
    rest_share = stream_sums(mix_cols, history, (3,), [near_shares, low])
    normed_rows = collect(after(streams_norm(stream_own, norm_gains[:3]), full))

    seg_row = segments[0]
    place_row = places(seg_row)
    col_ids = jnp.stack([seg_row, jnp.arange(row_tok, dtype=jnp.int32)])
    half = HEAD_DIM // 2
    frequency = jnp.exp(jnp.arange(half, dtype=f32) * (-2.0 * math.log(10000.0) / HEAD_DIM))
    angles = place_row.astype(f32)[:, None] * frequency[None, :]
    cosine, sine = jnp.cos(angles), jnp.sin(angles)
    cosine = jnp.concatenate([cosine, cosine], axis=1)
    sine = jnp.concatenate([-sine, sine], axis=1)
    row_ids = col_ids.T

    context, queries, keys, values, lse, hidden_part = attend(
        row_ids, col_ids, cosine, sine, normed_rows, rest_share, full, heads
    )
    hidden_in = spread(hidden_part)
    mlp_norm = row_norm(hidden_in, norm_gains[3])
    mlp_rows = collect(mlp_norm)
    active, slope, mlp_part = feed_forward(mlp_rows, full, 4 * heads)
    block = hidden_in.astype(f32) + spread(mlp_part).astype(f32)

    next_mix, mixer_pull = jax.vjp(mixer, block, norm_gains[4], w_first, w_second)
    block_part, mixer_gain_grad, first_grad, second_grad = mixer_pull(mix_cotangent)
    block_grad = out_cotangent + block_part
    branch_rows = collect(block_grad.astype(bf16))
    up_low, mlp_part = feed_back(branch_rows, full, 4 * heads, slope)
    mlp_back = spread(mlp_part)
    mixes = first_grad.shape[1]
    first_wide = jnp.pad(first_grad, ((0, 0), (0, -mixes % 128)))
    mlp_grad = mlp_grads(mlp_rows, after(up_low, mlp_part), branch_rows, active, first_wide)
    hidden_low, mlp_gain_grad = norm_back(
        hidden_in, [mlp_back], norm_gains[3], block_grad, [mlp_grad]
    )
    hidden_rows = collect(hidden_low)
    lin_grads = attend_back(
        row_ids, col_ids, cosine, sine, hidden_rows, full, queries, keys, values, lse
    )
    table = jnp.stack(order).astype(jnp.int32)
    stream_parts = stream_shares(table, lin_grads, full)
    mlp_sum = lax.psum_scatter(mlp_grad, "dp", scatter_dimension=0, tiled=True)
    gain_grads, stream_low = [], []
    for s in range(3):
        blocks = blocks_of(stream_parts[s])
        came = []
        for k in range(1, count):
            came = sum_hop(blocks, k, came, count)
        low, gain_grad = norm_back((stream_own, s), blocks[:1] + came, norm_gains[s])
        gain_grads.append(gain_grad)
        stream_low.append(low)
    near = collect(jnp.concatenate(stream_low, axis=1))

    gain_rows = jnp.stack(gain_grads + [mlp_gain_grad, mixer_gain_grad])
    lines = -(-mixes * mixes // width)
    second_flat = jnp.pad(second_grad.reshape(-1), (0, lines * width - mixes * mixes))
    small = jnp.concatenate([gain_rows, second_flat.reshape(lines, width)])
    small = doubling_sum(doubling_sum(small, "layer"), "dp")
    gains_sum = small[:5]
    second_sum = small[5:].reshape(-1)[: mixes * mixes].reshape(mixes, mixes)
    attention_grad = attention_grads(
        normed_rows, lin_grads, hidden_rows, context, stream_low + [mlp_sum]
    )
    attention_sum = lax.psum_scatter(attention_grad, "dp", scatter_dimension=0, tiled=True)
    up_sum, down_sum, first_part = unpack_mlp(mlp_sum, hidden, mixes)
    first_sum = lax.all_gather(doubling_sum(first_part, "layer"), "dp", axis=1, tiled=True)[:mixes].T
    history_grad, mix_back = history_grads(
        mix_cols,
        history,
        [(near, 0), (near, 1), (near, 2), (hidden_rows, 0)],
        [down_sum[:8], first_sum[:8], small, attention_grad],
    )
    *projections, output_sum = unpack_attention(attention_sum, heads)
    mix_grad = mix_back.T.reshape(4, stored, row_tok)
    return (
        block.astype(bf16),
        next_mix,
        history_grad,
        mix_grad,
        *projections,
        output_sum,
        up_sum,
        down_sum,
        gains_sum,
        first_sum,
        second_sum,
    )


def solution(mesh):
    placed = (
        P("layer", "dp", None),
        P(None, "layer", "dp"),
        P("dp", None),
        P("dp", "layer"),
        P("dp", "layer"),
        P("dp", "layer"),
        P("layer", "dp"),
        P("dp", "layer"),
        P("layer", "dp"),
        P(),
        P(),
        P(),
        P(("dp", "layer"), None),
        P(("dp", "layer"), None),
    )
    return jax.shard_map(
        local,
        mesh=mesh,
        in_specs=placed,
        out_specs=(
            P(("dp", "layer"), None),
            P(("dp", "layer"), None),
            P("layer", "dp", None),
            P(None, "layer", "dp"),
            P("dp", "layer"),
            P("dp", "layer"),
            P("dp", "layer"),
            P("layer", "dp"),
            P("dp", "layer"),
            P("layer", "dp"),
            P(),
            P(),
            P(),
        ),
        check_vma=False,
    )
```

```python
import math

import jax
import jax.numpy as jnp
from jax import lax
from jax.experimental import pallas as pl
from jax.experimental.pallas import tpu as pltpu
from jax.sharding import PartitionSpec as P

HEAD_DIM = 128
DOCS = 2


highest = lax.Precision.HIGHEST
epsilon = 1e-05
bf16 = jnp.bfloat16
f32 = jnp.float32
CHUNK = 16


def rms_norm(values, gain_vec):
    square = jnp.mean(values * values, axis=-1, keepdims=True)
    return values * lax.rsqrt(square + epsilon) * gain_vec


def gelu_exact(values):
    return jax.nn.gelu(values, approximate=False)


def mixer(out_rows, gain_vec, first_matrix, second_matrix):
    hidden = gelu_exact(jnp.dot(rms_norm(out_rows, gain_vec), first_matrix, precision=highest))
    return jnp.dot(hidden, second_matrix, precision=highest)


def plain_dot(left, right):
    return jnp.dot(left, right, preferred_element_type=f32)


def dot_left_t(left, right):
    return lax.dot_general(left, right, (((0,), (0,)), ((), ())), preferred_element_type=f32)


def dot_right_t(left, right):
    return lax.dot_general(left, right, (((1,), (1,)), ((), ())), preferred_element_type=f32)


def doubling_sum(value, axis):
    size = lax.axis_size(axis)
    step = 1
    while step < size:
        value = value + lax.ppermute(value, axis, [(i, i ^ step) for i in range(size)])
        step *= 2
    return value


def total_of(pieces):
    total = pieces[0]
    for piece in pieces[1:]:
        total = total + piece
    return total


def join(values, others):
    anywhere = pl.BlockSpec(memory_space=pl.ANY)
    return list(
        pl.pallas_call(
            lambda *refs: None,
            in_specs=[anywhere] * (len(values) + len(others)),
            out_specs=[anywhere] * len(values),
            out_shape=[jax.ShapeDtypeStruct(v.shape, v.dtype) for v in values],
            input_output_aliases={i: i for i in range(len(values))},
        )(*values, *others)
    )


def after(value, *others):
    return join([value], others)[0]


def sum_hop(blocks, k, came, count):
    up, down = blocks[k], blocks[count - k]
    if came:
        up, down = up + came[0], down + came[1]
    return [
        lax.ppermute(up, "layer", [(i, i + 1) for i in range(k)]),
        lax.ppermute(down, "layer", [(i, i - 1) for i in range(count - k, count)]),
    ]


def vmem(megabytes):
    return pltpu.CompilerParams(vmem_limit_bytes=megabytes << 20)


def row_loop(rows, body, carry):
    def turn_of(i, c):
        for n in range(2):
            c = body(pl.ds(pl.multiple_of((2 * i + n) * CHUNK, CHUNK), CHUNK), c)
        return c

    return lax.fori_loop(0, rows // CHUNK // 2, turn_of, carry)


def stream_kernel(mix_ref, hist_ref, *refs, stored, streams):
    out_ref = refs[-1]
    width = hist_ref.shape[2]
    lanes = 512

    def body(at, carry):
        mix = mix_ref[at, :]
        for c in range(0, width, lanes):
            rows = [hist_ref[j, at, c : c + lanes].astype(f32) for j in range(stored)]
            for n, s in enumerate(streams):
                total = total_of(
                    [rows[j] * mix[:, s * stored + j : s * stored + j + 1] for j in range(stored)]
                )
                out_ref[at, n * width + c : n * width + c + lanes] = total.astype(bf16)
        return carry

    row_loop(out_ref.shape[0], body, 0)


def stream_sums(mix_cols, history, streams, order):
    stored, tokens, width = history.shape
    rows = 128
    here = lambda i: (i, 0)
    return pl.pallas_call(
        lambda *refs: stream_kernel(*refs, stored=stored, streams=streams),
        grid=(tokens // rows,),
        in_specs=[
            pl.BlockSpec((rows, 4 * stored), here),
            pl.BlockSpec((stored, rows, width), lambda i: (0, i, 0)),
        ]
        + [pl.BlockSpec(memory_space=pl.ANY)] * len(order),
        out_specs=pl.BlockSpec((rows, len(streams) * width), here),
        out_shape=jax.ShapeDtypeStruct((tokens, len(streams) * width), bf16),
        compiler_params=vmem(48),
    )(mix_cols, history, *order)


def streams_norm(values, gains):
    block, width = values.shape[0], gains.shape[1]

    def kernel(gain_ref, value_ref, norm_ref):
        gain = gain_ref[pl.ds(pl.program_id(0), 1), :]

        def body(at, carry):
            rows = value_ref[at, :].astype(f32)
            centre = rows - jnp.mean(rows, axis=1, keepdims=True)
            spread = jnp.mean(centre * centre, axis=1, keepdims=True)
            norm_ref[at, :] = (centre * lax.rsqrt(spread + epsilon) * gain).astype(bf16)
            return carry

        row_loop(block, body, 0)

    stream = pl.BlockSpec((block, width), lambda s: (0, s))
    return pl.pallas_call(
        kernel,
        grid=(3,),
        in_specs=[pl.BlockSpec(gains.shape, lambda s: (0, 0)), stream],
        out_specs=stream,
        out_shape=jax.ShapeDtypeStruct(values.shape, bf16),
        compiler_params=vmem(48),
    )(gains, values)


def row_norm(values, gain_vec):
    def kernel(gain_ref, value_ref, norm_ref):
        def body(at, carry):
            rows = value_ref[at, :].astype(f32)
            centre = rows - jnp.mean(rows, axis=1, keepdims=True)
            spread = jnp.mean(centre * centre, axis=1, keepdims=True)
            norm_ref[at, :] = (centre * lax.rsqrt(spread + epsilon) * gain_ref[...]).astype(bf16)
            return carry

        row_loop(value_ref.shape[0], body, 0)

    return pl.pallas_call(
        kernel,
        out_shape=jax.ShapeDtypeStruct(values.shape, bf16),
        compiler_params=vmem(48),
    )(gain_vec[None], values)


def norm_grad(values, grad, gain):
    centre = values - jnp.mean(values, axis=1, keepdims=True)
    inv = lax.rsqrt(jnp.mean(centre * centre, axis=1, keepdims=True) + epsilon)
    hat = centre * inv
    scaled = grad * gain
    back = (
        scaled
        - jnp.mean(scaled, axis=1, keepdims=True)
        - hat * jnp.mean(scaled * hat, axis=1, keepdims=True)
    ) * inv
    return back, jnp.sum(grad * hat, axis=0, keepdims=True)


def back_kernel(gain_ref, value_ref, *refs, parts, based):
    part_refs = refs[:parts]
    base_ref = refs[parts] if based else None
    out_ref, dgain_ref = refs[-2:]

    def body(at, dgain):
        values = value_ref[at, :].astype(f32)
        grad = total_of([p[at, :].astype(f32) for p in part_refs])
        back, dgain_rows = norm_grad(values, grad, gain_ref[...])
        if based:
            back = back + base_ref[at, :]
        out_ref[at, :] = back.astype(bf16)
        return dgain + dgain_rows

    dgain_ref[...] = row_loop(value_ref.shape[0], body, jnp.zeros(dgain_ref.shape, f32))


def norm_back(values, parts, gain_vec, base=None, order=()):
    width = gain_vec.shape[0]
    operands = [gain_vec[None], values] + list(parts) + ([] if base is None else [base])
    arrays, specs = [], []
    for operand in operands:
        array, column = operand if isinstance(operand, tuple) else (operand, 0)
        rows = 1 if array.shape[0] == 1 else values_rows(values)
        arrays.append(array)
        specs.append(pl.BlockSpec((rows, width), lambda i, column=column: (0, column)))
    number = len(arrays)
    rows = values_rows(values)
    whole = lambda i: (0, 0)
    back, dgain = pl.pallas_call(
        lambda *refs: back_kernel(
            *refs[:number], *refs[-2:], parts=len(parts), based=base is not None
        ),
        grid=(1,),
        in_specs=specs + [pl.BlockSpec(memory_space=pl.ANY)] * len(order),
        out_specs=[pl.BlockSpec((rows, width), whole), pl.BlockSpec((1, width), whole)],
        out_shape=[
            jax.ShapeDtypeStruct((rows, width), bf16),
            jax.ShapeDtypeStruct((1, width), f32),
        ],
        compiler_params=vmem(48),
    )(*arrays, *order)
    return back, dgain[0]


def values_rows(values):
    return (values[0] if isinstance(values, tuple) else values).shape[0]


def history_kernel(mix_ref, hist_ref, *refs, stored):
    grad_refs, (hist_out, mix_out) = refs[:4], refs[-2:]
    rows, width = hist_out.shape[1:]
    lanes = 512
    group = 64

    token = lax.broadcasted_iota(jnp.int32, (group, stored * group), 0)
    other = lax.broadcasted_iota(jnp.int32, (group, stored * group), 1)
    for g in range(0, rows, group):
        grads = jnp.concatenate([r[g : g + group, :] for r in grad_refs], axis=0)
        stored_rows = jnp.concatenate([hist_ref[j, g : g + group, :] for j in range(stored)], axis=0)
        pairs = contract_cols(grads, stored_rows)
        columns = []
        for s in range(4):
            part = pairs[s * group : (s + 1) * group, :]
            for j in range(stored):
                kept = jnp.where(other == token + j * group, part, 0.0)
                columns.append(jnp.sum(kept, axis=1, keepdims=True))
        mix_out[g : g + group, :] = jnp.concatenate(columns, axis=1)

    def body(at, carry):
        mix = mix_ref[at, :]
        for c in range(0, width, lanes):
            cols = slice(c, c + lanes)
            wide = [r[at, cols].astype(f32) for r in grad_refs]
            for j in range(stored):
                total = total_of(
                    [wide[s] * mix[:, s * stored + j : s * stored + j + 1] for s in range(4)]
                )
                hist_out[j, at, cols] = total.astype(bf16)
        return carry

    row_loop(rows, body, 0)


def history_grads(mix_cols, history, grads, order):
    stored, tokens, width = history.shape
    rows = 128
    here = lambda i: (i, 0)
    there = lambda i: (0, i, 0)
    return pl.pallas_call(
        lambda *refs: history_kernel(*refs, stored=stored),
        grid=(tokens // rows,),
        in_specs=[
            pl.BlockSpec((rows, 4 * stored), here),
            pl.BlockSpec((stored, rows, width), there),
        ]
        + [pl.BlockSpec((rows, width), lambda i, column=column: (i, column)) for _, column in grads]
        + [pl.BlockSpec(memory_space=pl.ANY)] * len(order),
        out_specs=[
            pl.BlockSpec((stored, rows, width), there),
            pl.BlockSpec((rows, 4 * stored), here),
        ],
        out_shape=[
            jax.ShapeDtypeStruct((stored, tokens, width), bf16),
            jax.ShapeDtypeStruct((tokens, 4 * stored), f32),
        ],
        compiler_params=vmem(48),
    )(mix_cols, history, *[g for g, _ in grads], *order)


def contract_rows(left, right):
    return lax.dot_general(left, right, (((0,), (0,)), ((), ())), preferred_element_type=f32)


def contract_cols(left, right):
    return lax.dot_general(left, right, (((1,), (1,)), ((), ())), preferred_element_type=f32)


def mlp_grads(mlp_rows, up_low, branch_rows, active, first):
    tokens, width = mlp_rows.shape
    hidden = active.shape[1]
    rows = 256
    total = 2 * hidden + first.shape[1]

    def kernel(mlp_ref, up_ref, branch_ref, active_ref, first_ref, out_ref):
        out_ref[:, :hidden] = contract_rows(mlp_ref[...], up_ref[...]).astype(bf16)
        out_ref[:, hidden : 2 * hidden] = contract_rows(branch_ref[...], active_ref[...]).astype(bf16)
        out_ref[:, 2 * hidden :] = first_ref[...].astype(bf16)

    side = pl.BlockSpec((tokens, rows), lambda i: (0, i))
    return pl.pallas_call(
        kernel,
        grid=(width // rows,),
        in_specs=[side, resident(up_low), side, resident(active)]
        + [pl.BlockSpec((rows, first.shape[1]), lambda i: (i, 0))],
        out_specs=pl.BlockSpec((rows, total), lambda i: (i, 0)),
        out_shape=jax.ShapeDtypeStruct((width, total), bf16),
        compiler_params=vmem(56),
    )(mlp_rows, up_low, branch_rows, active, first)


def attention_grads(near, lin_grads, hidden_rows, context, order):
    tokens, width = hidden_rows.shape
    heads = context.shape[1]
    rows = 256

    def kernel(q_ref, k_ref, v_ref, dq_ref, dk_ref, dv_ref, hidden_ref, ctx_ref, *refs):
        out_ref = refs[-1]
        pairs = ((q_ref, dq_ref), (k_ref, dk_ref), (v_ref, dv_ref), (hidden_ref, ctx_ref))
        for s, (left, right) in enumerate(pairs):
            out_ref[:, s * heads : (s + 1) * heads] = contract_rows(left[...], right[...]).astype(bf16)

    side = pl.BlockSpec((tokens, rows), lambda i: (0, i))
    return pl.pallas_call(
        kernel,
        grid=(width // rows,),
        in_specs=[
            pl.BlockSpec((tokens, rows), lambda i, s=s: (0, s * (width // rows) + i))
            for s in range(3)
        ]
        + [resident(lin_grads[0])] * 3
        + [side, resident(context)]
        + [pl.BlockSpec(memory_space=pl.ANY)] * len(order),
        out_specs=pl.BlockSpec((rows, 4 * heads), lambda i: (i, 0)),
        out_shape=jax.ShapeDtypeStruct((width, 4 * heads), bf16),
        compiler_params=vmem(56),
    )(near, near, near, *lin_grads, hidden_rows, context, *order)


def round_weights(weights, turned, order):
    heights = [w.shape[1] if t else w.shape[0] for w, t in zip(weights, turned)]
    widths = [w.shape[0] if t else w.shape[1] for w, t in zip(weights, turned)]
    number = len(weights)

    def kernel(*refs):
        at = 0
        for ref, t, size in zip(refs[:number], turned, widths):
            value = ref[...].T if t else ref[...]
            refs[-1][:, at : at + size] = value.astype(bf16)
            at += size

    return pl.pallas_call(
        kernel,
        in_specs=[pl.BlockSpec(memory_space=pltpu.VMEM)] * number
        + [pl.BlockSpec(memory_space=pl.ANY)] * len(order),
        out_shape=jax.ShapeDtypeStruct((heights[0], sum(widths)), bf16),
        compiler_params=vmem(56),
    )(*weights, *order)


def feed_forward(rows, full, up_first):
    tokens, width = rows.shape
    hidden = (full.shape[1] - up_first) // 2
    cols = 512
    first = up_first // cols
    steps = hidden // cols

    def kernel(rows_ref, up_ref, down_ref, active_ref, slope_ref, out_ref, total_ref):
        step = pl.program_id(0)
        up = jnp.dot(rows_ref[...], up_ref[...], preferred_element_type=f32)
        below = 0.5 * (1.0 + lax.erf(up * (0.5**0.5)))
        active = (up * below).astype(bf16)
        active_ref[...] = active
        slope_ref[...] = below + up * jnp.exp(-0.5 * up * up) * ((2.0 * math.pi) ** -0.5)
        share = contract_cols(active, down_ref[...])

        @pl.when(step == 0)
        def _():
            total_ref[...] = share

        @pl.when(step > 0)
        def _():
            total_ref[...] += share

        @pl.when(step == steps - 1)
        def _():
            out_ref[...] = total_ref[...].astype(bf16)

    part = pl.BlockSpec((tokens, cols), lambda i: (0, i))
    return pl.pallas_call(
        kernel,
        grid=(steps,),
        in_specs=[
            resident(rows),
            pl.BlockSpec((width, cols), lambda i: (0, first + i)),
            pl.BlockSpec((width, cols), lambda i: (0, first + steps + i)),
        ],
        out_specs=[part, part, pl.BlockSpec((tokens, width), lambda i: (0, 0))],
        out_shape=[
            jax.ShapeDtypeStruct((tokens, hidden), bf16),
            jax.ShapeDtypeStruct((tokens, hidden), f32),
            jax.ShapeDtypeStruct((tokens, width), bf16),
        ],
        scratch_shapes=[pltpu.VMEM((tokens, width), f32)],
        compiler_params=vmem(60),
    )(rows, full, full)


def feed_back(rows, full, up_first, slope):
    tokens, width = rows.shape
    hidden = slope.shape[1]
    cols = 512
    first = up_first // cols
    steps = hidden // cols

    def kernel(rows_ref, up_ref, down_ref, slope_ref, *refs):
        low_ref, out_ref, total_ref = refs[-3:]
        step = pl.program_id(0)
        grad = jnp.dot(rows_ref[...], down_ref[...], preferred_element_type=f32)
        low = (grad * slope_ref[...]).astype(bf16)
        low_ref[...] = low
        share = contract_cols(low, up_ref[...])

        @pl.when(step == 0)
        def _():
            total_ref[...] = share

        @pl.when(step > 0)
        def _():
            total_ref[...] += share

        @pl.when(step == steps - 1)
        def _():
            out_ref[...] = total_ref[...].astype(bf16)

    part = pl.BlockSpec((tokens, cols), lambda i: (0, i))
    return pl.pallas_call(
        kernel,
        grid=(steps,),
        in_specs=[
            resident(rows),
            pl.BlockSpec((width, cols), lambda i: (0, first + i)),
            pl.BlockSpec((width, cols), lambda i: (0, first + steps + i)),
            part,
        ],
        out_specs=[part, pl.BlockSpec((tokens, width), lambda i: (0, 0))],
        out_shape=[
            jax.ShapeDtypeStruct((tokens, hidden), bf16),
            jax.ShapeDtypeStruct((tokens, width), bf16),
        ],
        scratch_shapes=[pltpu.VMEM((tokens, width), f32)],
        compiler_params=vmem(60),
    )(rows, full, full, slope)


def turn(values, cosine, sine):
    return values * cosine + pltpu.roll(values, HEAD_DIM // 2, 1) * sine


def score_block(queries, keys, allowed):
    scores = lax.dot_general(
        queries, keys, (((1,), (1,)), ((), ())), preferred_element_type=f32
    ) * (HEAD_DIM ** (-0.5))
    return jnp.where(allowed, scores, -1e30)


def allowed_block(row_ids, col_ids):
    return (row_ids[:, 0:1] == col_ids[0:1, :]) & (row_ids[:, 1:2] >= col_ids[1:2, :])


GROUP = 2


def attend_kernel(
    rows_ref, cols_ref, cos_ref, sin_ref, near_ref, rest_ref, wq_ref, wk_ref, wv_ref, wo_ref,
    ctx_ref, qr_ref, kr_ref, v_ref, lse_ref, out_ref, total_ref,
):
    step = pl.program_id(0)
    width = out_ref.shape[1]
    allowed = allowed_block(rows_ref[...], cols_ref[...])

    def lin(s, weight_ref):
        rows = near_ref[:, s * width : (s + 1) * width]
        return jnp.dot(rows, weight_ref[...], preferred_element_type=f32)

    q_lin, k_lin = lin(0, wq_ref), lin(1, wk_ref)
    v_ref[...] = lin(2, wv_ref).astype(bf16)
    for g in range(GROUP):
        cols = slice(g * HEAD_DIM, (g + 1) * HEAD_DIM)
        queries = turn(q_lin[:, cols], cos_ref[...], sin_ref[...]).astype(bf16)
        keys = turn(k_lin[:, cols], cos_ref[...], sin_ref[...]).astype(bf16)
        qr_ref[:, cols] = queries
        kr_ref[:, cols] = keys
        scores = score_block(queries, keys, allowed)
        row_max = jnp.max(scores, axis=1, keepdims=True)
        shifted = jnp.exp(scores - row_max)
        row_sum = jnp.sum(shifted, axis=1, keepdims=True)
        probs = (shifted / row_sum).astype(bf16)
        context = jnp.dot(probs, v_ref[:, cols], preferred_element_type=f32)
        ctx_ref[:, cols] = context.astype(bf16)
        lse_ref[g] = row_max + jnp.log(row_sum)
    share = contract_cols(ctx_ref[...], wo_ref[...])

    @pl.when(step == 0)
    def _():
        total_ref[...] = share + rest_ref[...].astype(f32)

    @pl.when(step > 0)
    def _():
        total_ref[...] += share

    @pl.when(step == pl.num_programs(0) - 1)
    def _():
        out_ref[...] = total_ref[...].astype(bf16)


def resident(array):
    return pl.BlockSpec(
        array.shape, lambda i: (0,) * array.ndim, pipeline_mode=pl.Buffered(buffer_count=1)
    )


def head_columns(full, first):
    lanes = GROUP * HEAD_DIM
    return pl.BlockSpec((full.shape[0], lanes), lambda h: (0, first // lanes + h))


def attend(row_ids, col_ids, cosine, sine, near, rest, full, heads):
    tokens, width = rest.shape
    head = pl.BlockSpec((tokens, GROUP * HEAD_DIM), lambda h: (0, h))
    fixed = [row_ids, col_ids, cosine, sine, near, rest]

    return pl.pallas_call(
        attend_kernel,
        grid=(heads // HEAD_DIM // GROUP,),
        in_specs=[resident(a) for a in fixed]
        + [head_columns(full, s * heads) for s in range(4)],
        out_specs=[head] * 4
        + [
            pl.BlockSpec((GROUP, tokens, 1), lambda h: (h, 0, 0)),
            pl.BlockSpec((tokens, width), lambda h: (0, 0)),
        ],
        out_shape=[jax.ShapeDtypeStruct((tokens, heads), bf16)] * 4
        + [
            jax.ShapeDtypeStruct((heads // HEAD_DIM, tokens, 1), f32),
            jax.ShapeDtypeStruct((tokens, width), bf16),
        ],
        scratch_shapes=[pltpu.VMEM((tokens, width), f32)],
        compiler_params=vmem(60),
    )(*fixed, *[full] * 4)


def attend_back_kernel(
    rows_ref, cols_ref, cos_ref, sin_ref, hidden_ref, wo_ref, q_ref, k_ref, v_ref, lse_ref,
    dq_ref, dk_ref, dv_ref,
):
    allowed = allowed_block(rows_ref[...], cols_ref[...])
    scale = HEAD_DIM ** (-0.5)
    grads = jnp.dot(hidden_ref[...], wo_ref[...], preferred_element_type=f32).astype(bf16)
    for g in range(GROUP):
        cols = slice(g * HEAD_DIM, (g + 1) * HEAD_DIM)
        queries, keys, values, grad = q_ref[:, cols], k_ref[:, cols], v_ref[:, cols], grads[:, cols]
        probs = jnp.exp(score_block(queries, keys, allowed) - lse_ref[g])
        prob_grad = contract_cols(grad, values)
        dv_ref[:, cols] = contract_rows(probs.astype(bf16), grad).astype(bf16)
        centre = jnp.sum(probs * prob_grad, axis=1, keepdims=True)
        score_grad = (probs * (prob_grad - centre)).astype(bf16)
        dq = jnp.dot(score_grad, keys, preferred_element_type=f32) * scale
        dk = contract_rows(score_grad, queries) * scale
        dq_ref[:, cols] = turn(dq, cos_ref[...], -sin_ref[...]).astype(bf16)
        dk_ref[:, cols] = turn(dk, cos_ref[...], -sin_ref[...]).astype(bf16)


def attend_back(row_ids, col_ids, cosine, sine, hidden_rows, full, queries, keys, values, lse):
    tokens, heads = queries.shape
    head = pl.BlockSpec((tokens, GROUP * HEAD_DIM), lambda h: (0, h))
    fixed = [row_ids, col_ids, cosine, sine, hidden_rows]

    return pl.pallas_call(
        attend_back_kernel,
        grid=(heads // HEAD_DIM // GROUP,),
        in_specs=[resident(a) for a in fixed]
        + [head_columns(full, 3 * heads), head, head, head]
        + [pl.BlockSpec((GROUP, tokens, 1), lambda h: (h, 0, 0))],
        out_specs=[head, head, head],
        out_shape=[jax.ShapeDtypeStruct((tokens, heads), bf16)] * 3,
        compiler_params=vmem(60),
    )(*fixed, full, queries, keys, values, lse)


def stream_shares(where, lin_grads, full):
    tokens, heads = lin_grads[0].shape
    width = full.shape[0]
    count = where.shape[0]
    block = tokens // count

    def kernel(where_ref, dq_ref, dk_ref, dv_ref, full_ref, *out_refs):
        for s, ref in enumerate((dq_ref, dk_ref, dv_ref)):

            @pl.when(pl.program_id(0) == s)
            def _(ref=ref, out_ref=out_refs[3 * s], leave_refs=out_refs[3 * s + 1 : 3 * s + 3]):
                share = contract_cols(ref[...], full_ref[...]).astype(bf16)
                for j in range(count):
                    at = pl.ds(pl.multiple_of(where_ref[j] * block, block), block)
                    out_ref[at, :] = share[j * block : (j + 1) * block, :]
                for k, leave_ref in zip((1, count - 1), leave_refs):
                    leave_ref[...] = out_ref[k * block : (k + 1) * block, :]

    fixed = pl.BlockSpec(
        (tokens, heads), lambda s, w: (0, 0), pipeline_mode=pl.Buffered(buffer_count=1)
    )
    return pl.pallas_call(
        kernel,
        grid_spec=pltpu.PrefetchScalarGridSpec(
            num_scalar_prefetch=1,
            grid=(3,),
            in_specs=[fixed] * 3 + [pl.BlockSpec((width, heads), lambda s, w: (0, s))],
            out_specs=(
                [pl.BlockSpec((tokens, width), lambda s, w: (0, 0))]
                + [pl.BlockSpec((block, width), lambda s, w: (0, 0))] * 2
            )
            * 3,
        ),
        out_shape=(
            [jax.ShapeDtypeStruct((tokens, width), bf16)]
            + [jax.ShapeDtypeStruct((block, width), bf16)] * 2
        )
        * 3,
        compiler_params=vmem(56),
    )(where, *lin_grads, full)


def unpack_mlp(mlp_sum, hidden, mixes):
    rows = mlp_sum.shape[0]

    def kernel(sum_ref, up_ref, down_ref, first_ref):
        up_ref[...] = sum_ref[:, :hidden].astype(f32)
        down_ref[...] = sum_ref[:, hidden : 2 * hidden].astype(f32).T
        first_ref[...] = sum_ref[:, 2 * hidden :].astype(f32).T[: first_ref.shape[0], :]

    return pl.pallas_call(
        kernel,
        out_shape=[
            jax.ShapeDtypeStruct((rows, hidden), f32),
            jax.ShapeDtypeStruct((hidden, rows), f32),
            jax.ShapeDtypeStruct((mixes + -mixes % 8, rows), f32),
        ],
        compiler_params=vmem(56),
    )(mlp_sum)


def unpack_attention(attention_sum, heads):
    rows = attention_sum.shape[0]

    def kernel(sum_ref, q_ref, k_ref, v_ref, o_ref):
        for s, ref in enumerate((q_ref, k_ref, v_ref)):
            ref[...] = sum_ref[:, s * heads : (s + 1) * heads].astype(f32)
        o_ref[...] = sum_ref[:, 3 * heads :].astype(f32).T

    shapes = [(rows, heads)] * 3 + [(heads, rows)]
    return pl.pallas_call(
        kernel,
        out_shape=[jax.ShapeDtypeStruct(shape, f32) for shape in shapes],
        compiler_params=vmem(56),
    )(attention_sum)


def places(seg_row):
    length = seg_row.shape[0]
    labels = jnp.arange(DOCS, dtype=jnp.int32)
    before = jnp.sum((seg_row[None, :] < labels[:, None]).astype(jnp.int32), axis=1)
    member = (seg_row[:, None] == labels[None, :]).astype(jnp.int32)
    begins = jnp.sum(member * before[None, :], axis=1)
    return jnp.arange(length, dtype=jnp.int32) - begins


def local(
    history,
    mix_weights,
    segments,
    w_query,
    w_key,
    w_value,
    w_output,
    w_up,
    w_down,
    norm_gains,
    w_first,
    w_second,
    out_cotangent,
    mix_cotangent,
):
    stored, row_tok, width = history.shape
    count = lax.axis_size("layer")
    me = lax.axis_index("layer")
    own_tok = row_tok // count
    last = count - 1
    order = [(me - k) % count for k in range(count)]

    def block_of(rows, k):
        return rows[k * own_tok : (k + 1) * own_tok]

    def blocks_of(rows):
        return [block_of(rows, k) for k in range(count)]

    def collect(rows):
        return lax.all_gather(rows, "layer", axis=0, tiled=True)

    def spread(rows):
        return lax.psum_scatter(rows, "layer", scatter_dimension=0, tiled=True)

    hidden = w_up.shape[1]
    heads = w_query.shape[1]
    mix_cols = mix_weights.reshape(4 * stored, row_tok).T
    near_shares = stream_sums(mix_cols, history, (0, 1, 2), [])
    low = round_weights(
        [w_query, w_key, w_value, w_output, w_up, w_down],
        [False, False, False, True, False, True],
        [near_shares],
    )
    full = lax.all_gather(low, "dp", axis=0, tiled=True)
    stream_own = spread(near_shares)
    rest_share = stream_sums(mix_cols, history, (3,), [near_shares, low])
    normed_rows = collect(after(streams_norm(stream_own, norm_gains[:3]), full))

    seg_row = segments[0]
    place_row = places(seg_row)
    col_ids = jnp.stack([seg_row, jnp.arange(row_tok, dtype=jnp.int32)])
    half = HEAD_DIM // 2
    frequency = jnp.exp(jnp.arange(half, dtype=f32) * (-2.0 * math.log(10000.0) / HEAD_DIM))
    angles = place_row.astype(f32)[:, None] * frequency[None, :]
    cosine, sine = jnp.cos(angles), jnp.sin(angles)
    cosine = jnp.concatenate([cosine, cosine], axis=1)
    sine = jnp.concatenate([-sine, sine], axis=1)
    row_ids = col_ids.T

    context, queries, keys, values, lse, hidden_part = attend(
        row_ids, col_ids, cosine, sine, normed_rows, rest_share, full, heads
    )
    hidden_in = spread(hidden_part)
    mlp_norm = row_norm(hidden_in, norm_gains[3])
    mlp_rows = collect(mlp_norm)
    active, slope, mlp_part = feed_forward(mlp_rows, full, 4 * heads)
    block = hidden_in.astype(f32) + spread(mlp_part).astype(f32)

    next_mix, mixer_pull = jax.vjp(mixer, block, norm_gains[4], w_first, w_second)
    block_part, mixer_gain_grad, first_grad, second_grad = mixer_pull(mix_cotangent)
    block_grad = out_cotangent + block_part
    branch_rows = collect(block_grad.astype(bf16))
    up_low, mlp_part = feed_back(branch_rows, full, 4 * heads, slope)
    mlp_back = spread(mlp_part)
    mixes = first_grad.shape[1]
    first_wide = jnp.pad(first_grad, ((0, 0), (0, -mixes % 128)))
    mlp_grad = mlp_grads(mlp_rows, after(up_low, mlp_part), branch_rows, active, first_wide)
    hidden_low, mlp_gain_grad = norm_back(
        hidden_in, [mlp_back], norm_gains[3], block_grad, [mlp_grad]
    )
    hidden_rows = collect(hidden_low)
    lin_grads = attend_back(
        row_ids, col_ids, cosine, sine, hidden_rows, full, queries, keys, values, lse
    )
    table = jnp.stack(order).astype(jnp.int32)
    stream_parts = stream_shares(table, lin_grads, full)
    mlp_sum = lax.psum_scatter(mlp_grad, "dp", scatter_dimension=0, tiled=True)
    gain_grads, stream_low = [], []
    for s in range(3):
        blocks = blocks_of(stream_parts[3 * s])
        blocks[1], blocks[last] = stream_parts[3 * s + 1 : 3 * s + 3]
        came = []
        for k in range(1, count):
            came = sum_hop(blocks, k, came, count)
        low, gain_grad = norm_back((stream_own, s), blocks[:1] + came, norm_gains[s])
        gain_grads.append(gain_grad)
        stream_low.append(low)
    near = collect(jnp.concatenate(stream_low, axis=1))

    gain_rows = jnp.stack(gain_grads + [mlp_gain_grad, mixer_gain_grad])
    lines = -(-mixes * mixes // width)
    second_flat = jnp.pad(second_grad.reshape(-1), (0, lines * width - mixes * mixes))
    small = jnp.concatenate([gain_rows, second_flat.reshape(lines, width)])
    small = doubling_sum(doubling_sum(small, "layer"), "dp")
    gains_sum = small[:5]
    second_sum = small[5:].reshape(-1)[: mixes * mixes].reshape(mixes, mixes)
    attention_grad = attention_grads(
        normed_rows, lin_grads, hidden_rows, context, stream_low + [mlp_sum]
    )
    attention_sum = lax.psum_scatter(attention_grad, "dp", scatter_dimension=0, tiled=True)
    up_sum, down_sum, first_part = unpack_mlp(mlp_sum, hidden, mixes)
    first_sum = lax.all_gather(doubling_sum(first_part, "layer"), "dp", axis=1, tiled=True)[:mixes].T
    history_grad, mix_back = history_grads(
        mix_cols,
        history,
        [(near, 0), (near, 1), (near, 2), (hidden_rows, 0)],
        [down_sum[:8], first_sum[:8], small, attention_grad],
    )
    *projections, output_sum = unpack_attention(attention_sum, heads)
    mix_grad = mix_back.T.reshape(4, stored, row_tok)
    return (
        block.astype(bf16),
        next_mix,
        history_grad,
        mix_grad,
        *projections,
        output_sum,
        up_sum,
        down_sum,
        gains_sum,
        first_sum,
        second_sum,
    )


def solution(mesh):
    placed = (
        P("layer", "dp", None),
        P(None, "layer", "dp"),
        P("dp", None),
        P("dp", "layer"),
        P("dp", "layer"),
        P("dp", "layer"),
        P("layer", "dp"),
        P("dp", "layer"),
        P("layer", "dp"),
        P(),
        P(),
        P(),
        P(("dp", "layer"), None),
        P(("dp", "layer"), None),
    )
    return jax.shard_map(
        local,
        mesh=mesh,
        in_specs=placed,
        out_specs=(
            P(("dp", "layer"), None),
            P(("dp", "layer"), None),
            P("layer", "dp", None),
            P(None, "layer", "dp"),
            P("dp", "layer"),
            P("dp", "layer"),
            P("dp", "layer"),
            P("layer", "dp"),
            P("dp", "layer"),
            P("layer", "dp"),
            P(),
            P(),
            P(),
        ),
        check_vma=False,
    )
```

```python
import math

import jax
import jax.numpy as jnp
from jax import lax
from jax.experimental import pallas as pl
from jax.experimental.pallas import tpu as pltpu
from jax.sharding import PartitionSpec as P

HEAD_DIM = 128
DOCS = 2


highest = lax.Precision.HIGHEST
epsilon = 1e-05
bf16 = jnp.bfloat16
f32 = jnp.float32
CHUNK = 16


def rms_norm(values, gain_vec):
    square = jnp.mean(values * values, axis=-1, keepdims=True)
    return values * lax.rsqrt(square + epsilon) * gain_vec


def gelu_exact(values):
    return jax.nn.gelu(values, approximate=False)


def mixer(out_rows, gain_vec, first_matrix, second_matrix):
    hidden = gelu_exact(jnp.dot(rms_norm(out_rows, gain_vec), first_matrix, precision=highest))
    return jnp.dot(hidden, second_matrix, precision=highest)


def plain_dot(left, right):
    return jnp.dot(left, right, preferred_element_type=f32)


def dot_left_t(left, right):
    return lax.dot_general(left, right, (((0,), (0,)), ((), ())), preferred_element_type=f32)


def dot_right_t(left, right):
    return lax.dot_general(left, right, (((1,), (1,)), ((), ())), preferred_element_type=f32)


def doubling_sum(value, axis):
    size = lax.axis_size(axis)
    step = 1
    while step < size:
        value = value + lax.ppermute(value, axis, [(i, i ^ step) for i in range(size)])
        step *= 2
    return value


def total_of(pieces):
    total = pieces[0]
    for piece in pieces[1:]:
        total = total + piece
    return total


def join(values, others):
    anywhere = pl.BlockSpec(memory_space=pl.ANY)
    return list(
        pl.pallas_call(
            lambda *refs: None,
            in_specs=[anywhere] * (len(values) + len(others)),
            out_specs=[anywhere] * len(values),
            out_shape=[jax.ShapeDtypeStruct(v.shape, v.dtype) for v in values],
            input_output_aliases={i: i for i in range(len(values))},
        )(*values, *others)
    )


def after(value, *others):
    return join([value], others)[0]


def sum_hop(blocks, k, came, count):
    up, down = blocks[k], blocks[count - k]
    if came:
        up, down = up + came[0], down + came[1]
    return [
        lax.ppermute(up, "layer", [(i, i + 1) for i in range(k)]),
        lax.ppermute(down, "layer", [(i, i - 1) for i in range(count - k, count)]),
    ]


def vmem(megabytes):
    return pltpu.CompilerParams(vmem_limit_bytes=megabytes << 20)


def row_loop(rows, body, carry):
    def turn_of(i, c):
        for n in range(2):
            c = body(pl.ds(pl.multiple_of((2 * i + n) * CHUNK, CHUNK), CHUNK), c)
        return c

    return lax.fori_loop(0, rows // CHUNK // 2, turn_of, carry)


def stream_kernel(mix_ref, hist_ref, *refs, stored, streams):
    out_ref = refs[-1]
    width = hist_ref.shape[2]
    lanes = 512

    def body(at, carry):
        mix = mix_ref[at, :]
        for c in range(0, width, lanes):
            rows = [hist_ref[j, at, c : c + lanes].astype(f32) for j in range(stored)]
            for n, s in enumerate(streams):
                total = total_of(
                    [rows[j] * mix[:, s * stored + j : s * stored + j + 1] for j in range(stored)]
                )
                out_ref[at, n * width + c : n * width + c + lanes] = total.astype(bf16)
        return carry

    row_loop(out_ref.shape[0], body, 0)


def stream_sums(mix_cols, history, streams, order):
    stored, tokens, width = history.shape
    rows = 128
    here = lambda i: (i, 0)
    return pl.pallas_call(
        lambda *refs: stream_kernel(*refs, stored=stored, streams=streams),
        grid=(tokens // rows,),
        in_specs=[
            pl.BlockSpec((rows, 4 * stored), here),
            pl.BlockSpec((stored, rows, width), lambda i: (0, i, 0)),
        ]
        + [pl.BlockSpec(memory_space=pl.ANY)] * len(order),
        out_specs=pl.BlockSpec((rows, len(streams) * width), here),
        out_shape=jax.ShapeDtypeStruct((tokens, len(streams) * width), bf16),
        compiler_params=vmem(48),
    )(mix_cols, history, *order)


def streams_norm(values, gains):
    block, width = values.shape[0], gains.shape[1]

    def kernel(gain_ref, value_ref, norm_ref):
        gain = gain_ref[pl.ds(pl.program_id(0), 1), :]

        def body(at, carry):
            rows = value_ref[at, :].astype(f32)
            centre = rows - jnp.mean(rows, axis=1, keepdims=True)
            spread = jnp.mean(centre * centre, axis=1, keepdims=True)
            norm_ref[at, :] = (centre * lax.rsqrt(spread + epsilon) * gain).astype(bf16)
            return carry

        row_loop(block, body, 0)

    stream = pl.BlockSpec((block, width), lambda s: (0, s))
    return pl.pallas_call(
        kernel,
        grid=(3,),
        in_specs=[pl.BlockSpec(gains.shape, lambda s: (0, 0)), stream],
        out_specs=stream,
        out_shape=jax.ShapeDtypeStruct(values.shape, bf16),
        compiler_params=vmem(48),
    )(gains, values)


def row_norm(values, gain_vec):
    def kernel(gain_ref, value_ref, norm_ref):
        def body(at, carry):
            rows = value_ref[at, :].astype(f32)
            centre = rows - jnp.mean(rows, axis=1, keepdims=True)
            spread = jnp.mean(centre * centre, axis=1, keepdims=True)
            norm_ref[at, :] = (centre * lax.rsqrt(spread + epsilon) * gain_ref[...]).astype(bf16)
            return carry

        row_loop(value_ref.shape[0], body, 0)

    return pl.pallas_call(
        kernel,
        out_shape=jax.ShapeDtypeStruct(values.shape, bf16),
        compiler_params=vmem(48),
    )(gain_vec[None], values)


def norm_grad(values, grad, gain):
    centre = values - jnp.mean(values, axis=1, keepdims=True)
    inv = lax.rsqrt(jnp.mean(centre * centre, axis=1, keepdims=True) + epsilon)
    hat = centre * inv
    scaled = grad * gain
    back = (
        scaled
        - jnp.mean(scaled, axis=1, keepdims=True)
        - hat * jnp.mean(scaled * hat, axis=1, keepdims=True)
    ) * inv
    return back, jnp.sum(grad * hat, axis=0, keepdims=True)


def back_kernel(gain_ref, value_ref, *refs, parts, based):
    part_refs = refs[:parts]
    base_ref = refs[parts] if based else None
    out_ref, dgain_ref = refs[-2:]

    def body(at, dgain):
        values = value_ref[at, :].astype(f32)
        grad = total_of([p[at, :].astype(f32) for p in part_refs])
        back, dgain_rows = norm_grad(values, grad, gain_ref[...])
        if based:
            back = back + base_ref[at, :]
        out_ref[at, :] = back.astype(bf16)
        return dgain + dgain_rows

    dgain_ref[...] = row_loop(value_ref.shape[0], body, jnp.zeros(dgain_ref.shape, f32))


def norm_back(values, parts, gain_vec, base=None, order=()):
    width = gain_vec.shape[0]
    operands = [gain_vec[None], values] + list(parts) + ([] if base is None else [base])
    arrays, specs = [], []
    for operand in operands:
        array, column = operand if isinstance(operand, tuple) else (operand, 0)
        rows = 1 if array.shape[0] == 1 else values_rows(values)
        arrays.append(array)
        specs.append(pl.BlockSpec((rows, width), lambda i, column=column: (0, column)))
    number = len(arrays)
    rows = values_rows(values)
    whole = lambda i: (0, 0)
    back, dgain = pl.pallas_call(
        lambda *refs: back_kernel(
            *refs[:number], *refs[-2:], parts=len(parts), based=base is not None
        ),
        grid=(1,),
        in_specs=specs + [pl.BlockSpec(memory_space=pl.ANY)] * len(order),
        out_specs=[pl.BlockSpec((rows, width), whole), pl.BlockSpec((1, width), whole)],
        out_shape=[
            jax.ShapeDtypeStruct((rows, width), bf16),
            jax.ShapeDtypeStruct((1, width), f32),
        ],
        compiler_params=vmem(48),
    )(*arrays, *order)
    return back, dgain[0]


def values_rows(values):
    return (values[0] if isinstance(values, tuple) else values).shape[0]


def history_kernel(mix_ref, hist_ref, *refs, stored):
    grad_refs, (hist_out, mix_out) = refs[:4], refs[-2:]
    rows, width = hist_out.shape[1:]
    lanes = 512
    group = 64

    token = lax.broadcasted_iota(jnp.int32, (group, stored * group), 0)
    other = lax.broadcasted_iota(jnp.int32, (group, stored * group), 1)
    for g in range(0, rows, group):
        grads = jnp.concatenate([r[g : g + group, :] for r in grad_refs], axis=0)
        stored_rows = jnp.concatenate([hist_ref[j, g : g + group, :] for j in range(stored)], axis=0)
        pairs = contract_cols(grads, stored_rows)
        columns = []
        for s in range(4):
            part = pairs[s * group : (s + 1) * group, :]
            for j in range(stored):
                kept = jnp.where(other == token + j * group, part, 0.0)
                columns.append(jnp.sum(kept, axis=1, keepdims=True))
        mix_out[g : g + group, :] = jnp.concatenate(columns, axis=1)

    def body(at, carry):
        mix = mix_ref[at, :]
        for c in range(0, width, lanes):
            cols = slice(c, c + lanes)
            wide = [r[at, cols].astype(f32) for r in grad_refs]
            for j in range(stored):
                total = total_of(
                    [wide[s] * mix[:, s * stored + j : s * stored + j + 1] for s in range(4)]
                )
                hist_out[j, at, cols] = total.astype(bf16)
        return carry

    row_loop(rows, body, 0)


def history_grads(mix_cols, history, grads, order):
    stored, tokens, width = history.shape
    rows = 128
    here = lambda i: (i, 0)
    there = lambda i: (0, i, 0)
    return pl.pallas_call(
        lambda *refs: history_kernel(*refs, stored=stored),
        grid=(tokens // rows,),
        in_specs=[
            pl.BlockSpec((rows, 4 * stored), here),
            pl.BlockSpec((stored, rows, width), there),
        ]
        + [pl.BlockSpec((rows, width), lambda i, column=column: (i, column)) for _, column in grads]
        + [pl.BlockSpec(memory_space=pl.ANY)] * len(order),
        out_specs=[
            pl.BlockSpec((stored, rows, width), there),
            pl.BlockSpec((rows, 4 * stored), here),
        ],
        out_shape=[
            jax.ShapeDtypeStruct((stored, tokens, width), bf16),
            jax.ShapeDtypeStruct((tokens, 4 * stored), f32),
        ],
        compiler_params=vmem(48),
    )(mix_cols, history, *[g for g, _ in grads], *order)


def contract_rows(left, right):
    return lax.dot_general(left, right, (((0,), (0,)), ((), ())), preferred_element_type=f32)


def contract_cols(left, right):
    return lax.dot_general(left, right, (((1,), (1,)), ((), ())), preferred_element_type=f32)


def mlp_grads(mlp_rows, up_low, branch_rows, active, first):
    tokens, width = mlp_rows.shape
    hidden = active.shape[1]
    rows = 256
    total = 2 * hidden + first.shape[1]

    def kernel(mlp_ref, up_ref, branch_ref, active_ref, first_ref, out_ref):
        out_ref[:, :hidden] = contract_rows(mlp_ref[...], up_ref[...]).astype(bf16)
        out_ref[:, hidden : 2 * hidden] = contract_rows(branch_ref[...], active_ref[...]).astype(bf16)
        out_ref[:, 2 * hidden :] = first_ref[...].astype(bf16)

    side = pl.BlockSpec((tokens, rows), lambda i: (0, i))
    return pl.pallas_call(
        kernel,
        grid=(width // rows,),
        in_specs=[side, resident(up_low), side, resident(active)]
        + [pl.BlockSpec((rows, first.shape[1]), lambda i: (i, 0))],
        out_specs=pl.BlockSpec((rows, total), lambda i: (i, 0)),
        out_shape=jax.ShapeDtypeStruct((width, total), bf16),
        compiler_params=vmem(56),
    )(mlp_rows, up_low, branch_rows, active, first)


def attention_grads(near, lin_grads, hidden_rows, context, order):
    tokens, width = hidden_rows.shape
    heads = context.shape[1]
    rows = 256

    def kernel(q_ref, k_ref, v_ref, dq_ref, dk_ref, dv_ref, hidden_ref, ctx_ref, *refs):
        out_ref = refs[-1]
        pairs = ((q_ref, dq_ref), (k_ref, dk_ref), (v_ref, dv_ref), (hidden_ref, ctx_ref))
        for s, (left, right) in enumerate(pairs):
            out_ref[:, s * heads : (s + 1) * heads] = contract_rows(left[...], right[...]).astype(bf16)

    side = pl.BlockSpec((tokens, rows), lambda i: (0, i))
    return pl.pallas_call(
        kernel,
        grid=(width // rows,),
        in_specs=[
            pl.BlockSpec((tokens, rows), lambda i, s=s: (0, s * (width // rows) + i))
            for s in range(3)
        ]
        + [resident(lin_grads[0])] * 3
        + [side, resident(context)]
        + [pl.BlockSpec(memory_space=pl.ANY)] * len(order),
        out_specs=pl.BlockSpec((rows, 4 * heads), lambda i: (i, 0)),
        out_shape=jax.ShapeDtypeStruct((width, 4 * heads), bf16),
        compiler_params=vmem(56),
    )(near, near, near, *lin_grads, hidden_rows, context, *order)


def round_weights(weights, turned, order):
    heights = [w.shape[1] if t else w.shape[0] for w, t in zip(weights, turned)]
    widths = [w.shape[0] if t else w.shape[1] for w, t in zip(weights, turned)]
    number = len(weights)

    def kernel(*refs):
        at = 0
        for ref, t, size in zip(refs[:number], turned, widths):
            value = ref[...].T if t else ref[...]
            refs[-1][:, at : at + size] = value.astype(bf16)
            at += size

    block = min(128, heights[0])
    return pl.pallas_call(
        kernel,
        grid=(heights[0] // block,),
        in_specs=[
            pl.BlockSpec((size, block), lambda i: (0, i))
            if t
            else pl.BlockSpec((block, size), lambda i: (i, 0))
            for t, size in zip(turned, widths)
        ]
        + [pl.BlockSpec(memory_space=pl.ANY)] * len(order),
        out_specs=pl.BlockSpec((block, sum(widths)), lambda i: (i, 0)),
        out_shape=jax.ShapeDtypeStruct((heights[0], sum(widths)), bf16),
        compiler_params=vmem(56),
    )(*weights, *order)


def feed_forward(rows, full, up_first):
    tokens, width = rows.shape
    hidden = (full.shape[1] - up_first) // 2
    cols = 512
    first = up_first // cols
    steps = hidden // cols

    def kernel(rows_ref, up_ref, down_ref, active_ref, slope_ref, out_ref, total_ref):
        step = pl.program_id(0)
        up = jnp.dot(rows_ref[...], up_ref[...], preferred_element_type=f32)
        below = 0.5 * (1.0 + lax.erf(up * (0.5**0.5)))
        active = (up * below).astype(bf16)
        active_ref[...] = active
        slope_ref[...] = below + up * jnp.exp(-0.5 * up * up) * ((2.0 * math.pi) ** -0.5)
        share = contract_cols(active, down_ref[...])

        @pl.when(step == 0)
        def _():
            total_ref[...] = share

        @pl.when(step > 0)
        def _():
            total_ref[...] += share

        @pl.when(step == steps - 1)
        def _():
            out_ref[...] = total_ref[...].astype(bf16)

    part = pl.BlockSpec((tokens, cols), lambda i: (0, i))
    return pl.pallas_call(
        kernel,
        grid=(steps,),
        in_specs=[
            resident(rows),
            pl.BlockSpec((width, cols), lambda i: (0, first + i)),
            pl.BlockSpec((width, cols), lambda i: (0, first + steps + i)),
        ],
        out_specs=[part, part, pl.BlockSpec((tokens, width), lambda i: (0, 0))],
        out_shape=[
            jax.ShapeDtypeStruct((tokens, hidden), bf16),
            jax.ShapeDtypeStruct((tokens, hidden), f32),
            jax.ShapeDtypeStruct((tokens, width), bf16),
        ],
        scratch_shapes=[pltpu.VMEM((tokens, width), f32)],
        compiler_params=vmem(60),
    )(rows, full, full)


def feed_back(rows, full, up_first, slope):
    tokens, width = rows.shape
    hidden = slope.shape[1]
    cols = 512
    first = up_first // cols
    steps = hidden // cols

    def kernel(rows_ref, up_ref, down_ref, slope_ref, *refs):
        low_ref, out_ref, total_ref = refs[-3:]
        step = pl.program_id(0)
        grad = jnp.dot(rows_ref[...], down_ref[...], preferred_element_type=f32)
        low = (grad * slope_ref[...]).astype(bf16)
        low_ref[...] = low
        share = contract_cols(low, up_ref[...])

        @pl.when(step == 0)
        def _():
            total_ref[...] = share

        @pl.when(step > 0)
        def _():
            total_ref[...] += share

        @pl.when(step == steps - 1)
        def _():
            out_ref[...] = total_ref[...].astype(bf16)

    part = pl.BlockSpec((tokens, cols), lambda i: (0, i))
    return pl.pallas_call(
        kernel,
        grid=(steps,),
        in_specs=[
            resident(rows),
            pl.BlockSpec((width, cols), lambda i: (0, first + i)),
            pl.BlockSpec((width, cols), lambda i: (0, first + steps + i)),
            part,
        ],
        out_specs=[part, pl.BlockSpec((tokens, width), lambda i: (0, 0))],
        out_shape=[
            jax.ShapeDtypeStruct((tokens, hidden), bf16),
            jax.ShapeDtypeStruct((tokens, width), bf16),
        ],
        scratch_shapes=[pltpu.VMEM((tokens, width), f32)],
        compiler_params=vmem(60),
    )(rows, full, full, slope)


def turn(values, cosine, sine):
    return values * cosine + pltpu.roll(values, HEAD_DIM // 2, 1) * sine


def score_block(queries, keys, allowed):
    scores = lax.dot_general(
        queries, keys, (((1,), (1,)), ((), ())), preferred_element_type=f32
    ) * (HEAD_DIM ** (-0.5))
    return jnp.where(allowed, scores, -1e30)


def allowed_block(row_ids, col_ids):
    return (row_ids[:, 0:1] == col_ids[0:1, :]) & (row_ids[:, 1:2] >= col_ids[1:2, :])


GROUP = 2


def attend_kernel(
    rows_ref, cols_ref, cos_ref, sin_ref, near_ref, rest_ref, wq_ref, wk_ref, wv_ref, wo_ref,
    ctx_ref, qr_ref, kr_ref, v_ref, lse_ref, out_ref, total_ref,
):
    step = pl.program_id(0)
    width = out_ref.shape[1]
    allowed = allowed_block(rows_ref[...], cols_ref[...])

    def lin(s, weight_ref):
        rows = near_ref[:, s * width : (s + 1) * width]
        return jnp.dot(rows, weight_ref[...], preferred_element_type=f32)

    q_lin, k_lin = lin(0, wq_ref), lin(1, wk_ref)
    v_ref[...] = lin(2, wv_ref).astype(bf16)
    for g in range(GROUP):
        cols = slice(g * HEAD_DIM, (g + 1) * HEAD_DIM)
        queries = turn(q_lin[:, cols], cos_ref[...], sin_ref[...]).astype(bf16)
        keys = turn(k_lin[:, cols], cos_ref[...], sin_ref[...]).astype(bf16)
        qr_ref[:, cols] = queries
        kr_ref[:, cols] = keys
        scores = score_block(queries, keys, allowed)
        row_max = jnp.max(scores, axis=1, keepdims=True)
        shifted = jnp.exp(scores - row_max)
        row_sum = jnp.sum(shifted, axis=1, keepdims=True)
        probs = (shifted / row_sum).astype(bf16)
        context = jnp.dot(probs, v_ref[:, cols], preferred_element_type=f32)
        ctx_ref[:, cols] = context.astype(bf16)
        lse_ref[g] = row_max + jnp.log(row_sum)
    share = contract_cols(ctx_ref[...], wo_ref[...])

    @pl.when(step == 0)
    def _():
        total_ref[...] = share + rest_ref[...].astype(f32)

    @pl.when(step > 0)
    def _():
        total_ref[...] += share

    @pl.when(step == pl.num_programs(0) - 1)
    def _():
        out_ref[...] = total_ref[...].astype(bf16)


def resident(array):
    return pl.BlockSpec(
        array.shape, lambda i: (0,) * array.ndim, pipeline_mode=pl.Buffered(buffer_count=1)
    )


def head_columns(full, first):
    lanes = GROUP * HEAD_DIM
    return pl.BlockSpec((full.shape[0], lanes), lambda h: (0, first // lanes + h))


def attend(row_ids, col_ids, cosine, sine, near, rest, full, heads):
    tokens, width = rest.shape
    head = pl.BlockSpec((tokens, GROUP * HEAD_DIM), lambda h: (0, h))
    fixed = [row_ids, col_ids, cosine, sine, near, rest]

    return pl.pallas_call(
        attend_kernel,
        grid=(heads // HEAD_DIM // GROUP,),
        in_specs=[resident(a) for a in fixed]
        + [head_columns(full, s * heads) for s in range(4)],
        out_specs=[head] * 4
        + [
            pl.BlockSpec((GROUP, tokens, 1), lambda h: (h, 0, 0)),
            pl.BlockSpec((tokens, width), lambda h: (0, 0)),
        ],
        out_shape=[jax.ShapeDtypeStruct((tokens, heads), bf16)] * 4
        + [
            jax.ShapeDtypeStruct((heads // HEAD_DIM, tokens, 1), f32),
            jax.ShapeDtypeStruct((tokens, width), bf16),
        ],
        scratch_shapes=[pltpu.VMEM((tokens, width), f32)],
        compiler_params=vmem(60),
    )(*fixed, *[full] * 4)


def attend_back_kernel(
    rows_ref, cols_ref, cos_ref, sin_ref, hidden_ref, wo_ref, q_ref, k_ref, v_ref, lse_ref,
    dq_ref, dk_ref, dv_ref,
):
    allowed = allowed_block(rows_ref[...], cols_ref[...])
    scale = HEAD_DIM ** (-0.5)
    grads = jnp.dot(hidden_ref[...], wo_ref[...], preferred_element_type=f32).astype(bf16)
    for g in range(GROUP):
        cols = slice(g * HEAD_DIM, (g + 1) * HEAD_DIM)
        queries, keys, values, grad = q_ref[:, cols], k_ref[:, cols], v_ref[:, cols], grads[:, cols]
        probs = jnp.exp(score_block(queries, keys, allowed) - lse_ref[g])
        prob_grad = contract_cols(grad, values)
        dv_ref[:, cols] = contract_rows(probs.astype(bf16), grad).astype(bf16)
        centre = jnp.sum(probs * prob_grad, axis=1, keepdims=True)
        score_grad = (probs * (prob_grad - centre)).astype(bf16)
        dq = jnp.dot(score_grad, keys, preferred_element_type=f32) * scale
        dk = contract_rows(score_grad, queries) * scale
        dq_ref[:, cols] = turn(dq, cos_ref[...], -sin_ref[...]).astype(bf16)
        dk_ref[:, cols] = turn(dk, cos_ref[...], -sin_ref[...]).astype(bf16)


def attend_back(row_ids, col_ids, cosine, sine, hidden_rows, full, queries, keys, values, lse):
    tokens, heads = queries.shape
    head = pl.BlockSpec((tokens, GROUP * HEAD_DIM), lambda h: (0, h))
    fixed = [row_ids, col_ids, cosine, sine, hidden_rows]

    return pl.pallas_call(
        attend_back_kernel,
        grid=(heads // HEAD_DIM // GROUP,),
        in_specs=[resident(a) for a in fixed]
        + [head_columns(full, 3 * heads), head, head, head]
        + [pl.BlockSpec((GROUP, tokens, 1), lambda h: (h, 0, 0))],
        out_specs=[head, head, head],
        out_shape=[jax.ShapeDtypeStruct((tokens, heads), bf16)] * 3,
        compiler_params=vmem(60),
    )(*fixed, full, queries, keys, values, lse)


def stream_shares(where, lin_grads, full):
    tokens, heads = lin_grads[0].shape
    width = full.shape[0]
    count = where.shape[0]
    block = tokens // count

    def kernel(where_ref, dq_ref, dk_ref, dv_ref, full_ref, *out_refs):
        for s, ref in enumerate((dq_ref, dk_ref, dv_ref)):

            @pl.when(pl.program_id(0) == s)
            def _(ref=ref, out_ref=out_refs[3 * s], leave_refs=out_refs[3 * s + 1 : 3 * s + 3]):
                share = contract_cols(ref[...], full_ref[...]).astype(bf16)
                for j in range(count):
                    at = pl.ds(pl.multiple_of(where_ref[j] * block, block), block)
                    out_ref[at, :] = share[j * block : (j + 1) * block, :]
                for k, leave_ref in zip((1, count - 1), leave_refs):
                    leave_ref[...] = out_ref[k * block : (k + 1) * block, :]

    fixed = pl.BlockSpec(
        (tokens, heads), lambda s, w: (0, 0), pipeline_mode=pl.Buffered(buffer_count=1)
    )
    return pl.pallas_call(
        kernel,
        grid_spec=pltpu.PrefetchScalarGridSpec(
            num_scalar_prefetch=1,
            grid=(3,),
            in_specs=[fixed] * 3 + [pl.BlockSpec((width, heads), lambda s, w: (0, s))],
            out_specs=(
                [pl.BlockSpec((tokens, width), lambda s, w: (0, 0))]
                + [pl.BlockSpec((block, width), lambda s, w: (0, 0))] * 2
            )
            * 3,
        ),
        out_shape=(
            [jax.ShapeDtypeStruct((tokens, width), bf16)]
            + [jax.ShapeDtypeStruct((block, width), bf16)] * 2
        )
        * 3,
        compiler_params=vmem(56),
    )(where, *lin_grads, full)


def unpack_mlp(mlp_sum, hidden, mixes):
    rows = mlp_sum.shape[0]

    def kernel(sum_ref, up_ref, down_ref, first_ref):
        up_ref[...] = sum_ref[:, :hidden].astype(f32)
        down_ref[...] = sum_ref[:, hidden : 2 * hidden].astype(f32).T
        first_ref[...] = sum_ref[:, 2 * hidden :].astype(f32).T[: first_ref.shape[0], :]

    return pl.pallas_call(
        kernel,
        out_shape=[
            jax.ShapeDtypeStruct((rows, hidden), f32),
            jax.ShapeDtypeStruct((hidden, rows), f32),
            jax.ShapeDtypeStruct((mixes + -mixes % 8, rows), f32),
        ],
        compiler_params=vmem(56),
    )(mlp_sum)


def unpack_attention(attention_sum, heads):
    rows = attention_sum.shape[0]

    def kernel(sum_ref, q_ref, k_ref, v_ref, o_ref):
        for s, ref in enumerate((q_ref, k_ref, v_ref)):
            ref[...] = sum_ref[:, s * heads : (s + 1) * heads].astype(f32)
        o_ref[...] = sum_ref[:, 3 * heads :].astype(f32).T

    shapes = [(rows, heads)] * 3 + [(heads, rows)]
    return pl.pallas_call(
        kernel,
        out_shape=[jax.ShapeDtypeStruct(shape, f32) for shape in shapes],
        compiler_params=vmem(56),
    )(attention_sum)


def places(seg_row):
    length = seg_row.shape[0]
    labels = jnp.arange(DOCS, dtype=jnp.int32)
    before = jnp.sum((seg_row[None, :] < labels[:, None]).astype(jnp.int32), axis=1)
    member = (seg_row[:, None] == labels[None, :]).astype(jnp.int32)
    begins = jnp.sum(member * before[None, :], axis=1)
    return jnp.arange(length, dtype=jnp.int32) - begins


def local(
    history,
    mix_weights,
    segments,
    w_query,
    w_key,
    w_value,
    w_output,
    w_up,
    w_down,
    norm_gains,
    w_first,
    w_second,
    out_cotangent,
    mix_cotangent,
):
    stored, row_tok, width = history.shape
    count = lax.axis_size("layer")
    me = lax.axis_index("layer")
    own_tok = row_tok // count
    last = count - 1
    order = [(me - k) % count for k in range(count)]

    def block_of(rows, k):
        return rows[k * own_tok : (k + 1) * own_tok]

    def blocks_of(rows):
        return [block_of(rows, k) for k in range(count)]

    def collect(rows):
        return lax.all_gather(rows, "layer", axis=0, tiled=True)

    def spread(rows):
        return lax.psum_scatter(rows, "layer", scatter_dimension=0, tiled=True)

    hidden = w_up.shape[1]
    heads = w_query.shape[1]
    mix_cols = mix_weights.reshape(4 * stored, row_tok).T
    near_shares = stream_sums(mix_cols, history, (0, 1, 2), [])
    low = round_weights(
        [w_query, w_key, w_value, w_output, w_up, w_down],
        [False, False, False, True, False, True],
        [near_shares],
    )
    full = lax.all_gather(low, "dp", axis=0, tiled=True)
    stream_own = spread(near_shares)
    rest_share = stream_sums(mix_cols, history, (3,), [near_shares, low])
    normed_rows = collect(after(streams_norm(stream_own, norm_gains[:3]), full))

    seg_row = segments[0]
    place_row = places(seg_row)
    col_ids = jnp.stack([seg_row, jnp.arange(row_tok, dtype=jnp.int32)])
    half = HEAD_DIM // 2
    frequency = jnp.exp(jnp.arange(half, dtype=f32) * (-2.0 * math.log(10000.0) / HEAD_DIM))
    angles = place_row.astype(f32)[:, None] * frequency[None, :]
    cosine, sine = jnp.cos(angles), jnp.sin(angles)
    cosine = jnp.concatenate([cosine, cosine], axis=1)
    sine = jnp.concatenate([-sine, sine], axis=1)
    row_ids = col_ids.T

    context, queries, keys, values, lse, hidden_part = attend(
        row_ids, col_ids, cosine, sine, normed_rows, rest_share, full, heads
    )
    hidden_in = spread(hidden_part)
    mlp_norm = row_norm(hidden_in, norm_gains[3])
    mlp_rows = collect(mlp_norm)
    active, slope, mlp_part = feed_forward(mlp_rows, full, 4 * heads)
    block = hidden_in.astype(f32) + spread(mlp_part).astype(f32)

    next_mix, mixer_pull = jax.vjp(mixer, block, norm_gains[4], w_first, w_second)
    block_part, mixer_gain_grad, first_grad, second_grad = mixer_pull(mix_cotangent)
    block_grad = out_cotangent + block_part
    branch_rows = collect(block_grad.astype(bf16))
    up_low, mlp_part = feed_back(branch_rows, full, 4 * heads, slope)
    mlp_back = spread(mlp_part)
    mixes = first_grad.shape[1]
    first_wide = jnp.pad(first_grad, ((0, 0), (0, -mixes % 128)))
    mlp_grad = mlp_grads(mlp_rows, after(up_low, mlp_part), branch_rows, active, first_wide)
    hidden_low, mlp_gain_grad = norm_back(
        hidden_in, [mlp_back], norm_gains[3], block_grad, [mlp_grad]
    )
    hidden_rows = collect(hidden_low)
    lin_grads = attend_back(
        row_ids, col_ids, cosine, sine, hidden_rows, full, queries, keys, values, lse
    )
    table = jnp.stack(order).astype(jnp.int32)
    stream_parts = stream_shares(table, lin_grads, full)
    mlp_sum = lax.psum_scatter(mlp_grad, "dp", scatter_dimension=0, tiled=True)
    gain_grads, stream_low = [], []
    for s in range(3):
        blocks = blocks_of(stream_parts[3 * s])
        blocks[1], blocks[last] = stream_parts[3 * s + 1 : 3 * s + 3]
        came = []
        for k in range(1, count):
            came = sum_hop(blocks, k, came, count)
        low, gain_grad = norm_back((stream_own, s), blocks[:1] + came, norm_gains[s])
        gain_grads.append(gain_grad)
        stream_low.append(low)
    near = collect(jnp.concatenate(stream_low, axis=1))

    gain_rows = jnp.stack(gain_grads + [mlp_gain_grad, mixer_gain_grad])
    lines = -(-mixes * mixes // width)
    second_flat = jnp.pad(second_grad.reshape(-1), (0, lines * width - mixes * mixes))
    small = jnp.concatenate([gain_rows, second_flat.reshape(lines, width)])
    small = doubling_sum(doubling_sum(small, "layer"), "dp")
    gains_sum = small[:5]
    second_sum = small[5:].reshape(-1)[: mixes * mixes].reshape(mixes, mixes)
    attention_grad = attention_grads(
        normed_rows, lin_grads, hidden_rows, context, stream_low + [mlp_sum]
    )
    attention_sum = lax.psum_scatter(attention_grad, "dp", scatter_dimension=0, tiled=True)
    up_sum, down_sum, first_part = unpack_mlp(mlp_sum, hidden, mixes)
    first_sum = lax.all_gather(doubling_sum(first_part, "layer"), "dp", axis=1, tiled=True)[:mixes].T
    history_grad, mix_back = history_grads(
        mix_cols,
        history,
        [(near, 0), (near, 1), (near, 2), (hidden_rows, 0)],
        [down_sum[:8], first_sum[:8], small, attention_grad],
    )
    *projections, output_sum = unpack_attention(attention_sum, heads)
    mix_grad = mix_back.T.reshape(4, stored, row_tok)
    return (
        block.astype(bf16),
        next_mix,
        history_grad,
        mix_grad,
        *projections,
        output_sum,
        up_sum,
        down_sum,
        gains_sum,
        first_sum,
        second_sum,
    )


def solution(mesh):
    placed = (
        P("layer", "dp", None),
        P(None, "layer", "dp"),
        P("dp", None),
        P("dp", "layer"),
        P("dp", "layer"),
        P("dp", "layer"),
        P("layer", "dp"),
        P("dp", "layer"),
        P("layer", "dp"),
        P(),
        P(),
        P(),
        P(("dp", "layer"), None),
        P(("dp", "layer"), None),
    )
    return jax.shard_map(
        local,
        mesh=mesh,
        in_specs=placed,
        out_specs=(
            P(("dp", "layer"), None),
            P(("dp", "layer"), None),
            P("layer", "dp", None),
            P(None, "layer", "dp"),
            P("dp", "layer"),
            P("dp", "layer"),
            P("dp", "layer"),
            P("layer", "dp"),
            P("dp", "layer"),
            P("layer", "dp"),
            P(),
            P(),
            P(),
        ),
        check_vma=False,
    )
```
